256 devices in a mesh: shot: 128 (over z, x, y_hi, core), ap: 2 (over y_lo).
Axes of the slice: x: 4, y: 4 (y_hi: 2, y_lo: 2; y = y_hi * 2 + y_lo), z: 8, core: 2. Of those that a mesh axis runs over, the one named last changes fastest.
Arguments:
- wave_prev: float32 [128, 32, 64, 256], P('shot', None, None, 'ap'), may hold values from -6 to 6
- wave_now: float32 [128, 32, 64, 256], P('shot', None, None, 'ap'), may hold values from -6 to 6
- adjoint_late: float32 [128, 32, 64, 256], P('shot', None, None, 'ap'), may hold values from -6 to 6
- adjoint_next: float32 [128, 32, 64, 256], P('shot', None, None, 'ap'), may hold values from -6 to 6
- bulk: float32 [128, 32, 64, 256], P('shot', None, None, 'ap'), may hold values from 0.5 to 2
- buoyancy: float32 [128, 32, 64, 256], P('shot', None, None, 'ap'), may hold values from 0.5 to 2
- traces: bfloat16 [32768, 2048], P(('shot', 'ap')), may hold values from -6 to 6
- group_filter: bfloat16 [128, 2, 2048], P('shot'), may hold values from -0.125 to 0.125
- trace_group: int32 [32768, 1], P(('shot', 'ap')), may hold values from 0 to 127; in each aligned block of 128 rows (0 to 127, 128 to 255, ...) at most 2 rows name the same one
- trace_receiver: int32 [32768], P(('shot', 'ap')), may hold values from 0 to 255
- receiver_cell: int32 [128, 512], P('shot', 'ap'), may hold values from 0 to 262143
- tile_owner: int32 [32768, 1], P('shot'), may hold values from 0 to 127; in each aligned block of 256 rows (0 to 255, 256 to 511, ...) at most 4 rows name the same one
- tile_slot: int32 [32768], P('shot'), may hold values from 0 to 7
Outputs:
- model_grad: float32 [1024, 8, 256], P('shot', None, 'ap')
- wave_last: float32 [128, 32, 64, 256], P('shot', None, None, 'ap')
- adjoint_last: float32 [128, 32, 64, 256], P('shot', None, None, 'ap')
The draws below stay inside these ranges and needn't reach their ends.
Inputs may be any that keep to these rules, and one draw needn't show every extreme that they name: `trace_group`: in each device's aligned block of 128 rows no shot group is named by more than 2 rows, and some block reaches 2; every group is named somewhere. `tile_owner`: in each group's aligned block of 256 rows no owner is named by more than 4 rows, and some block reaches 4; every owner is named somewhere.
All inputs are finite; a program needn't handle non-finite values.
Results may differ from the reference program's by a relative error of at most 0.002.
Values may be sent and summed in bfloat16 or wider, within the bound.
No kernel may reach another device: no remote copies, remote signals or barrier semaphores. Data moves between devices by JAX's collectives and lax.ppermute only.
A program may use at most 128 MiB of HBM per device.

```python
import math
import jax
import jax.numpy as jnp
import numpy as np
from jax import lax

SX = 32
SY = 64
APERTURE_DEPTH = 128
TILE_CELLS_SECOND = 8
TSAMP = 2048
NREC = 256
MT_DEV = 8
TR_DEV = 128
NZ = 256
ROWS = 32768
ATILES = 256
MODEL_TILE_TOTAL = 1024
CAP = 2
CAPT = 4
N_SHOT = 128
N_AP = 2


def touch_ends(drawn, own_key, low, largest):
    longest = drawn.shape.index(max(drawn.shape))
    spots = []
    for shift in (0, 1):
        where = [jax.random.randint(jax.random.fold_in(own_key, axis), (), 0, length) for axis, length in enumerate(drawn.shape)]
        where[longest] = (where[longest] + shift) % drawn.shape[longest]
        spots.append(tuple(where))
    return drawn.at[spots[0]].set(low).at[spots[1]].set(largest)


def levels(key, dims, cuts, low, high):
    gain, own = 1.0, jax.random.fold_in(key, 6)
    for axis_at, shards_of in cuts:
        steps = jnp.exp(jax.random.uniform(jax.random.fold_in(own, axis_at), (shards_of,), jnp.float32, low / len(cuts), high / len(cuts)))
        gain = gain * jnp.repeat(steps, dims[axis_at] // shards_of).reshape([-1 if axis == axis_at else 1 for axis in range(len(dims))])
    return gain


def routed_block(stream_key, own, number, rows, amount, top, limit, lean):
    ranking = jax.random.permutation(stream_key, amount)
    heavy_load, usual = portions_of(amount, rows * top, limit, lean, True), portions_of(amount, rows * top, limit, lean, False)
    places = jnp.arange(amount)

    def named(sizes, rotation):
        used = int((sizes > 0).sum())
        fixed = max(1, used // 4)
        passed = fixed + (places - fixed + rotation * (used - fixed)) % max(1, amount - fixed)
        return jnp.zeros((amount,), jnp.int32).at[ranking[jnp.where(places < fixed, places, passed)]].set(jnp.asarray(sizes, jnp.int32))

    sizes = jnp.where(number % 4 == 0, named(heavy_load, number // 4), named(usual, number - number // 4 - 1))
    mixed = jax.random.permutation(jax.random.fold_in(own, 3), amount)
    source_of, taker = mixed[0:amount // 2 * 2:2], mixed[1:amount // 2 * 2:2]
    room = jnp.minimum(sizes[source_of] - 1, limit - sizes[taker]) // 2
    room = jnp.where((source_of == ranking[0]) | (taker == ranking[0]) | (sizes[taker] == 0), 0, jnp.maximum(room, 0))
    passed = jax.random.randint(jax.random.fold_in(own, 4), (amount // 2,), 0, 1 << 20) % (room + 1)
    sizes = sizes.at[source_of].add(-passed).at[taker].add(passed)
    labels = jnp.searchsorted(jnp.cumsum(sizes), jnp.arange(rows * top), side="right").astype(jnp.int32)
    listing = labels.reshape(top, rows).T
    listing = listing[jax.random.permutation(jax.random.fold_in(own, 1), rows)]
    rotation = jax.random.randint(jax.random.fold_in(own, 2), (rows, 1), 0, top)
    return jnp.take_along_axis(listing, (jnp.arange(top)[None, :] + rotation) % top, axis=1)


def portions_of(amount, total, most, skew, full):
    portions = [(1 << 20) // math.isqrt(rank ** skew) + 1 for rank in range(1, amount + 1)]
    largest = most if full else min(most, max(-(-total // amount), total * portions[0] // sum(portions)))
    least = 1 if total - largest >= amount - 1 else 0
    counts, rest = [largest] + [least] * (amount - 1), total - largest - least * (amount - 1)
    while rest > 0:
        candidates = [i for i in range(1, amount) if counts[i] < largest] or [i for i in range(1, amount) if counts[i] < most]
        whole, budget = sum([portions[i] for i in candidates]), rest
        for i in candidates:
            addition = min(most - counts[i], max(1, budget * portions[i] // whole), rest)
            counts[i] = counts[i] + addition
            rest = rest - addition
    return np.array(counts)


def bell_draw(own_key, dims, width, most, cuts=(), held_as=jnp.bfloat16):
    drawn = width * jax.random.normal(own_key, dims, jnp.float32)
    if cuts:
        drawn = drawn * levels(own_key, dims, cuts, -0.22, 0.18)
    return jnp.clip(drawn, -most, most).astype(held_as)


def setup_inputs(seed: int = 0) -> dict:
    keys = jax.random.split(jax.random.key(seed), 14)
    wave_prev = bell_draw(keys[0], (N_SHOT, SX, SY, NZ), 1.0, 6.0, ((0, 128), (3, 2)), jnp.float32)
    wave_now = bell_draw(keys[1], (N_SHOT, SX, SY, NZ), 1.0, 6.0, ((0, 128), (3, 2)), jnp.float32)
    adjoint_late = bell_draw(keys[2], (N_SHOT, SX, SY, NZ), 1.0, 6.0, ((0, 128), (3, 2)), jnp.float32)
    adjoint_next = bell_draw(keys[3], (N_SHOT, SX, SY, NZ), 1.0, 6.0, ((0, 128), (3, 2)), jnp.float32)
    bulk = jnp.clip(jnp.exp(math.log(2.0) - 1.3862944 * jax.random.uniform(keys[4], (N_SHOT, SX, SY, NZ), jnp.float32) ** levels(keys[4], (N_SHOT, SX, SY, NZ), ((0, 128), (3, 2)), -0.2, 0.2)), 0.5, 2.0)
    buoyancy = jnp.clip(jnp.exp(math.log(2.0) - 1.3862944 * jax.random.uniform(keys[5], (N_SHOT, SX, SY, NZ), jnp.float32) ** levels(keys[5], (N_SHOT, SX, SY, NZ), ((0, 128), (3, 2)), -0.2, 0.2)), 0.5, 2.0)
    traces = bell_draw(keys[6], (ROWS, TSAMP), 1.0, 6.0, ((0, 256),))
    group_filter = bell_draw(keys[7], (N_SHOT, 2, TSAMP), TSAMP ** -0.5, 0.125, ((0, 128),))
    trace_group_keys = jax.random.split(jax.random.fold_in(keys[8], 1), ROWS // TR_DEV)
    trace_group_turns = jax.random.permutation(jax.random.fold_in(keys[8], 3), ROWS // TR_DEV)
    trace_group = jax.vmap(lambda own, number: routed_block(jax.random.fold_in(keys[8], 2), own, number, TR_DEV, N_SHOT, 1, CAP, 2))(trace_group_keys, trace_group_turns).reshape((ROWS, 1))
    trace_receiver = touch_ends(jax.random.randint(keys[9], (ROWS,), 0, NREC), jax.random.fold_in(keys[9], 1), 0, NREC - 1).astype(jnp.int32)
    receiver_cell = touch_ends(jax.random.randint(keys[10], (N_SHOT, N_AP * NREC), 0, SX * SY * APERTURE_DEPTH), jax.random.fold_in(keys[10], 1), 0, (SX * SY * APERTURE_DEPTH) - 1).astype(jnp.int32)
    tile_owner_keys = jax.random.split(jax.random.fold_in(keys[11], 1), (N_SHOT * ATILES) // ATILES)
    tile_owner_turns = jax.random.permutation(jax.random.fold_in(keys[11], 3), (N_SHOT * ATILES) // ATILES)
    tile_owner = jax.vmap(lambda own, number: routed_block(jax.random.fold_in(keys[11], 2), own, number, ATILES, N_SHOT, 1, CAPT, 2))(tile_owner_keys, tile_owner_turns).reshape((N_SHOT * ATILES, 1))
    tile_slot = touch_ends(jax.random.randint(keys[12], (N_SHOT * ATILES,), 0, MT_DEV), jax.random.fold_in(keys[12], 1), 0, MT_DEV - 1).astype(jnp.int32)
    return {"wave_prev": wave_prev, "wave_now": wave_now, "adjoint_late": adjoint_late, "adjoint_next": adjoint_next, "bulk": bulk, "buoyancy": buoyancy, "traces": traces, "group_filter": group_filter, "trace_group": trace_group, "trace_receiver": trace_receiver, "receiver_cell": receiver_cell, "tile_owner": tile_owner, "tile_slot": tile_slot}


STEP = 0.08


def neighbours(padded_field):
    return (padded_field[2:, 1:-1, 1:-1], padded_field[:-2, 1:-1, 1:-1], padded_field[1:-1, 2:, 1:-1],
            padded_field[1:-1, :-2, 1:-1], padded_field[1:-1, 1:-1, 2:], padded_field[1:-1, 1:-1, :-2])


def operate(wavefield, buoyancy, buoy_pad):
    total = jnp.zeros_like(wavefield)
    for wave_side, buoy_side in zip(neighbours(jnp.pad(wavefield, 1)), neighbours(buoy_pad)):
        total = total + 0.5 * (buoyancy + buoy_side) * (wave_side - wavefield)
    return total


def reference(wave_prev, wave_now, adjoint_late, adjoint_next, bulk, buoyancy, traces, group_filter, trace_group, trace_receiver, receiver_cell, tile_owner, tile_slot):
    row_total = traces.shape[0]
    block_count = row_total // TR_DEV

    def filter_block(block_index):
        first_row = block_index * TR_DEV
        trace_rows = lax.dynamic_slice_in_dim(traces, first_row, TR_DEV, 0).astype(jnp.float32)
        row_groups = lax.dynamic_slice_in_dim(trace_group[:, 0], first_row, TR_DEV, 0)
        row_filters = group_filter[row_groups].astype(jnp.float32)
        return jnp.einsum("rt,rkt->rk", trace_rows, row_filters)

    filtered = lax.map(filter_block, jnp.arange(block_count, dtype=jnp.int32)).reshape(row_total, 2)
    half_index = (jnp.arange(row_total, dtype=jnp.int32) // TR_DEV) % N_AP
    targets = trace_group[:, 0] * (N_AP * NREC) + half_index * NREC + trace_receiver
    observed = jax.ops.segment_sum(filtered, targets, num_segments=N_SHOT * N_AP * NREC)
    observed = observed.reshape(N_SHOT, N_AP * NREC, 2)
    receiver_half = jnp.arange(N_AP * NREC, dtype=jnp.int32) // NREC
    owners = tile_owner[:, 0].reshape(N_SHOT, ATILES)
    slots = tile_slot.reshape(N_SHOT, ATILES)

    def halves(wavefield):
        return wavefield.reshape(SX, SY, N_AP, APERTURE_DEPTH).transpose(2, 0, 1, 3).reshape(N_AP, SX * SY * APERTURE_DEPTH)

    def whole(split_field):
        return split_field.reshape(N_AP, SX, SY, APERTURE_DEPTH).transpose(1, 2, 0, 3).reshape(SX, SY, N_AP * APERTURE_DEPTH)

    def one_group(model_grad, inputs):
        (wave_old, wave_cur, adjoint_old, adjoint_current, bulk_here, buoy_here,
         observed_here, cells_here, owners_here, slots_here) = inputs
        buoy_pad = jnp.pad(buoy_here, 1)
        lap_now = operate(wave_cur, buoy_here, buoy_pad)
        wave_mid = 2.0 * wave_cur - wave_old + STEP * bulk_here * lap_now
        lap_mid = operate(wave_mid, buoy_here, buoy_pad)
        wave_end = 2.0 * wave_mid - wave_cur + STEP * bulk_here * lap_mid
        resid_mid = halves(wave_mid)[receiver_half, cells_here] - observed_here[:, 0]
        resid_end = halves(wave_end)[receiver_half, cells_here] - observed_here[:, 1]

        def inject(residual):
            base = jnp.zeros((N_AP, SX * SY * APERTURE_DEPTH), jnp.float32)
            return whole(base.at[receiver_half, cells_here].add(residual))

        adjoint_mid = 2.0 * adjoint_current - adjoint_old + STEP * operate(bulk_here * adjoint_current, buoy_here, buoy_pad) + inject(resid_end)
        adjoint_end = 2.0 * adjoint_mid - adjoint_current + STEP * operate(bulk_here * adjoint_mid, buoy_here, buoy_pad) + inject(resid_mid)
        image = STEP * (adjoint_mid * lap_mid + adjoint_end * lap_now)
        tile_rows = image.reshape(ATILES, TILE_CELLS_SECOND, N_AP * APERTURE_DEPTH)
        model_grad = model_grad.at[owners_here * MT_DEV + slots_here].add(tile_rows)
        return model_grad, (wave_end, adjoint_end)

    initial_gradient = jnp.zeros((MODEL_TILE_TOTAL, TILE_CELLS_SECOND, N_AP * APERTURE_DEPTH), jnp.float32)
    model_grad, (wave_last, adjoint_last) = lax.scan(
        one_group, initial_gradient,
        (wave_prev, wave_now, adjoint_late, adjoint_next, bulk, buoyancy, observed, receiver_cell, owners, slots))
    return model_grad, wave_last, adjoint_last
```

```python
import jax
import jax.numpy as jnp
from jax import lax
from jax.sharding import PartitionSpec as P

TILE_CELLS_SECOND = 8
NREC = 256
MT_DEV = 8


STEP = 0.08


def padded(cells, sides, width):
    for axis, dim in sides:
        count = lax.axis_size(axis)
        ends = count - 1
        head = lax.slice_in_dim(cells, 0, width, axis=dim)
        tail = lax.slice_in_dim(cells, cells.shape[dim] - width, cells.shape[dim], axis=dim)
        cells = jnp.concatenate(
            [
                lax.ppermute(tail, axis, [(i, (i + 1) % count) for i in range(ends)]),
                cells,
                lax.ppermute(head, axis, [((i + 1) % count, i) for i in range(ends)]),
            ],
            axis=dim,
        )
    return cells


def neighbours(padded_field):
    return (
        padded_field[2:, 1:-1, 1:-1],
        padded_field[:-2, 1:-1, 1:-1],
        padded_field[1:-1, 2:, 1:-1],
        padded_field[1:-1, :-2, 1:-1],
        padded_field[1:-1, 1:-1, 2:],
        padded_field[1:-1, 1:-1, :-2],
    )


def operate(wavefield, buoyancy, buoy_pad, rimmed):
    rimmed = padded(wavefield, (("ap", 2),), 1)
    wavefield_padded = jnp.pad(rimmed, ((1, 1), (1, 1), (0, 0)))
    total = jnp.zeros_like(wavefield)
    for wave_side, buoy_side in zip(neighbours(wavefield_padded), neighbours(buoy_pad)):
        total = total + 0.5 * (buoyancy + buoy_side) * (wave_side - wavefield)
    return total


def ranking(keys, width):
    onehot = (keys[:, None] == jnp.arange(width, dtype=jnp.int32)[None, :]).astype(jnp.int32)
    return jnp.sum(jnp.cumsum(onehot, axis=0) * onehot, axis=1) - 1


def local(
    wave_prev,
    wave_now,
    adjoint_late,
    adjoint_next,
    bulk,
    buoyancy,
    traces,
    group_filter,
    trace_group,
    trace_receiver,
    receiver_cell,
    tile_owner,
    tile_slot,
):
    shot_count = lax.axis_size("shot")
    trace_count = traces.shape[0]
    samples = traces.shape[1]
    capacity = max(2, 2 * trace_count // shot_count)
    row_groups = trace_group[:, 0]
    position = row_groups * capacity + ranking(row_groups, shot_count)
    send_ids = jnp.zeros((shot_count * capacity,), jnp.int32).at[position].set(trace_receiver)
    send_ids = send_ids.reshape(shot_count, capacity)
    own_filter = group_filter[0]
    send_rows = jnp.zeros((shot_count * capacity, samples), traces.dtype).at[position].set(traces)
    send_rows = send_rows.reshape(shot_count, capacity, samples)
    values_out = jnp.einsum(
        "sct,kt->sck",
        lax.all_to_all(send_rows, "shot", split_axis=0, concat_axis=0, tiled=True),
        own_filter,
        preferred_element_type=jnp.float32,
    )
    got_ids = lax.all_to_all(send_ids, "shot", split_axis=0, concat_axis=0, tiled=True)
    observed = (
        jnp.zeros((NREC, 2), jnp.float32).at[got_ids.reshape(-1)].add(values_out.reshape(-1, 2))
    )
    wave_old = wave_prev[0]
    wave_cur = wave_now[0]
    adjoint_old = adjoint_late[0]
    adjoint_current = adjoint_next[0]
    bulk_here = bulk[0]
    buoy_here = buoyancy[0]
    cells_x, cells_y, depth = wave_cur.shape
    adjoint_scaled = bulk_here * adjoint_current
    buoy_rimmed = padded(buoy_here.astype(jnp.bfloat16), (("ap", 2),), 1).astype(buoy_here.dtype)
    buoy_pad = jnp.pad(buoy_rimmed, ((1, 1), (1, 1), (0, 0)))
    receiver_cells = receiver_cell[0]
    lap_now = operate(wave_cur, buoy_here, buoy_pad, None)
    wave_mid = 2.0 * wave_cur - wave_old + STEP * bulk_here * lap_now
    lap_mid = operate(wave_mid, buoy_here, buoy_pad, None)
    wave_end = 2.0 * wave_mid - wave_cur + STEP * bulk_here * lap_mid
    resid_mid = wave_mid.reshape(-1)[receiver_cells] - observed[:, 0]
    resid_end = wave_end.reshape(-1)[receiver_cells] - observed[:, 1]

    def inject(residual):
        base = jnp.zeros((cells_x * cells_y * depth,), jnp.float32)
        return base.at[receiver_cells].add(residual).reshape(cells_x, cells_y, depth)

    adjoint_mid = (
        2.0 * adjoint_current
        - adjoint_old
        + STEP * operate(adjoint_scaled, buoy_here, buoy_pad, None)
        + inject(resid_end)
    )
    adjoint_end = (
        2.0 * adjoint_mid
        - adjoint_current
        + STEP * operate(bulk_here * adjoint_mid, buoy_here, buoy_pad, None)
        + inject(resid_mid)
    )
    image = STEP * (adjoint_mid * lap_mid + adjoint_end * lap_now)
    tile_total = cells_x * (cells_y // TILE_CELLS_SECOND)
    tile_rows = image.reshape(tile_total, TILE_CELLS_SECOND, depth)
    owners = tile_owner[:, 0]
    tile_cap = 4
    slot_at = owners * tile_cap + ranking(owners, shot_count)
    flat_tiles = tile_rows.reshape(tile_total, TILE_CELLS_SECOND * depth)
    send_slots = jnp.full((shot_count * tile_cap,), MT_DEV, jnp.int32).at[slot_at].set(tile_slot)
    got_slots = lax.all_to_all(
        send_slots.reshape(shot_count, tile_cap), "shot", split_axis=0, concat_axis=0, tiled=True
    ).reshape(-1)
    send_tiles = jnp.zeros((shot_count * tile_cap, TILE_CELLS_SECOND * depth), jnp.float32)
    send_tiles = send_tiles.at[slot_at].set(flat_tiles)
    got_tiles = lax.all_to_all(
        send_tiles.reshape(shot_count, tile_cap * TILE_CELLS_SECOND, depth),
        "shot",
        split_axis=0,
        concat_axis=0,
        tiled=True,
    ).reshape(shot_count * tile_cap, TILE_CELLS_SECOND * depth)
    selector = (jnp.arange(MT_DEV, dtype=jnp.int32)[:, None] == got_slots[None, :])
    summed = jnp.dot(
        selector.astype(jnp.float32),
        got_tiles,
        precision=lax.Precision.HIGHEST,
        preferred_element_type=jnp.float32,
    )
    model_grad = summed.reshape(MT_DEV, TILE_CELLS_SECOND, depth)
    return (model_grad, wave_end[None], adjoint_end[None])


def solution(mesh):
    placed = (
        P("shot", None, None, "ap"),
        P("shot", None, None, "ap"),
        P("shot", None, None, "ap"),
        P("shot", None, None, "ap"),
        P("shot", None, None, "ap"),
        P("shot", None, None, "ap"),
        P(("shot", "ap"), None),
        P("shot", None, None),
        P(("shot", "ap"), None),
        P(("shot", "ap")),
        P("shot", "ap"),
        P("shot", None),
        P("shot"),
    )
    return jax.shard_map(
        local,
        mesh=mesh,
        in_specs=placed,
        out_specs=(P("shot", None, "ap"), P("shot", None, None, "ap"), P("shot", None, None, "ap")),
        check_vma=False,
    )
```

```python
import functools

import jax
import jax.numpy as jnp
from jax import lax
from jax.experimental import pallas as pl
from jax.experimental.pallas import tpu as pltpu
from jax.sharding import PartitionSpec as P

STEP = 0.08
MT_DEV = 8
CAP = 2
CAPT = 4
CLASSES = 16
CODE_ZERO = 4096.0
VMEM_LIMIT = 56 * 1024 * 1024

F32 = jnp.float32
BF16 = jnp.bfloat16
I32 = jnp.int32


def call(kernel, name, out_shape, scratch=(), smem=()):
    def run(*args):
        specs = [
            pl.BlockSpec(memory_space=pltpu.SMEM if i in smem else pltpu.VMEM)
            for i in range(len(args))
        ]
        outs = jax.tree.map(lambda s: pl.BlockSpec(memory_space=pltpu.VMEM), out_shape)
        return pl.pallas_call(
            kernel,
            out_shape=out_shape,
            in_specs=specs,
            out_specs=outs,
            scratch_shapes=list(scratch),
            name=name,
            compiler_params=pltpu.CompilerParams(vmem_limit_bytes=VMEM_LIMIT),
        )(*args)

    return run


def sds(shape, dtype=F32):
    return jax.ShapeDtypeStruct(shape, dtype)


def iota(shape, dim):
    return lax.broadcasted_iota(I32, shape, dim)


def pieces(value):
    first = value.astype(BF16)
    rest = value - first.astype(F32)
    second = rest.astype(BF16)
    third = (rest - second.astype(F32)).astype(BF16)
    return first, second, third


def exact_dot(onehot, value):
    first, second, third = pieces(value)
    out = jnp.dot(onehot, third, preferred_element_type=F32)
    out = out + jnp.dot(onehot, second, preferred_element_type=F32)
    return out + jnp.dot(onehot, first, preferred_element_type=F32)


def as_column(row):
    size = row.shape[1]
    eye = iota((size, size), 0) == iota((size, size), 1)
    return jnp.sum(jnp.where(eye, row, 0), axis=1, keepdims=True)


def rank_row(keys):
    size = keys.shape[1]
    first, second = iota((size, size), 0), iota((size, size), 1)
    same = (as_column(keys) == keys) & (first < second)
    return jnp.sum(same.astype(F32), axis=0, keepdims=True)


def face_row(plane, half, high):
    rows, lanes = plane.shape
    column = jnp.where(high, plane[:, lanes - 1 : lanes], plane[:, 0:1])
    here = iota((rows, lanes), 1) == iota((rows, lanes), 0) + half * rows
    return jnp.sum(jnp.where(here, column, 0.0), axis=0, keepdims=True)


def face_planes(stored, kind, pair, half, low, rows):
    lanes = stored.shape[1]
    target = jnp.where(low, lanes - 1, 0)
    shift = lax.rem(target - (kind * 16 + pair) + 2 * lanes, lanes)
    return pltpu.roll(stored[half * rows : (half + 1) * rows, :], shift, 1)


def along_second(plane):
    rows, lanes = plane.shape
    place = iota((rows, lanes), 0)
    up = jnp.where(place == rows - 1, 0.0, pltpu.roll(plane, rows - 1, 0))
    down = jnp.where(place == 0, 0.0, pltpu.roll(plane, 1, 0))
    return up, down


def along_depth(plane, halo, is_low, is_high):
    rows, lanes = plane.shape
    place = iota((rows, lanes), 1)
    up = jnp.where(place == lanes - 1, halo * is_low, pltpu.roll(plane, lanes - 1, 1))
    down = jnp.where(place == 0, halo * is_high, pltpu.roll(plane, 1, 1))
    return up, down


def around(load, x, last, halo, is_low, is_high):
    here = load(x)
    after = load(jnp.minimum(x + 1, last)) * (x < last).astype(F32)
    before = load(jnp.maximum(x - 1, 0)) * (x > 0).astype(F32)
    return here, (
        after,
        before,
        *along_second(here),
        *along_depth(here, halo, is_low, is_high),
    )


def weights(load, x, last, halo, is_low, is_high):
    here, sides = around(load, x, last, halo, is_low, is_high)
    return [0.5 * (here + side) for side in sides]


def operate(load, x, last, halo, is_low, is_high, factors):
    here, sides = around(load, x, last, halo, is_low, is_high)
    total = factors[0] * (sides[0] - here)
    for factor, side in zip(factors[1:], sides[1:]):
        total = total + factor * (side - here)
    return here, total


def which_half():
    half = lax.axis_index("ap")
    low = half == 0
    return low, low.astype(F32), (half == 1).astype(F32)


def faces_kernel(now, buoy, bulk, nxt, out):
    low, _, _ = which_half()
    out[...] = jnp.zeros_like(out)

    def body(pair, carry):
        for kind in range(3):
            row = jnp.zeros((1, now.shape[2]), F32)
            for half in range(2):
                x = 2 * pair + half
                plane = (now[x], buoy[x], None)[kind] if kind < 2 else bulk[x] * nxt[x]
                row = row + face_row(plane, half, low)
            out[pl.ds(kind * 16 + pair, 1), :] = row
        return carry

    lax.fori_loop(0, now.shape[0] // 2, body, 0)


def stored_faces(faces, scratch):
    copies = scratch.shape[0] // faces.shape[0]
    scratch[...] = jnp.transpose(jnp.concatenate([faces[...]] * copies, axis=0))


def first_kernel(
    faces, now, prev, bulk, buoy, nxt, late, lap_out, mid_out, base_out, face_out, stored
):
    low, is_low, is_high = which_half()
    stored_faces(faces, stored)
    count, rows, lanes = now.shape
    last = count - 1

    def body(pair, carry):
        row = jnp.zeros((1, lanes), F32)
        for half in range(2):
            x = 2 * pair + half
            halos = [face_planes(stored, k, pair, half, low, rows) for k in range(3)]
            factors = weights(lambda i: buoy[i], x, last, halos[1], is_low, is_high)
            here, lap = operate(lambda i: now[i], x, last, halos[0], is_low, is_high, factors)
            lap_out[x] = lap
            scale = STEP * bulk[x]
            mid = 2.0 * here - prev[x] + scale * lap
            mid_out[x] = mid
            row = row + face_row(mid, half, low)
            _, lap_adj = operate(
                lambda i: bulk[i] * nxt[i], x, last, halos[2], is_low, is_high, factors
            )
            base_out[x] = 2.0 * nxt[x] - late[x] + STEP * lap_adj
        face_out[pl.ds(pair, 1), :] = row
        return carry

    lax.fori_loop(0, count // 2, body, 0)


def second_kernel(faces, mid_face, mid, now, bulk, buoy, lap_out, end_out, stored, stored_mid):
    low, is_low, is_high = which_half()
    stored_faces(faces, stored)
    stored_faces(mid_face, stored_mid)
    count, rows, lanes = now.shape
    last = count - 1

    def body(pair, carry):
        for half in range(2):
            x = 2 * pair + half
            halo_b = face_planes(stored, 1, pair, half, low, rows)
            halo_v = face_planes(stored_mid, 0, pair, half, low, rows)
            factors = weights(lambda i: buoy[i], x, last, halo_b, is_low, is_high)
            here, lap = operate(lambda i: mid[i], x, last, halo_v, is_low, is_high, factors)
            lap_out[x] = lap
            end_out[x] = 2.0 * here - now[x] + (STEP * bulk[x]) * lap
        return carry

    lax.fori_loop(0, count // 2, body, 0)


def pack_traces_kernel(groups, receivers, traces, out):
    keys = groups[...]
    place = keys.astype(F32) * CAP + rank_row(keys)
    slots = out.shape[0]
    count, samples = traces.shape
    chosen = (iota((slots, count), 0).astype(F32) == place).astype(F32).astype(BF16)
    ids = as_column(receivers[...].astype(F32))
    ids = jnp.where(iota((count, 128), 1) == 0, ids, 0.0).astype(BF16)
    out[:, :samples] = jnp.dot(chosen, traces[...], preferred_element_type=F32).astype(BF16)
    out[:, samples:] = jnp.dot(chosen, ids, preferred_element_type=F32).astype(BF16)


def places_kernel(
    cells, mid, end, owners, slots, seen_out, hot_depth_out, hot_rows_out, place_out, cls_out,
    spot_out, ids_out,
):
    lanes = 128
    count = cells.shape[1]
    rows = hot_rows_out.shape[0]
    cell_row = cells[...]
    row_of = lax.shift_right_logical(cell_row, 7)
    hot_rows_out[...] = (iota((rows, count), 0) == row_of).astype(F32).astype(BF16)
    cell_col = as_column(cell_row)
    hot_depth = (iota((count, lanes), 1) == (cell_col & (lanes - 1))).astype(F32)
    hot_depth_out[...] = hot_depth
    row_col = lax.shift_right_logical(cell_col, 7)
    picked = jnp.zeros((count, 2 * lanes), F32)
    chunk = 256
    for start in range(0, rows, chunk):
        hot = (iota((count, chunk), 1) + start == row_col).astype(F32).astype(BF16)
        planes = slice(start // 64, (start + chunk) // 64)
        both = jnp.concatenate(
            [mid[planes].reshape(chunk, lanes), end[planes].reshape(chunk, lanes)], axis=1
        )
        picked = picked + exact_dot(hot, both)
    seen_mid = jnp.sum(picked[:, :lanes] * hot_depth, axis=1, keepdims=True)
    seen_end = jnp.sum(picked[:, lanes:] * hot_depth, axis=1, keepdims=True)
    seen_out[...] = jnp.where(iota((count, lanes), 1) == 0, seen_mid, seen_end)

    owner = owners[...]
    tiles = owner.shape[1]
    rank = rank_row(owner).astype(I32)
    cls = owner & (CLASSES - 1)
    spot = lax.shift_right_logical(owner, 4) * CAPT + rank
    per_class = 8 * CAPT
    place_out[...] = cls * (per_class + 1) + spot
    cls_hot = (iota((CLASSES, tiles), 0) == cls).astype(F32).astype(BF16)
    cls_out[...] = cls_hot
    spot_hot = (iota((tiles, lanes), 1) == as_column(spot)).astype(F32)
    spot_out[...] = spot_hot
    slot_col = as_column(slots[...]).astype(F32)
    ids_out[...] = jnp.dot(
        cls_hot, (spot_hot * slot_col).astype(BF16), preferred_element_type=F32
    )


def inject_kernel(
    rows_in, filters, seen, hot_depth, hot_rows, base, bulk, mid_out, add_out, face_out
):
    low, _, _ = which_half()
    samples = filters.shape[1]
    count, lanes = hot_depth.shape
    slots = rows_in.shape[0]
    last_dims = (((1,), (1,)), ((), ()))
    values = lax.dot_general(
        rows_in[:, :samples], filters[...], last_dims, preferred_element_type=F32
    )
    pick = ((iota((8, 128), 0) == 0) & (iota((8, 128), 1) == 0)).astype(F32).astype(BF16)
    ids = lax.dot_general(pick, rows_in[:, samples:], last_dims, preferred_element_type=F32)
    hot = (iota((count, slots), 0).astype(F32) == ids[0:1, :]).astype(F32).astype(BF16)
    observed = exact_dot(hot, values)
    resid_mid = seen[:, 0:1] - observed[:, 0:1]
    resid_end = seen[:, 1:2] - observed[:, 1:2]
    spread = jnp.concatenate([hot_depth[...] * resid_end, hot_depth[...] * resid_mid], axis=1)
    first, second, third = pieces(spread)

    def body(pair, carry):
        hot_here = hot_rows[pl.ds(pl.multiple_of(pair * 128, 128), 128), :]
        added = jnp.dot(hot_here, third, preferred_element_type=F32)
        added = added + jnp.dot(hot_here, second, preferred_element_type=F32)
        added = added + jnp.dot(hot_here, first, preferred_element_type=F32)
        row = jnp.zeros((1, lanes), F32)
        for half in range(2):
            x = 2 * pair + half
            field = base[x] + added[half * 64 : (half + 1) * 64, :lanes]
            mid_out[x] = field
            add_out[x] = added[half * 64 : (half + 1) * 64, lanes:]
            row = row + face_row(bulk[x] * field, half, low)
        face_out[pl.ds(pair, 1), :] = row
        return carry

    lax.fori_loop(0, base.shape[0] // 2, body, 0)


def image_kernel(
    faces, adj_face, mid, add, nxt, bulk, buoy, lap_mid, lap_now, place, cls_hot, spot_hot, ids,
    last_out, send_out, stored, stored_adj, codes,
):
    low, is_low, is_high = which_half()
    stored_faces(faces, stored)
    stored_faces(adj_face, stored_adj)
    count, rows, lanes = mid.shape
    last = count - 1
    tiles = rows // 8
    per_class = send_out.shape[0] // CLASSES

    def clear(c, carry):
        send_out[pl.ds(c * per_class, per_class)] = jnp.zeros((per_class, 8, lanes), jnp.int16)
        return carry

    lax.fori_loop(0, CLASSES, clear, 0)

    def body(pair, carry):
        for half in range(2):
            x = 2 * pair + half
            halo_b = face_planes(stored, 1, pair, half, low, rows)
            halo_v = face_planes(stored_adj, 0, pair, half, low, rows)
            factors = weights(lambda i: buoy[i], x, last, halo_b, is_low, is_high)
            _, lap = operate(
                lambda i: bulk[i] * mid[i], x, last, halo_v, is_low, is_high, factors
            )
            here = mid[x]
            end = 2.0 * here - nxt[x] + STEP * lap + add[x]
            last_out[x] = end
            image = (STEP * (here * lap_mid[x] + end * lap_now[x])).reshape(tiles, 8, lanes)
            peak = jnp.max(jnp.max(jnp.abs(image), axis=1), axis=1, keepdims=True)
            code = jnp.ceil(16.0 * jnp.log2(jnp.maximum(peak, 1e-30))) + 1.0
            codes[pl.ds(pl.multiple_of(x * tiles, tiles), tiles), :] = jnp.broadcast_to(
                code + CODE_ZERO, (tiles, lanes)
            )
            gain = jnp.broadcast_to(32767.0 * jnp.exp2(code * (-1.0 / 16.0)), (tiles, lanes))
            whole = jnp.round(image * gain[:, None, :]).astype(I32).astype(jnp.int16)
            for t in range(tiles):
                send_out[place[0, x * tiles + t]] = whole[t]
        return carry

    lax.fori_loop(0, count // 2, body, 0)
    code = codes[...]
    upper = jnp.floor(code * (1.0 / 64.0))
    lower = code - 64.0 * upper
    hot = cls_hot[...]
    spread = spot_hot[...]
    sent = 64.0 * jnp.dot(hot, (spread * upper).astype(BF16), preferred_element_type=F32)
    sent = sent + jnp.dot(hot, (spread * lower).astype(BF16), preferred_element_type=F32)
    place_row = iota((8, lanes), 0)
    for c in range(CLASSES):
        tile = jnp.where(
            place_row == 0,
            ids[c : c + 1, :],
            jnp.where(place_row == 1, sent[c : c + 1, :], 0.0),
        )
        send_out[c * per_class + per_class - 1] = tile.astype(I32).astype(jnp.int16)


def combine_kernel(slots, gains, got, out, *partial):
    per_class = got.shape[0] // CLASSES
    used = per_class - 1
    for part in partial:
        part[...] = jnp.zeros_like(part)

    def body(src, carry):
        for s in range(used):
            part = partial[s % CAPT]
            at = (s // CAPT) * MT_DEV + slots[src, s]
            value = got[src * per_class + s].astype(I32).astype(F32) * gains[src, s]
            part[at] = part[at] + value
        return carry

    lax.fori_loop(0, CLASSES, body, 0)
    total = partial[0][...]
    for part in partial[1:]:
        total = total + part[...]
    out[...] = total


def swap(face):
    return lax.ppermute(face, "ap", [(0, 1), (1, 0)])


def local(
    wave_prev,
    wave_now,
    adjoint_late,
    adjoint_next,
    bulk,
    buoyancy,
    traces,
    group_filter,
    trace_group,
    trace_receiver,
    receiver_cell,
    tile_owner,
    tile_slot,
):
    shots = lax.axis_size("shot")
    rings = shots // CLASSES
    prev, now, late, nxt = wave_prev[0], wave_now[0], adjoint_late[0], adjoint_next[0]
    bulk, buoy = bulk[0], buoyancy[0]
    count, rows, lanes = now.shape
    field = sds(now.shape)
    samples = traces.shape[1]
    face = sds((16, lanes))
    square = pltpu.VMEM((lanes, lanes), F32)

    packed = call(pack_traces_kernel, "pack_traces", sds((shots * CAP, samples + 128), BF16))(
        trace_group.reshape(1, -1), trace_receiver.reshape(1, -1), traces
    )
    got_rows = lax.all_to_all(
        packed.reshape(shots, CAP, samples + 128), "shot", split_axis=0, concat_axis=0, tiled=True
    ).reshape(shots * CAP, samples + 128)

    faces = swap(call(faces_kernel, "faces", sds((64, lanes)))(now, buoy, bulk, nxt))
    lap_now, wave_mid, adj_base, mid_face = call(
        first_kernel, "first_step", (field, field, field, face), [square]
    )(faces, now, prev, bulk, buoy, nxt, late)
    lap_mid, wave_end = call(second_kernel, "second_step", (field, field), [square, square])(
        faces, swap(mid_face), wave_mid, now, bulk, buoy
    )
    receivers = receiver_cell.shape[1]
    tiles = tile_owner.shape[0]
    seen, hot_depth, hot_rows, place, cls_hot, spot_hot, ids = call(
        places_kernel,
        "places",
        (
            sds((receivers, lanes)),
            sds((receivers, lanes)),
            sds((count * rows, receivers), BF16),
            sds((1, tiles), I32),
            sds((CLASSES, tiles), BF16),
            sds((tiles, lanes)),
            sds((CLASSES, lanes)),
        ),
    )(receiver_cell, wave_mid, wave_end, tile_owner.reshape(1, -1), tile_slot.reshape(1, -1))
    filters = jnp.pad(group_filter[0], ((0, 14), (0, 0)))
    adj_mid, adj_add, adj_face = call(inject_kernel, "inject", (field, field, face))(
        got_rows, filters, seen, hot_depth, hot_rows, adj_base, bulk
    )
    per_class = (shots // CLASSES) * CAPT + 1
    adj_end, send = call(
        image_kernel,
        "image",
        (field, sds((CLASSES * per_class, 8, lanes), jnp.int16)),
        [square, square, pltpu.VMEM((tiles, lanes), F32)],
        smem=(9,),
    )(
        faces, swap(adj_face), adj_mid, adj_add, nxt, bulk, buoy, lap_mid, lap_now, place,
        cls_hot, spot_hot, ids,
    )
    near = [[r * CLASSES + c for c in range(CLASSES)] for r in range(rings)]
    far = [[r * CLASSES + c for r in range(rings)] for c in range(CLASSES)]
    got = lax.all_to_all(
        send.reshape(CLASSES, per_class * 8, lanes),
        "shot",
        split_axis=0,
        concat_axis=0,
        axis_index_groups=near,
        tiled=True,
    ).reshape(CLASSES, per_class, 8, lanes)
    used = per_class - 1
    slots = got[:, used, 0, :used].astype(I32)
    code = got[:, used, 1, :used].astype(F32)
    gains = jnp.where(code > 0, jnp.exp2((code - CODE_ZERO) * (1.0 / 16.0)) * (1.0 / 32767.0), 0.0)
    owned = rings * MT_DEV
    dense = call(
        combine_kernel,
        "combine",
        sds((owned, 8, lanes)),
        [pltpu.VMEM((owned, 8, lanes), F32)] * CAPT,
        smem=(0, 1),
    )(slots, gains, got.reshape(CLASSES * per_class, 8, lanes))
    shared = lax.all_to_all(
        dense.reshape(rings, MT_DEV * 8, lanes),
        "shot",
        split_axis=0,
        concat_axis=0,
        axis_index_groups=far,
        tiled=True,
    )
    model_grad = jnp.sum(shared, axis=0).reshape(MT_DEV, 8, lanes)
    return (model_grad, wave_end[None], adj_end[None])


def solution(mesh):
    placed = (
        P("shot", None, None, "ap"),
        P("shot", None, None, "ap"),
        P("shot", None, None, "ap"),
        P("shot", None, None, "ap"),
        P("shot", None, None, "ap"),
        P("shot", None, None, "ap"),
        P(("shot", "ap"), None),
        P("shot", None, None),
        P(("shot", "ap"), None),
        P(("shot", "ap")),
        P("shot", "ap"),
        P("shot", None),
        P("shot"),
    )
    return jax.shard_map(
        local,
        mesh=mesh,
        in_specs=placed,
        out_specs=(P("shot", None, "ap"), P("shot", None, None, "ap"), P("shot", None, None, "ap")),
        check_vma=False,
    )
```

```python
import jax
import jax.numpy as jnp
from jax import lax
from jax.experimental import pallas as pl
from jax.experimental.pallas import tpu as pltpu
from jax.sharding import PartitionSpec as P

STEP = 0.08
MT_DEV = 8
CAP = 2
CAPT = 4
CLASSES = 16
CODE_ZERO = 4096.0
VMEM_LIMIT = 16 * 1024 * 1024

F32 = jnp.float32
BF16 = jnp.bfloat16
I32 = jnp.int32


def call(kernel, name, out_shape, scratch=(), smem=(), hbm_out=()):
    def run(*args):
        args = [
            x if i in smem else pltpu.with_memory_space_constraint(x, pltpu.VMEM)
            for i, x in enumerate(args)
        ]
        specs = [
            pl.BlockSpec(memory_space=pltpu.SMEM if i in smem else pltpu.VMEM)
            for i in range(len(args))
        ]
        flat, tree = jax.tree.flatten(out_shape)
        outs = [pl.BlockSpec(memory_space=pltpu.VMEM) for _ in flat]
        shapes = [
            s if i in hbm_out else pltpu.VMEM(s.shape, s.dtype) for i, s in enumerate(flat)
        ]
        return pl.pallas_call(
            kernel,
            out_shape=jax.tree.unflatten(tree, shapes),
            in_specs=specs,
            out_specs=jax.tree.unflatten(tree, outs),
            scratch_shapes=list(scratch),
            name=name,
            compiler_params=pltpu.CompilerParams(vmem_limit_bytes=VMEM_LIMIT),
        )(*args)

    return run


def sds(shape, dtype=F32):
    return jax.ShapeDtypeStruct(shape, dtype)


def iota(shape, dim):
    return lax.broadcasted_iota(I32, shape, dim)


def pieces(value):
    first = value.astype(BF16)
    rest = value - first.astype(F32)
    second = rest.astype(BF16)
    third = (rest - second.astype(F32)).astype(BF16)
    return first, second, third


def exact_dot(onehot, value):
    first, second, third = pieces(value)
    out = jnp.dot(onehot, third, preferred_element_type=F32)
    out = out + jnp.dot(onehot, second, preferred_element_type=F32)
    return out + jnp.dot(onehot, first, preferred_element_type=F32)


def as_column(row):
    size = row.shape[1]
    eye = iota((size, size), 0) == iota((size, size), 1)
    return jnp.sum(jnp.where(eye, row, 0), axis=1, keepdims=True)


def rank_row(keys):
    size = keys.shape[1]
    first, second = iota((size, size), 0), iota((size, size), 1)
    same = (as_column(keys) == keys) & (first < second)
    return jnp.sum(same.astype(F32), axis=0, keepdims=True)


def which_half():
    low = lax.axis_index("ap") == 0
    return low


def edge_lane(low, lanes):
    return jnp.where(low, lanes - 1, 0)


def put_face(held, plane, at, low):
    lanes = plane.shape[1]
    shift = lax.rem(at - edge_lane(low, lanes) + lanes, lanes)
    return jnp.where(iota(plane.shape, 1) == at, pltpu.roll(plane, shift, 1), held)


def take_face(held, at, low):
    lanes = held.shape[1]
    edge = edge_lane(low, lanes)
    shift = lax.rem(edge - at + lanes, lanes)
    return jnp.where(iota(held.shape, 1) == edge, pltpu.roll(held, shift, 1), 0.0)


def next_second(plane):
    rows = plane.shape[0]
    rolled = pltpu.roll(plane, rows - 1, 0)
    return jnp.where(iota(plane.shape, 0) == rows - 1, 0.0, rolled)


def next_depth(plane, halo):
    lanes = plane.shape[1]
    rolled = pltpu.roll(plane, lanes - 1, 1)
    return jnp.where(iota(plane.shape, 1) == lanes - 1, halo, rolled)


def sums(here, after, halo):
    return here, here + after, here + next_second(here), here + next_depth(here, halo), here + halo


def twice_operate(here, after, halo, before_flux, side_sums):
    buoy, along_x, along_y, along_z, low_z = side_sums
    flux = along_x * (after - here)
    total = flux - before_flux
    flux_y = along_y * (next_second(here) - here)
    under = jnp.where(iota(here.shape, 0) == 0, buoy * here, pltpu.roll(flux_y, 1, 0))
    total = total + (flux_y - under)
    flux_z = along_z * (next_depth(here, halo) - here)
    below = jnp.where(iota(here.shape, 1) == 0, low_z * (here - halo), pltpu.roll(flux_z, 1, 1))
    return total + (flux_z - below), flux


def following(x, count):
    return jnp.minimum(x + 1, count - 1), (x < count - 1).astype(F32)


def faces_kernel(now, buoy, bulk, nxt, out):
    low = which_half()
    count = now.shape[0]

    def body(x, held):
        held = put_face(held, now[x], x, low)
        held = put_face(held, buoy[x], 32 + x, low)
        return put_face(held, bulk[x] * nxt[x], 64 + x, low)

    out[...] = lax.fori_loop(0, count, body, jnp.zeros(now.shape[1:], F32), unroll=2)


def first_kernel(
    faces, now, prev, bulk, buoy, nxt, late, lap_out, mid_out, base_out, face_out
):
    low = which_half()
    count = now.shape[0]

    def body(x, carry):
        flux_v, flux_a, held = carry
        after, keep = following(x, count)
        side_sums = sums(buoy[x], keep * buoy[after], take_face(faces[...], 32 + x, low))
        here = now[x]
        lap, flux_v = twice_operate(
            here, keep * now[after], take_face(faces[...], x, low), flux_v, side_sums
        )
        lap = 0.5 * lap
        lap_out[x] = lap
        mid = 2.0 * here - prev[x] + (STEP * bulk[x]) * lap
        mid_out[x] = mid
        held = put_face(held, mid, x, low)
        scaled = bulk[x] * nxt[x]
        scaled_after = (keep * bulk[after]) * nxt[after]
        lap, flux_a = twice_operate(
            scaled, scaled_after, take_face(faces[...], 64 + x, low), flux_a, side_sums
        )
        base_out[x] = 2.0 * nxt[x] - late[x] + (0.5 * STEP) * lap
        return flux_v, flux_a, held

    start = (buoy[0] * now[0], buoy[0] * (bulk[0] * nxt[0]), jnp.zeros(now.shape[1:], F32))
    _, _, held = lax.fori_loop(0, count, body, start)
    face_out[...] = held


def second_kernel(faces, mid_face, mid, now, bulk, buoy, lap_out, end_out):
    low = which_half()
    count = now.shape[0]

    def body(x, flux):
        after, keep = following(x, count)
        side_sums = sums(buoy[x], keep * buoy[after], take_face(faces[...], 32 + x, low))
        here = mid[x]
        lap, flux = twice_operate(
            here, keep * mid[after], take_face(mid_face[...], x, low), flux, side_sums
        )
        lap = 0.5 * lap
        lap_out[x] = lap
        end_out[x] = 2.0 * here - now[x] + (STEP * bulk[x]) * lap
        return flux

    lax.fori_loop(0, count, body, buoy[0] * mid[0])


def pack_traces_kernel(groups, receivers, traces, out):
    keys = groups[...]
    place = keys.astype(F32) * CAP + rank_row(keys)
    slots = out.shape[0]
    count, samples = traces.shape
    chosen = (iota((slots, count), 0).astype(F32) == place).astype(F32).astype(BF16)
    ids = as_column(receivers[...].astype(F32))
    ids = jnp.where(iota((count, 128), 1) == 0, ids, 0.0).astype(BF16)
    out[:, :samples] = jnp.dot(chosen, traces[...], preferred_element_type=F32).astype(BF16)
    out[:, samples:] = jnp.dot(chosen, ids, preferred_element_type=F32).astype(BF16)


def places_kernel(
    at, cells, mid, end, owners, slots, seen_out, hot_depth_out, place_out, cls_out, spot_out,
    ids_out, rows_mid, rows_end,
):
    lanes = 128
    count = cells.shape[1]

    def body(r, carry):
        row = lax.shift_right_logical(at[0, r], 7)
        rows_mid[pl.ds(r, 1), :] = mid[pl.ds(row, 1), :]
        rows_end[pl.ds(r, 1), :] = end[pl.ds(row, 1), :]
        return carry

    lax.fori_loop(0, count, body, 0, unroll=8)
    cell_col = as_column(cells[...])
    here = iota((count, lanes), 1) == (cell_col & (lanes - 1))
    hot_depth_out[...] = here.astype(F32)
    seen_mid = jnp.sum(jnp.where(here, rows_mid[...], 0.0), axis=1, keepdims=True)
    seen_end = jnp.sum(jnp.where(here, rows_end[...], 0.0), axis=1, keepdims=True)
    seen_out[...] = jnp.where(iota((count, lanes), 1) == 0, seen_mid, seen_end)

    owner = owners[...]
    tiles = owner.shape[1]
    rank = rank_row(owner).astype(I32)
    cls = owner & (CLASSES - 1)
    spot = lax.shift_right_logical(owner, 4) * CAPT + rank
    per_class = 8 * CAPT
    place_out[...] = cls * (per_class + 1) + spot
    cls_hot = (iota((CLASSES, tiles), 0) == cls).astype(F32).astype(BF16)
    cls_out[...] = cls_hot
    spot_hot = (iota((tiles, lanes), 1) == as_column(spot)).astype(F32)
    spot_out[...] = spot_hot
    slot_col = as_column(slots[...]).astype(F32)
    ids_out[...] = jnp.dot(
        cls_hot, (spot_hot * slot_col).astype(BF16), preferred_element_type=F32
    )


def inject_kernel(
    at, rows_in, filters, seen, hot_depth, base, bulk, mid_out, add_out, face_out, sum_mid, sum_end
):
    low = which_half()
    samples = filters.shape[1]
    count, lanes = hot_depth.shape
    slots = rows_in.shape[0]
    last_dims = (((1,), (1,)), ((), ()))
    values = lax.dot_general(
        rows_in[:, :samples], filters[...], last_dims, preferred_element_type=F32
    )
    pick = ((iota((8, 128), 0) == 0) & (iota((8, 128), 1) == 0)).astype(F32).astype(BF16)
    ids = lax.dot_general(pick, rows_in[:, samples:], last_dims, preferred_element_type=F32)
    hot = (iota((count, slots), 0).astype(F32) == ids[0:1, :]).astype(F32).astype(BF16)
    observed = exact_dot(hot, values)
    sum_mid[...] = hot_depth[...] * (seen[:, 0:1] - observed[:, 0:1])
    sum_end[...] = hot_depth[...] * (seen[:, 1:2] - observed[:, 1:2])
    mid_out[...] = base[...]
    add_out[...] = jnp.zeros_like(add_out)

    def body(r, carry):
        row = lax.shift_right_logical(at[0, r], 7)
        mid_out[pl.ds(row, 1), :] = mid_out[pl.ds(row, 1), :] + sum_end[pl.ds(r, 1), :]
        add_out[pl.ds(row, 1), :] = add_out[pl.ds(row, 1), :] + sum_mid[pl.ds(r, 1), :]
        return carry

    lax.fori_loop(0, count, body, 0, unroll=8)
    rows = bulk.shape[1]

    def edge(x, held):
        field = mid_out[pl.ds(pl.multiple_of(x * rows, rows), rows), :]
        return put_face(held, bulk[x] * field, x, low)

    face_out[...] = lax.fori_loop(
        0, bulk.shape[0], edge, jnp.zeros(bulk.shape[1:], F32), unroll=2
    )


def image_kernel(
    faces, adj_face, mid, add, nxt, bulk, buoy, lap_mid, lap_now, place, cls_hot, spot_hot, ids,
    last_out, send_out, codes,
):
    low = which_half()
    count, rows, lanes = mid.shape
    tiles = rows // 8
    per_class = send_out.shape[0] // CLASSES

    def clear(c, carry):
        send_out[pl.ds(c * per_class, per_class)] = jnp.zeros((per_class, 8, lanes), jnp.int16)
        return carry

    lax.fori_loop(0, CLASSES, clear, 0)

    def body(x, flux):
        after, keep = following(x, count)
        side_sums = sums(buoy[x], keep * buoy[after], take_face(faces[...], 32 + x, low))
        here = mid[x]
        lap, flux = twice_operate(
            bulk[x] * here,
            (keep * bulk[after]) * mid[after],
            take_face(adj_face[...], x, low),
            flux,
            side_sums,
        )
        end = 2.0 * here - nxt[x] + (0.5 * STEP) * lap + add[x]
        last_out[x] = end
        image = (STEP * (here * lap_mid[x] + end * lap_now[x])).reshape(tiles, 8, lanes)
        peak = jnp.max(jnp.max(jnp.abs(image), axis=1), axis=1, keepdims=True)
        code = jnp.ceil(16.0 * jnp.log2(jnp.maximum(peak, 1e-30))) + 1.0
        codes[pl.ds(pl.multiple_of(x * tiles, tiles), tiles), :] = jnp.broadcast_to(
            code + CODE_ZERO, (tiles, lanes)
        )
        gain = jnp.broadcast_to(32767.0 * jnp.exp2(code * (-1.0 / 16.0)), (tiles, lanes))
        whole = jnp.round(image * gain[:, None, :]).astype(I32).astype(jnp.int16)
        for t in range(tiles):
            send_out[place[0, x * tiles + t]] = whole[t]
        return flux

    lax.fori_loop(0, count, body, buoy[0] * (bulk[0] * mid[0]))
    code = codes[...]
    upper = jnp.floor(code * (1.0 / 64.0))
    lower = code - 64.0 * upper
    hot = cls_hot[...]
    spread = spot_hot[...]
    sent = 64.0 * jnp.dot(hot, (spread * upper).astype(BF16), preferred_element_type=F32)
    sent = sent + jnp.dot(hot, (spread * lower).astype(BF16), preferred_element_type=F32)
    place_row = iota((8, lanes), 0)
    for c in range(CLASSES):
        tile = jnp.where(
            place_row == 0,
            ids[c : c + 1, :],
            jnp.where(place_row == 1, sent[c : c + 1, :], 0.0),
        )
        send_out[c * per_class + per_class - 1] = tile.astype(I32).astype(jnp.int16)


def combine_kernel(got, out, gains_v, slots_v, gains, slots, sems, *partial):
    per_class = got.shape[0] // CLASSES
    used = per_class - 1
    lanes = got.shape[2]
    for c in range(CLASSES):
        meta = got[c * per_class + used].astype(I32)
        slots_v[c : c + 1, :] = meta[0:1, :]
        code = meta[1:2, :].astype(F32)
        gain = jnp.exp2((code - CODE_ZERO) * (1.0 / 16.0)) * (1.0 / 32767.0)
        gains_v[c : c + 1, :] = jnp.where(code > 0, gain, 0.0)
    copies = [
        pltpu.make_async_copy(gains_v, gains, sems.at[0]),
        pltpu.make_async_copy(slots_v, slots, sems.at[1]),
    ]
    for copy in copies:
        copy.start()
    for part in partial:
        part[...] = jnp.zeros_like(part)
    for copy in copies:
        copy.wait()

    def body(src, carry):
        for s in range(used):
            part = partial[s % CAPT]
            at = (s // CAPT) * MT_DEV + slots[src, s]
            value = got[src * per_class + s].astype(I32).astype(F32) * gains[src, s]
            part[at] = part[at] + value
        return carry

    lax.fori_loop(0, CLASSES, body, 0)
    total = partial[0][...]
    for part in partial[1:]:
        total = total + part[...]
    out[...] = total


def swap(face):
    return lax.ppermute(face, "ap", [(0, 1), (1, 0)])


def local(
    wave_prev,
    wave_now,
    adjoint_late,
    adjoint_next,
    bulk,
    buoyancy,
    traces,
    group_filter,
    trace_group,
    trace_receiver,
    receiver_cell,
    tile_owner,
    tile_slot,
):
    shots = lax.axis_size("shot")
    rings = shots // CLASSES
    prev, now, late, nxt = wave_prev[0], wave_now[0], adjoint_late[0], adjoint_next[0]
    bulk, buoy = bulk[0], buoyancy[0]
    count, rows, lanes = now.shape
    field = sds(now.shape)
    flat = sds((count * rows, lanes))
    samples = traces.shape[1]
    face = sds((rows, lanes))

    packed = call(pack_traces_kernel, "pack_traces", sds((shots * CAP, samples + 128), BF16))(
        trace_group.reshape(1, -1), trace_receiver.reshape(1, -1), traces
    )
    got_rows = lax.all_to_all(
        packed.reshape(shots, CAP, samples + 128), "shot", split_axis=0, concat_axis=0, tiled=True
    ).reshape(shots * CAP, samples + 128)

    faces = swap(call(faces_kernel, "faces", face)(now, buoy, bulk, nxt))
    lap_now, wave_mid, adj_base, mid_face = call(
        first_kernel, "first_step", (field, field, field, face)
    )(faces, now, prev, bulk, buoy, nxt, late)
    lap_mid, wave_end = call(second_kernel, "second_step", (field, field))(
        faces, swap(mid_face), wave_mid, now, bulk, buoy
    )
    receivers = receiver_cell.shape[1]
    tiles = tile_owner.shape[0]
    per_receiver = pltpu.VMEM((receivers, lanes), F32)
    seen, hot_depth, place, cls_hot, spot_hot, ids = call(
        places_kernel,
        "places",
        (
            sds((receivers, lanes)),
            sds((receivers, lanes)),
            sds((1, tiles), I32),
            sds((CLASSES, tiles), BF16),
            sds((tiles, lanes)),
            sds((CLASSES, lanes)),
        ),
        [per_receiver, per_receiver],
        smem=(0,),
        hbm_out=(2,),
    )(
        receiver_cell,
        receiver_cell,
        wave_mid.reshape(flat.shape),
        wave_end.reshape(flat.shape),
        tile_owner.reshape(1, -1),
        tile_slot.reshape(1, -1),
    )
    filters = jnp.pad(group_filter[0], ((0, 14), (0, 0)))
    adj_mid, adj_add, adj_face = call(
        inject_kernel, "inject", (flat, flat, face), [per_receiver, per_receiver], smem=(0,)
    )(receiver_cell, got_rows, filters, seen, hot_depth, adj_base.reshape(flat.shape), bulk)
    per_class = (shots // CLASSES) * CAPT + 1
    adj_end, send = call(
        image_kernel,
        "image",
        (field, sds((CLASSES * per_class, 8, lanes), jnp.int16)),
        [pltpu.VMEM((tiles, lanes), F32)],
        smem=(9,),
    )(
        faces, swap(adj_face), adj_mid.reshape(now.shape), adj_add.reshape(now.shape), nxt, bulk,
        buoy, lap_mid, lap_now, place, cls_hot, spot_hot, ids,
    )
    near = [[r * CLASSES + c for c in range(CLASSES)] for r in range(rings)]
    far = [[r * CLASSES + c for r in range(rings)] for c in range(CLASSES)]
    got = lax.all_to_all(
        send.reshape(CLASSES, per_class * 8, lanes),
        "shot",
        split_axis=0,
        concat_axis=0,
        axis_index_groups=near,
        tiled=True,
    )
    owned = rings * MT_DEV
    table = (CLASSES, lanes)
    dense = call(
        combine_kernel,
        "combine",
        sds((owned, 8, lanes)),
        [
            pltpu.VMEM(table, F32),
            pltpu.VMEM(table, I32),
            pltpu.SMEM(table, F32),
            pltpu.SMEM(table, I32),
            pltpu.SemaphoreType.DMA((2,)),
        ]
        + [pltpu.VMEM((owned, 8, lanes), F32)] * CAPT,
    )(got.reshape(CLASSES * per_class, 8, lanes))
    shared = lax.all_to_all(
        dense.reshape(rings, MT_DEV * 8, lanes),
        "shot",
        split_axis=0,
        concat_axis=0,
        axis_index_groups=far,
        tiled=True,
    )
    model_grad = jnp.sum(shared, axis=0).reshape(MT_DEV, 8, lanes)
    return (model_grad, wave_end[None], adj_end[None])


def solution(mesh):
    placed = (
        P("shot", None, None, "ap"),
        P("shot", None, None, "ap"),
        P("shot", None, None, "ap"),
        P("shot", None, None, "ap"),
        P("shot", None, None, "ap"),
        P("shot", None, None, "ap"),
        P(("shot", "ap"), None),
        P("shot", None, None),
        P(("shot", "ap"), None),
        P(("shot", "ap")),
        P("shot", "ap"),
        P("shot", None),
        P("shot"),
    )
    return jax.shard_map(
        local,
        mesh=mesh,
        in_specs=placed,
        out_specs=(P("shot", None, "ap"), P("shot", None, None, "ap"), P("shot", None, None, "ap")),
        check_vma=False,
    )
```

```python
import jax
import jax.numpy as jnp
from jax import lax
from jax.experimental import pallas as pl
from jax.experimental.pallas import tpu as pltpu
from jax.sharding import PartitionSpec as P

STEP = 0.08
MT_DEV = 8
CAP = 2
CAPT = 4
CLASSES = 16
CODE_ZERO = 4096.0
VMEM_LIMIT = 6 * 1024 * 1024

F32 = jnp.float32
BF16 = jnp.bfloat16
I32 = jnp.int32


def call(kernel, name, out_shape, scratch=(), smem=(), hbm_out=(), free=(), hbm=()):
    def run(*args):
        spaces = [
            pltpu.SMEM if i in smem else pltpu.HBM if i in hbm else pltpu.VMEM
            for i in range(len(args))
        ]
        args = [
            pltpu.with_memory_space_constraint(x, space)
            if space is not pltpu.SMEM and i not in free
            else x
            for i, (x, space) in enumerate(zip(args, spaces))
        ]
        specs = [pl.BlockSpec(memory_space=space) for space in spaces]
        flat, tree = jax.tree.flatten(out_shape)
        outs = [pl.BlockSpec(memory_space=pltpu.VMEM) for _ in flat]
        shapes = [
            (pltpu.HBM if i in hbm_out else pltpu.VMEM)(s.shape, s.dtype)
            for i, s in enumerate(flat)
        ]
        return pl.pallas_call(
            kernel,
            out_shape=jax.tree.unflatten(tree, shapes),
            in_specs=specs,
            out_specs=jax.tree.unflatten(tree, outs),
            scratch_shapes=list(scratch),
            name=name,
            compiler_params=pltpu.CompilerParams(vmem_limit_bytes=VMEM_LIMIT),
        )(*args)

    return run


def sds(shape, dtype=F32):
    return jax.ShapeDtypeStruct(shape, dtype)


def iota(shape, dim):
    return lax.broadcasted_iota(I32, shape, dim)


def pieces(value):
    first = value.astype(BF16)
    rest = value - first.astype(F32)
    second = rest.astype(BF16)
    third = (rest - second.astype(F32)).astype(BF16)
    return first, second, third


def exact_dot(onehot, value):
    first, second, third = pieces(value)
    out = jnp.dot(onehot, third, preferred_element_type=F32)
    out = out + jnp.dot(onehot, second, preferred_element_type=F32)
    return out + jnp.dot(onehot, first, preferred_element_type=F32)


def as_column(row):
    size = row.shape[1]
    eye = iota((size, size), 0) == iota((size, size), 1)
    return jnp.sum(jnp.where(eye, row, 0), axis=1, keepdims=True)


def rank_row(keys):
    size = keys.shape[1]
    first, second = iota((size, size), 0), iota((size, size), 1)
    same = (as_column(keys) == keys) & (first < second)
    return jnp.sum(same.astype(F32), axis=0, keepdims=True)


def which_half():
    low = lax.axis_index("ap") == 0
    return low


def edge_lane(low, lanes):
    return jnp.where(low, lanes - 1, 0)


def put_face(held, plane, at, low):
    lanes = plane.shape[1]
    shift = lax.rem(at - edge_lane(low, lanes) + lanes, lanes)
    return jnp.where(iota(plane.shape, 1) == at, pltpu.roll(plane, shift, 1), held)


def take_face(held, at, low):
    lanes = held.shape[1]
    edge = edge_lane(low, lanes)
    shift = lax.rem(edge - at + lanes, lanes)
    return jnp.where(iota(held.shape, 1) == edge, pltpu.roll(held, shift, 1), 0.0)


def next_second(plane):
    rows = plane.shape[0]
    rolled = pltpu.roll(plane, rows - 1, 0)
    return jnp.where(iota(plane.shape, 0) == rows - 1, 0.0, rolled)


def next_depth(plane, halo):
    lanes = plane.shape[1]
    rolled = pltpu.roll(plane, lanes - 1, 1)
    return jnp.where(iota(plane.shape, 1) == lanes - 1, halo, rolled)


def sums(here, after, halo):
    return here, here + after, here + next_second(here), here + next_depth(here, halo), here + halo


def twice_operate(here, after, halo, before_flux, side_sums):
    buoy, along_x, along_y, along_z, low_z = side_sums
    flux = along_x * (after - here)
    total = flux - before_flux
    flux_y = along_y * (next_second(here) - here)
    under = jnp.where(iota(here.shape, 0) == 0, buoy * here, pltpu.roll(flux_y, 1, 0))
    total = total + (flux_y - under)
    flux_z = along_z * (next_depth(here, halo) - here)
    below = jnp.where(iota(here.shape, 1) == 0, low_z * (here - halo), pltpu.roll(flux_z, 1, 1))
    return total + (flux_z - below), flux


def following(x, count):
    return jnp.minimum(x + 1, count - 1), (x < count - 1).astype(F32)


def faces_kernel(now, buoy, bulk, nxt, out):
    low = which_half()
    count = now.shape[0]

    def body(x, held):
        held = put_face(held, now[x], x, low)
        held = put_face(held, buoy[x], 32 + x, low)
        return put_face(held, bulk[x] * nxt[x], 64 + x, low)

    out[...] = lax.fori_loop(0, count, body, jnp.zeros(now.shape[1:], F32), unroll=2)


def first_kernel(
    faces, now, prev, bulk, buoy, nxt, late, lap_out, mid_out, base_out, face_out
):
    low = which_half()
    count = now.shape[0]

    def body(x, carry):
        flux_v, flux_a, held = carry
        after, keep = following(x, count)
        side_sums = sums(buoy[x], keep * buoy[after], take_face(faces[...], 32 + x, low))
        here = now[x]
        lap, flux_v = twice_operate(
            here, keep * now[after], take_face(faces[...], x, low), flux_v, side_sums
        )
        lap = 0.5 * lap
        lap_out[x] = lap
        mid = 2.0 * here - prev[x] + (STEP * bulk[x]) * lap
        mid_out[x] = mid
        held = put_face(held, mid, x, low)
        scaled = bulk[x] * nxt[x]
        scaled_after = (keep * bulk[after]) * nxt[after]
        lap, flux_a = twice_operate(
            scaled, scaled_after, take_face(faces[...], 64 + x, low), flux_a, side_sums
        )
        base_out[x] = 2.0 * nxt[x] - late[x] + (0.5 * STEP) * lap
        return flux_v, flux_a, held

    start = (buoy[0] * now[0], buoy[0] * (bulk[0] * nxt[0]), jnp.zeros(now.shape[1:], F32))
    _, _, held = lax.fori_loop(0, count, body, start, unroll=4)
    face_out[...] = held


def second_kernel(faces, mid_face, mid, now, bulk, buoy, lap_out, end_out):
    low = which_half()
    count = now.shape[0]

    def body(x, flux):
        after, keep = following(x, count)
        side_sums = sums(buoy[x], keep * buoy[after], take_face(faces[...], 32 + x, low))
        here = mid[x]
        lap, flux = twice_operate(
            here, keep * mid[after], take_face(mid_face[...], x, low), flux, side_sums
        )
        lap = 0.5 * lap
        lap_out[x] = lap
        end_out[x] = 2.0 * here - now[x] + (STEP * bulk[x]) * lap
        return flux

    lax.fori_loop(0, count, body, buoy[0] * mid[0], unroll=4)


def pack_traces_kernel(groups_in, receivers_in, traces_in, out, groups, receivers, traces, sems):
    copies = [
        pltpu.make_async_copy(src, dst, sems.at[i])
        for i, (src, dst) in enumerate(
            ((groups_in, groups), (receivers_in, receivers), (traces_in, traces))
        )
    ]
    for copy in copies:
        copy.start()
    shots, cap, wide = out.shape
    slots = shots * cap
    count, samples = traces.shape
    copies[0].wait()
    keys = groups[...]
    place = keys.astype(F32) * CAP + rank_row(keys)
    chosen = (iota((slots, count), 0).astype(F32) == place).astype(F32).astype(BF16)
    copies[1].wait()
    ids = as_column(receivers[...].astype(F32))
    ids = jnp.where(iota((count, 128), 1) == 0, ids, 0.0).astype(BF16)
    named = jnp.dot(chosen, ids, preferred_element_type=F32).astype(BF16)
    out[:, :, samples:] = named.reshape(shots, cap, wide - samples)
    copies[2].wait()
    moved = jnp.dot(chosen, traces[...], preferred_element_type=F32).astype(BF16)
    out[:, :, :samples] = moved.reshape(shots, cap, samples)


def places_kernel(
    at, cells, mid, end, owners, slots, seen_out, hot_depth_out, place_out, cls_out, spot_out,
    ids_out, rows_mid, rows_end,
):
    lanes = 128
    count = cells.shape[1]

    def body(r, carry):
        row = lax.shift_right_logical(at[0, r], 7)
        rows_mid[pl.ds(r, 1), :] = mid[pl.ds(row, 1), :]
        rows_end[pl.ds(r, 1), :] = end[pl.ds(row, 1), :]
        return carry

    lax.fori_loop(0, count, body, 0, unroll=8)
    cell_col = as_column(cells[...])
    here = iota((count, lanes), 1) == (cell_col & (lanes - 1))
    hot_depth_out[...] = here.astype(F32)
    seen_mid = jnp.sum(jnp.where(here, rows_mid[...], 0.0), axis=1, keepdims=True)
    seen_end = jnp.sum(jnp.where(here, rows_end[...], 0.0), axis=1, keepdims=True)
    seen_out[...] = jnp.where(iota((count, lanes), 1) == 0, seen_mid, seen_end)

    owner = owners[...]
    tiles = owner.shape[1]
    rank = rank_row(owner).astype(I32)
    cls = owner & (CLASSES - 1)
    spot = lax.shift_right_logical(owner, 4) * CAPT + rank
    per_class = 8 * CAPT
    place_out[...] = cls * (per_class + 1) + spot
    cls_hot = (iota((CLASSES, tiles), 0) == cls).astype(F32).astype(BF16)
    cls_out[...] = cls_hot
    spot_hot = (iota((tiles, lanes), 1) == as_column(spot)).astype(F32)
    spot_out[...] = spot_hot
    slot_col = as_column(slots[...]).astype(F32)
    ids_out[...] = jnp.dot(
        cls_hot, (spot_hot * slot_col).astype(BF16), preferred_element_type=F32
    )


def inject_kernel(
    at, rows_in, filters, seen, hot_depth, base, bulk, mid_out, add_out, face_out, sum_mid, sum_end
):
    low = which_half()
    samples = filters.shape[1]
    count, lanes = hot_depth.shape
    slots = rows_in.shape[0] * rows_in.shape[1]
    last_dims = (((1,), (1,)), ((), ()))
    values = lax.dot_general(
        rows_in[:, :, :samples].reshape(slots, samples), filters[...], last_dims, preferred_element_type=F32
    )
    pick = ((iota((8, 128), 0) == 0) & (iota((8, 128), 1) == 0)).astype(F32).astype(BF16)
    ids = lax.dot_general(
        pick,
        rows_in[:, :, samples:].reshape(slots, rows_in.shape[2] - samples),
        last_dims,
        preferred_element_type=F32,
    )
    hot = (iota((count, slots), 0).astype(F32) == ids[0:1, :]).astype(F32).astype(BF16)
    observed = exact_dot(hot, values)
    sum_mid[...] = hot_depth[...] * (seen[:, 0:1] - observed[:, 0:1])
    sum_end[...] = hot_depth[...] * (seen[:, 1:2] - observed[:, 1:2])
    mid_out[...] = base[...]
    add_out[...] = jnp.zeros_like(add_out)

    def body(r, carry):
        row = lax.shift_right_logical(at[0, r], 7)
        mid_out[pl.ds(row, 1), :] = mid_out[pl.ds(row, 1), :] + sum_end[pl.ds(r, 1), :]
        add_out[pl.ds(row, 1), :] = add_out[pl.ds(row, 1), :] + sum_mid[pl.ds(r, 1), :]
        return carry

    lax.fori_loop(0, count, body, 0, unroll=8)
    rows = bulk.shape[1]

    def edge(x, held):
        field = mid_out[pl.ds(pl.multiple_of(x * rows, rows), rows), :]
        return put_face(held, bulk[x] * field, x, low)

    face_out[...] = lax.fori_loop(
        0, bulk.shape[0], edge, jnp.zeros(bulk.shape[1:], F32), unroll=2
    )


def image_kernel(
    faces, adj_face, mid, add, nxt, bulk, buoy, lap_mid, lap_now, place, cls_hot, spot_hot, ids,
    last_out, send_out, codes,
):
    low = which_half()
    count, rows, lanes = mid.shape
    tiles = rows // 8
    per_class = send_out.shape[0] // CLASSES

    def clear(c, carry):
        send_out[pl.ds(c * per_class, per_class)] = jnp.zeros((per_class, 8, lanes), jnp.int16)
        return carry

    lax.fori_loop(0, CLASSES, clear, 0)

    def body(x, flux):
        after, keep = following(x, count)
        side_sums = sums(buoy[x], keep * buoy[after], take_face(faces[...], 32 + x, low))
        here = mid[x]
        lap, flux = twice_operate(
            bulk[x] * here,
            (keep * bulk[after]) * mid[after],
            take_face(adj_face[...], x, low),
            flux,
            side_sums,
        )
        end = 2.0 * here - nxt[x] + (0.5 * STEP) * lap + add[x]
        last_out[x] = end
        image = (STEP * (here * lap_mid[x] + end * lap_now[x])).reshape(tiles, 8, lanes)
        peak = jnp.max(jnp.max(jnp.abs(image), axis=1), axis=1, keepdims=True)
        code = jnp.ceil(16.0 * jnp.log2(jnp.maximum(peak, 1e-30))) + 1.0
        codes[pl.ds(pl.multiple_of(x * tiles, tiles), tiles), :] = jnp.broadcast_to(
            code + CODE_ZERO, (tiles, lanes)
        )
        gain = jnp.broadcast_to(32767.0 * jnp.exp2(code * (-1.0 / 16.0)), (tiles, lanes))
        whole = jnp.round(image * gain[:, None, :]).astype(I32).astype(jnp.int16)
        for t in range(tiles):
            send_out[place[0, x * tiles + t]] = whole[t]
        return flux

    lax.fori_loop(0, count, body, buoy[0] * (bulk[0] * mid[0]), unroll=4)
    code = codes[...]
    upper = jnp.floor(code * (1.0 / 64.0))
    lower = code - 64.0 * upper
    hot = cls_hot[...]
    spread = spot_hot[...]
    sent = 64.0 * jnp.dot(hot, (spread * upper).astype(BF16), preferred_element_type=F32)
    sent = sent + jnp.dot(hot, (spread * lower).astype(BF16), preferred_element_type=F32)
    place_row = iota((8, lanes), 0)
    for c in range(CLASSES):
        tile = jnp.where(
            place_row == 0,
            ids[c : c + 1, :],
            jnp.where(place_row == 1, sent[c : c + 1, :], 0.0),
        )
        send_out[c * per_class + per_class - 1] = tile.astype(I32).astype(jnp.int16)


def combine_kernel(got, out, gains_v, slots_v, gains, slots, sems, *partial):
    per_class = got.shape[0] // CLASSES
    used = per_class - 1
    lanes = got.shape[2]
    for c in range(CLASSES):
        meta = got[c * per_class + used].astype(I32)
        slots_v[c : c + 1, :] = meta[0:1, :]
        code = meta[1:2, :].astype(F32)
        gain = jnp.exp2((code - CODE_ZERO) * (1.0 / 16.0)) * (1.0 / 32767.0)
        gains_v[c : c + 1, :] = jnp.where(code > 0, gain, 0.0)
    copies = [
        pltpu.make_async_copy(gains_v, gains, sems.at[0]),
        pltpu.make_async_copy(slots_v, slots, sems.at[1]),
    ]
    for copy in copies:
        copy.start()
    for part in partial:
        part[...] = jnp.zeros_like(part)
    for copy in copies:
        copy.wait()

    def body(src, carry):
        for s in range(used):
            part = partial[s % CAPT]
            at = (s // CAPT) * MT_DEV + slots[src, s]
            value = got[src * per_class + s].astype(I32).astype(F32) * gains[src, s]
            part[at] = part[at] + value
        return carry

    lax.fori_loop(0, CLASSES, body, 0)
    total = partial[0][...]
    for part in partial[1:]:
        total = total + part[...]
    out[...] = total


def swap(face):
    return lax.ppermute(face, "ap", [(0, 1), (1, 0)])


def local(
    wave_prev,
    wave_now,
    adjoint_late,
    adjoint_next,
    bulk,
    buoyancy,
    traces,
    group_filter,
    trace_group,
    trace_receiver,
    receiver_cell,
    tile_owner,
    tile_slot,
):
    shots = lax.axis_size("shot")
    rings = shots // CLASSES
    prev, now, late, nxt = wave_prev[0], wave_now[0], adjoint_late[0], adjoint_next[0]
    bulk, buoy = bulk[0], buoyancy[0]
    count, rows, lanes = now.shape
    field = sds(now.shape)
    flat = sds((count * rows, lanes))
    samples = traces.shape[1]
    face = sds((rows, lanes))

    own_rows = traces.shape[0]
    packed = call(
        pack_traces_kernel,
        "pack_traces",
        sds((shots, CAP, samples + 128), BF16),
        [
            pltpu.VMEM((1, own_rows), I32),
            pltpu.VMEM((1, own_rows), I32),
            pltpu.VMEM((own_rows, samples), BF16),
            pltpu.SemaphoreType.DMA((3,)),
        ],
        hbm=(0, 1, 2),
        hbm_out=(0,),
    )(
        trace_group.reshape(1, -1), trace_receiver.reshape(1, -1), traces
    )
    got_rows = lax.all_to_all(
        packed, "shot", split_axis=0, concat_axis=0, tiled=True
    )

    faces = swap(call(faces_kernel, "faces", face)(now, buoy, bulk, nxt))
    lap_now, wave_mid, adj_base, mid_face = call(
        first_kernel, "first_step", (field, field, field, face), hbm_out=(0, 2)
    )(faces, now, prev, bulk, buoy, nxt, late)
    lap_mid, wave_end = call(second_kernel, "second_step", (field, field), hbm_out=(0,))(
        faces, swap(mid_face), wave_mid, now, bulk, buoy
    )
    receivers = receiver_cell.shape[1]
    tiles = tile_owner.shape[0]
    per_receiver = pltpu.VMEM((receivers, lanes), F32)
    seen, hot_depth, place, cls_hot, spot_hot, ids = call(
        places_kernel,
        "places",
        (
            sds((receivers, lanes)),
            sds((receivers, lanes)),
            sds((1, tiles), I32),
            sds((CLASSES, tiles), BF16),
            sds((tiles, lanes)),
            sds((CLASSES, lanes)),
        ),
        [per_receiver, per_receiver],
        smem=(0,),
        hbm_out=(1, 2, 3, 4, 5),
    )(
        receiver_cell,
        receiver_cell,
        wave_mid.reshape(flat.shape),
        wave_end.reshape(flat.shape),
        tile_owner.reshape(1, -1),
        tile_slot.reshape(1, -1),
    )
    filters = jnp.pad(group_filter[0], ((0, 14), (0, 0)))
    adj_mid, adj_add, adj_face = call(
        inject_kernel, "inject", (flat, flat, face), [per_receiver, per_receiver], smem=(0,), free=(1,)
    )(receiver_cell, got_rows, filters, seen, hot_depth, adj_base.reshape(flat.shape), bulk)
    per_class = (shots // CLASSES) * CAPT + 1
    adj_end, send = call(
        image_kernel,
        "image",
        (field, sds((CLASSES * per_class, 8, lanes), jnp.int16)),
        [pltpu.VMEM((tiles, lanes), F32)],
        smem=(9,),
    )(
        faces, swap(adj_face), adj_mid.reshape(now.shape), adj_add.reshape(now.shape), nxt, bulk,
        buoy, lap_mid, lap_now, place, cls_hot, spot_hot, ids,
    )
    near = [[r * CLASSES + c for c in range(CLASSES)] for r in range(rings)]
    far = [[r * CLASSES + c for r in range(rings)] for c in range(CLASSES)]
    got = lax.all_to_all(
        send.reshape(CLASSES, per_class * 8, lanes),
        "shot",
        split_axis=0,
        concat_axis=0,
        axis_index_groups=near,
        tiled=True,
    )
    owned = rings * MT_DEV
    table = (CLASSES, lanes)
    dense = call(
        combine_kernel,
        "combine",
        sds((owned, 8, lanes)),
        [
            pltpu.VMEM(table, F32),
            pltpu.VMEM(table, I32),
            pltpu.SMEM(table, F32),
            pltpu.SMEM(table, I32),
            pltpu.SemaphoreType.DMA((2,)),
        ]
        + [pltpu.VMEM((owned, 8, lanes), F32)] * CAPT,
    )(got.reshape(CLASSES * per_class, 8, lanes))
    shared = lax.all_to_all(
        dense.reshape(rings, MT_DEV * 8, lanes),
        "shot",
        split_axis=0,
        concat_axis=0,
        axis_index_groups=far,
        tiled=True,
    )
    model_grad = jnp.sum(shared, axis=0).reshape(MT_DEV, 8, lanes)
    return (model_grad, wave_end[None], adj_end[None])


def solution(mesh):
    placed = (
        P("shot", None, None, "ap"),
        P("shot", None, None, "ap"),
        P("shot", None, None, "ap"),
        P("shot", None, None, "ap"),
        P("shot", None, None, "ap"),
        P("shot", None, None, "ap"),
        P(("shot", "ap"), None),
        P("shot", None, None),
        P(("shot", "ap"), None),
        P(("shot", "ap")),
        P("shot", "ap"),
        P("shot", None),
        P("shot"),
    )
    return jax.shard_map(
        local,
        mesh=mesh,
        in_specs=placed,
        out_specs=(P("shot", None, "ap"), P("shot", None, None, "ap"), P("shot", None, None, "ap")),
        check_vma=False,
    )
```

```python
import functools

import jax
import jax.numpy as jnp
from jax import lax
from jax.experimental import pallas as pl
from jax.experimental.pallas import tpu as pltpu
from jax.sharding import PartitionSpec as P

STEP = 0.08
MT_DEV = 8
CAP = 2
CAPT = 4
CLASSES = 16
CODE_ZERO = 4096.0
VMEM_LIMIT = 6 * 1024 * 1024

F32 = jnp.float32
BF16 = jnp.bfloat16
I32 = jnp.int32


def staged_kernel(kernel, stage, late, count_in, count_out, *refs):
    inputs, rest = list(refs[:count_in]), refs[count_in : len(refs) - len(stage) - 1]
    sems, buffers = refs[len(refs) - len(stage) - 1], refs[len(refs) - len(stage) :]
    copies = []
    for n, (i, buffer) in enumerate(zip(stage, buffers)):
        copies.append(pltpu.make_async_copy(inputs[i], buffer, sems.at[n]))
        copies[-1].start()
        inputs[i] = buffer

    def arrived():
        for copy in copies:
            copy.wait()

    if late:
        kernel(arrived, *inputs, *rest)
    else:
        arrived()
        kernel(*inputs, *rest)


def call(
    kernel, name, out_shape, scratch=(), smem=(), hbm_out=(), hbm=(), raw_out=(), stage=(),
    late=False,
):
    def run(*args):
        spaces = [
            pltpu.SMEM if i in smem else pltpu.HBM if i in hbm or i in stage else pltpu.VMEM
            for i in range(len(args))
        ]
        args = [
            x if space is pltpu.SMEM else pltpu.with_memory_space_constraint(x, space)
            for x, space in zip(args, spaces)
        ]
        specs = [pl.BlockSpec(memory_space=space) for space in spaces]
        flat, tree = jax.tree.flatten(out_shape)
        outs = [
            pl.BlockSpec(memory_space=pltpu.HBM if i in raw_out else pltpu.VMEM)
            for i in range(len(flat))
        ]
        shapes = [
            (pltpu.HBM if i in hbm_out or i in raw_out else pltpu.VMEM)(s.shape, s.dtype)
            for i, s in enumerate(flat)
        ]
        body, extra = kernel, []
        if stage:
            body = functools.partial(
                staged_kernel, kernel, stage, late, len(args), len(flat)
            )
            extra = [pltpu.SemaphoreType.DMA((len(stage),))]
            extra += [pltpu.VMEM(args[i].shape, args[i].dtype) for i in stage]
        return pl.pallas_call(
            body,
            out_shape=jax.tree.unflatten(tree, shapes),
            in_specs=specs,
            out_specs=jax.tree.unflatten(tree, outs),
            scratch_shapes=list(scratch) + extra,
            name=name,
            compiler_params=pltpu.CompilerParams(vmem_limit_bytes=VMEM_LIMIT),
        )(*args)

    return run


def sds(shape, dtype=F32):
    return jax.ShapeDtypeStruct(shape, dtype)


def iota(shape, dim):
    return lax.broadcasted_iota(I32, shape, dim)


def pieces(value):
    first = value.astype(BF16)
    rest = value - first.astype(F32)
    second = rest.astype(BF16)
    third = (rest - second.astype(F32)).astype(BF16)
    return first, second, third


def exact_dot(onehot, value):
    first, second, third = pieces(value)
    out = jnp.dot(onehot, third, preferred_element_type=F32)
    out = out + jnp.dot(onehot, second, preferred_element_type=F32)
    return out + jnp.dot(onehot, first, preferred_element_type=F32)


def as_column(row):
    size = row.shape[1]
    eye = iota((size, size), 0) == iota((size, size), 1)
    return jnp.sum(jnp.where(eye, row, 0), axis=1, keepdims=True)


def rank_row(keys):
    size = keys.shape[1]
    first, second = iota((size, size), 0), iota((size, size), 1)
    same = (as_column(keys) == keys) & (first < second)
    return jnp.sum(same.astype(F32), axis=0, keepdims=True)


def which_half():
    low = lax.axis_index("ap") == 0
    return low


def edge_lane(low, lanes):
    return jnp.where(low, lanes - 1, 0)


def put_face(held, plane, at, low):
    lanes = plane.shape[1]
    shift = lax.rem(at - edge_lane(low, lanes) + lanes, lanes)
    return jnp.where(iota(plane.shape, 1) == at, pltpu.roll(plane, shift, 1), held)


def take_face(held, at, low):
    lanes = held.shape[1]
    edge = edge_lane(low, lanes)
    shift = lax.rem(edge - at + lanes, lanes)
    return jnp.where(iota(held.shape, 1) == edge, pltpu.roll(held, shift, 1), 0.0)


def next_second(plane):
    rows = plane.shape[0]
    rolled = pltpu.roll(plane, rows - 1, 0)
    return jnp.where(iota(plane.shape, 0) == rows - 1, 0.0, rolled)


def next_depth(plane, halo):
    lanes = plane.shape[1]
    rolled = pltpu.roll(plane, lanes - 1, 1)
    return jnp.where(iota(plane.shape, 1) == lanes - 1, halo, rolled)


def sums(here, after, halo):
    return here, here + after, here + next_second(here), here + next_depth(here, halo), here + halo


def twice_operate(here, after, halo, before_flux, side_sums):
    buoy, along_x, along_y, along_z, low_z = side_sums
    flux = along_x * (after - here)
    total = flux - before_flux
    flux_y = along_y * (next_second(here) - here)
    under = jnp.where(iota(here.shape, 0) == 0, buoy * here, pltpu.roll(flux_y, 1, 0))
    total = total + (flux_y - under)
    flux_z = along_z * (next_depth(here, halo) - here)
    below = jnp.where(iota(here.shape, 1) == 0, low_z * (here - halo), pltpu.roll(flux_z, 1, 1))
    return total + (flux_z - below), flux


def following(x, count):
    return jnp.minimum(x + 1, count - 1), (x < count - 1).astype(F32)


def faces_kernel(now, buoy, bulk, nxt, out):
    low = which_half()
    count = now.shape[0]

    def body(x, held):
        held = put_face(held, now[x], x, low)
        held = put_face(held, buoy[x], 32 + x, low)
        return put_face(held, bulk[x] * nxt[x], 64 + x, low)

    out[...] = lax.fori_loop(0, count, body, jnp.zeros(now.shape[1:], F32), unroll=2)


def first_kernel(
    faces, now, prev, bulk, buoy, nxt, late, lap_out, mid_out, base_out, face_out
):
    low = which_half()
    count = now.shape[0]

    def body(x, carry):
        flux_v, flux_a, held = carry
        after, keep = following(x, count)
        side_sums = sums(buoy[x], keep * buoy[after], take_face(faces[...], 32 + x, low))
        here = now[x]
        lap, flux_v = twice_operate(
            here, keep * now[after], take_face(faces[...], x, low), flux_v, side_sums
        )
        lap = 0.5 * lap
        lap_out[x] = lap
        mid = 2.0 * here - prev[x] + (STEP * bulk[x]) * lap
        mid_out[x] = mid
        held = put_face(held, mid, x, low)
        scaled = bulk[x] * nxt[x]
        scaled_after = (keep * bulk[after]) * nxt[after]
        lap, flux_a = twice_operate(
            scaled, scaled_after, take_face(faces[...], 64 + x, low), flux_a, side_sums
        )
        base = 2.0 * nxt[x] - late[x] + (0.5 * STEP) * lap
        base_out[x] = base
        return flux_v, flux_a, put_face(held, bulk[x] * base, 32 + x, low)

    start = (buoy[0] * now[0], buoy[0] * (bulk[0] * nxt[0]), jnp.zeros(now.shape[1:], F32))
    _, _, held = lax.fori_loop(0, count, body, start, unroll=4)
    face_out[...] = held


def second_kernel(faces, mid_face, mid, now, bulk, buoy, lap_out, end_out):
    low = which_half()
    count = now.shape[0]

    def body(x, flux):
        after, keep = following(x, count)
        side_sums = sums(buoy[x], keep * buoy[after], take_face(faces[...], 32 + x, low))
        here = mid[x]
        lap, flux = twice_operate(
            here, keep * mid[after], take_face(mid_face[...], x, low), flux, side_sums
        )
        lap = 0.5 * lap
        lap_out[x] = lap
        end_out[x] = 2.0 * here - now[x] + (STEP * bulk[x]) * lap
        return flux

    lax.fori_loop(0, count, body, buoy[0] * mid[0], unroll=4)


PACK_CHUNK = 512


def pack_traces_kernel(groups_in, receivers_in, traces_in, out, groups, receivers, traces, made, sems):
    shots, cap, wide = out.shape
    slots = shots * cap
    count, samples = traces.shape
    starts = range(0, samples, PACK_CHUNK)
    small = [
        pltpu.make_async_copy(groups_in, groups, sems.at[0]),
        pltpu.make_async_copy(receivers_in, receivers, sems.at[1]),
    ]
    loads = []
    for i, start in enumerate(starts):
        part = pl.ds(start, PACK_CHUNK)
        loads.append(
            pltpu.make_async_copy(traces_in.at[:, part], traces.at[:, part], sems.at[2 + i])
        )
    for copy in small + loads:
        copy.start()
    small[0].wait()
    keys = groups[...]
    place = keys.astype(F32) * CAP + rank_row(keys)
    chosen = (iota((slots, count), 0).astype(F32) == place).astype(F32).astype(BF16)
    small[1].wait()
    ids = as_column(receivers[...].astype(F32))
    ids = jnp.where(iota((count, 128), 1) == 0, ids, 0.0).astype(BF16)
    named = jnp.dot(chosen, ids, preferred_element_type=F32).astype(BF16)
    made[:, :, samples:] = named.reshape(shots, cap, wide - samples)
    stores = []

    def send(start, width):
        part = pl.ds(start, width)
        copy = pltpu.make_async_copy(
            made.at[:, :, part], out.at[:, :, part], sems.at[2 + len(loads) + len(stores)]
        )
        copy.start()
        stores.append(copy)

    send(samples, wide - samples)
    for load, start in zip(loads, starts):
        load.wait()
        moved = jnp.dot(
            chosen, traces[:, start : start + PACK_CHUNK], preferred_element_type=F32
        ).astype(BF16)
        made[:, :, start : start + PACK_CHUNK] = moved.reshape(shots, cap, PACK_CHUNK)
        send(start, PACK_CHUNK)
    for copy in stores:
        copy.wait()


def places_kernel(
    at, cells, mid, end, bulk, owners, slots, about_out, hot_second_out, place_out, cls_out,
    spot_out, ids_out, rows_mid, rows_end, rows_bulk,
):
    low = which_half()
    lanes = 128
    count = cells.shape[1]

    def body(r, carry):
        row = lax.shift_right_logical(at[0, r], 7)
        rows_mid[pl.ds(r, 1), :] = mid[pl.ds(row, 1), :]
        rows_end[pl.ds(r, 1), :] = end[pl.ds(row, 1), :]
        rows_bulk[pl.ds(r, 1), :] = bulk[pl.ds(row, 1), :]
        return carry

    lax.fori_loop(0, count, body, 0, unroll=8)
    cell_row = cells[...]
    cell_col = as_column(cell_row)
    lane = iota((count, lanes), 1)
    depth_col = cell_col & (lanes - 1)
    here = lane == depth_col
    seen_mid = jnp.sum(jnp.where(here, rows_mid[...], 0.0), axis=1, keepdims=True)
    seen_end = jnp.sum(jnp.where(here, rows_end[...], 0.0), axis=1, keepdims=True)
    at_edge = here & (lane == edge_lane(low, lanes))
    edge_bulk = jnp.sum(jnp.where(at_edge, rows_bulk[...], 0.0), axis=1, keepdims=True)
    about_out[:, :lanes] = jnp.where(lane == 0, seen_mid, seen_end)
    about_out[:, lanes : 2 * lanes] = here.astype(F32)
    first_col = lax.shift_right_logical(cell_col, 13)
    about_out[:, 2 * lanes :] = jnp.where(lane == first_col + 32, edge_bulk, 0.0)
    rows = hot_second_out.shape[0]
    second_row = lax.shift_right_logical(cell_row, 7) & (rows - 1)
    hot_second_out[...] = (iota((rows, count), 0) == second_row).astype(F32).astype(BF16)

    owner = owners[...]
    tiles = owner.shape[1]
    rank = rank_row(owner).astype(I32)
    cls = owner & (CLASSES - 1)
    spot = lax.shift_right_logical(owner, 4) * CAPT + rank
    per_class = 8 * CAPT
    place_out[...] = cls * (per_class + 1) + spot
    cls_hot = (iota((CLASSES, tiles), 0) == cls).astype(F32).astype(BF16)
    cls_out[...] = cls_hot
    spot_hot = (iota((tiles, lanes), 1) == as_column(spot)).astype(F32)
    spot_out[...] = spot_hot
    slot_col = as_column(slots[...]).astype(F32)
    ids_out[...] = jnp.dot(
        cls_hot, (spot_hot * slot_col).astype(BF16), preferred_element_type=F32
    )


def residual_kernel(rows_in, filters, about, hot_second, sum_mid, sum_end, face_out):
    samples = filters.shape[1]
    count, lanes = sum_mid.shape
    slots = rows_in.shape[0] * rows_in.shape[1]
    last_dims = (((1,), (1,)), ((), ()))
    values = lax.dot_general(
        rows_in[:, :, :samples].reshape(slots, samples),
        filters[...],
        last_dims,
        preferred_element_type=F32,
    )
    pick = ((iota((8, 128), 0) == 0) & (iota((8, 128), 1) == 0)).astype(F32).astype(BF16)
    ids = lax.dot_general(
        pick,
        rows_in[:, :, samples:].reshape(slots, rows_in.shape[2] - samples),
        last_dims,
        preferred_element_type=F32,
    )
    hot = (iota((count, slots), 0).astype(F32) == ids[0:1, :]).astype(F32).astype(BF16)
    observed = exact_dot(hot, values)
    resid_mid = about[:, 0:1] - observed[:, 0:1]
    resid_end = about[:, 1:2] - observed[:, 1:2]
    hot_depth = about[:, lanes : 2 * lanes]
    sum_mid[...] = hot_depth * resid_mid
    sum_end[...] = hot_depth * resid_end
    face_out[...] = exact_dot(hot_second[...], about[:, 2 * lanes :] * resid_end)


def inject_kernel(at, sum_mid, sum_end, base, mid_out, add_out):
    mid_out[...] = base[...]
    add_out[...] = jnp.zeros_like(add_out)

    def body(r, carry):
        row = lax.shift_right_logical(at[0, r], 7)
        mid_out[pl.ds(row, 1), :] = mid_out[pl.ds(row, 1), :] + sum_end[pl.ds(r, 1), :]
        add_out[pl.ds(row, 1), :] = add_out[pl.ds(row, 1), :] + sum_mid[pl.ds(r, 1), :]
        return carry

    lax.fori_loop(0, sum_mid.shape[0], body, 0, unroll=8)


def image_kernel(
    arrived, faces, mid_face, adj_face, mid, add, nxt, bulk, buoy, lap_mid, lap_now, place, cls_hot, spot_hot, ids,
    last_out, send_out, codes, scaled_face,
):
    low = which_half()
    count, rows, lanes = mid.shape
    tiles = rows // 8
    per_class = send_out.shape[0] // CLASSES
    scaled_face[...] = mid_face[...] + adj_face[...]

    def clear(c, carry):
        send_out[pl.ds(c * per_class, per_class)] = jnp.zeros((per_class, 8, lanes), jnp.int16)
        return carry

    lax.fori_loop(0, CLASSES, clear, 0)

    def body(x, flux):
        after, keep = following(x, count)
        side_sums = sums(buoy[x], keep * buoy[after], take_face(faces[...], 32 + x, low))
        here = mid[x]
        lap, flux = twice_operate(
            bulk[x] * here,
            (keep * bulk[after]) * mid[after],
            take_face(scaled_face[...], 32 + x, low),
            flux,
            side_sums,
        )
        last_out[x] = 2.0 * here - nxt[x] + (0.5 * STEP) * lap + add[x]
        return flux

    lax.fori_loop(0, count, body, buoy[0] * (bulk[0] * mid[0]), unroll=4)
    arrived()

    def pack(x, carry):
        image = mid[x] * lap_mid[x] + last_out[x] * lap_now[x]
        image = (STEP * image).reshape(tiles, 8, lanes)
        peak = jnp.max(jnp.max(jnp.abs(image), axis=1), axis=1, keepdims=True)
        code = jnp.ceil(16.0 * jnp.log2(jnp.maximum(peak, 1e-30))) + 1.0
        codes[pl.ds(pl.multiple_of(x * tiles, tiles), tiles), :] = jnp.broadcast_to(
            code + CODE_ZERO, (tiles, lanes)
        )
        gain = jnp.broadcast_to(32767.0 * jnp.exp2(code * (-1.0 / 16.0)), (tiles, lanes))
        whole = jnp.round(image * gain[:, None, :]).astype(I32).astype(jnp.int16)
        for t in range(tiles):
            send_out[place[0, x * tiles + t]] = whole[t]
        return carry

    lax.fori_loop(0, count, pack, 0, unroll=4)
    code = codes[...]
    upper = jnp.floor(code * (1.0 / 64.0))
    lower = code - 64.0 * upper
    hot = cls_hot[...]
    spread = spot_hot[...]
    sent = 64.0 * jnp.dot(hot, (spread * upper).astype(BF16), preferred_element_type=F32)
    sent = sent + jnp.dot(hot, (spread * lower).astype(BF16), preferred_element_type=F32)
    place_row = iota((8, lanes), 0)
    for c in range(CLASSES):
        tile = jnp.where(
            place_row == 0,
            ids[c : c + 1, :],
            jnp.where(place_row == 1, sent[c : c + 1, :], 0.0),
        )
        send_out[c * per_class + per_class - 1] = tile.astype(I32).astype(jnp.int16)


def combine_kernel(got, out, gains_v, slots_v, gains, slots, sems, *partial):
    per_class = got.shape[0] // CLASSES
    used = per_class - 1
    lanes = got.shape[2]
    for c in range(CLASSES):
        meta = got[c * per_class + used].astype(I32)
        slots_v[c : c + 1, :] = meta[0:1, :]
        code = meta[1:2, :].astype(F32)
        gain = jnp.exp2((code - CODE_ZERO) * (1.0 / 16.0)) * (1.0 / 32767.0)
        gains_v[c : c + 1, :] = jnp.where(code > 0, gain, 0.0)
    copies = [
        pltpu.make_async_copy(gains_v, gains, sems.at[0]),
        pltpu.make_async_copy(slots_v, slots, sems.at[1]),
    ]
    for copy in copies:
        copy.start()
    for part in partial:
        part[...] = jnp.zeros_like(part)
    for copy in copies:
        copy.wait()

    def body(src, carry):
        for s in range(used):
            part = partial[s % CAPT]
            at = (s // CAPT) * MT_DEV + slots[src, s]
            value = got[src * per_class + s].astype(I32).astype(F32) * gains[src, s]
            part[at] = part[at] + value
        return carry

    lax.fori_loop(0, CLASSES, body, 0)
    total = partial[0][...]
    for part in partial[1:]:
        total = total + part[...]
    out[...] = total


def swap(face):
    return lax.ppermute(face, "ap", [(0, 1), (1, 0)])


def local(
    wave_prev,
    wave_now,
    adjoint_late,
    adjoint_next,
    bulk,
    buoyancy,
    traces,
    group_filter,
    trace_group,
    trace_receiver,
    receiver_cell,
    tile_owner,
    tile_slot,
):
    shots = lax.axis_size("shot")
    rings = shots // CLASSES
    prev, now, late, nxt = wave_prev[0], wave_now[0], adjoint_late[0], adjoint_next[0]
    bulk, buoy = bulk[0], buoyancy[0]
    count, rows, lanes = now.shape
    field = sds(now.shape)
    flat = sds((count * rows, lanes))
    samples = traces.shape[1]
    face = sds((rows, lanes))

    own_rows = traces.shape[0]
    packed = call(
        pack_traces_kernel,
        "pack_traces",
        sds((shots, CAP, samples + 128), BF16),
        [
            pltpu.VMEM((1, own_rows), I32),
            pltpu.VMEM((1, own_rows), I32),
            pltpu.VMEM((own_rows, samples), BF16),
            pltpu.VMEM((shots, CAP, samples + 128), BF16),
            pltpu.SemaphoreType.DMA((3 + 2 * (samples // PACK_CHUNK),)),
        ],
        hbm=(0, 1, 2),
        raw_out=(0,),
    )(
        trace_group.reshape(1, -1), trace_receiver.reshape(1, -1), traces
    )
    got_rows = lax.all_to_all(
        packed, "shot", split_axis=0, concat_axis=0, tiled=True
    )

    faces = swap(call(faces_kernel, "faces", face)(now, buoy, bulk, nxt))
    lap_now, wave_mid, adj_base, mid_face = call(
        first_kernel, "first_step", (field, field, field, face), hbm_out=(0, 2)
    )(faces, now, prev, bulk, buoy, nxt, late)
    mid_face = swap(mid_face)
    lap_mid, wave_end = call(second_kernel, "second_step", (field, field), hbm_out=(0,))(
        faces, mid_face, wave_mid, now, bulk, buoy
    )
    receivers = receiver_cell.shape[1]
    tiles = tile_owner.shape[0]
    per_receiver = pltpu.VMEM((receivers, lanes), F32)
    about, hot_second, place, cls_hot, spot_hot, ids = call(
        places_kernel,
        "places",
        (
            sds((receivers, 3 * lanes)),
            sds((rows, receivers), BF16),
            sds((1, tiles), I32),
            sds((CLASSES, tiles), BF16),
            sds((tiles, lanes)),
            sds((CLASSES, lanes)),
        ),
        [per_receiver] * 3,
        smem=(0,),
        hbm_out=(1, 2, 3, 4, 5),
    )(
        receiver_cell,
        receiver_cell,
        wave_mid.reshape(flat.shape),
        wave_end.reshape(flat.shape),
        bulk.reshape(flat.shape),
        tile_owner.reshape(1, -1),
        tile_slot.reshape(1, -1),
    )
    spread = sds((receivers, lanes))
    sum_mid, sum_end, adj_face = call(
        residual_kernel, "residual", (spread, spread, face), stage=(0, 1, 3)
    )(got_rows, group_filter[0], about, hot_second)
    adj_face = swap(adj_face)
    adj_mid, adj_add = call(inject_kernel, "inject", (flat, flat), smem=(0,))(
        receiver_cell, sum_mid, sum_end, adj_base.reshape(flat.shape)
    )
    per_class = (shots // CLASSES) * CAPT + 1
    adj_end, send = call(
        image_kernel,
        "image",
        (field, sds((CLASSES * per_class, 8, lanes), jnp.int16)),
        [pltpu.VMEM((tiles, lanes), F32), pltpu.VMEM((rows, lanes), F32)],
        smem=(10,),
        stage=(8, 9),
        late=True,
    )(
        faces, mid_face, adj_face, adj_mid.reshape(now.shape), adj_add.reshape(now.shape), nxt,
        bulk, buoy, lap_mid, lap_now, place, cls_hot, spot_hot, ids,
    )
    near = [[r * CLASSES + c for c in range(CLASSES)] for r in range(rings)]
    far = [[r * CLASSES + c for r in range(rings)] for c in range(CLASSES)]
    got = lax.all_to_all(
        send.reshape(CLASSES, per_class * 8, lanes),
        "shot",
        split_axis=0,
        concat_axis=0,
        axis_index_groups=near,
        tiled=True,
    )
    owned = rings * MT_DEV
    table = (CLASSES, lanes)
    dense = call(
        combine_kernel,
        "combine",
        sds((owned, 8, lanes)),
        [
            pltpu.VMEM(table, F32),
            pltpu.VMEM(table, I32),
            pltpu.SMEM(table, F32),
            pltpu.SMEM(table, I32),
            pltpu.SemaphoreType.DMA((2,)),
        ]
        + [pltpu.VMEM((owned, 8, lanes), F32)] * CAPT,
    )(got.reshape(CLASSES * per_class, 8, lanes))
    shared = lax.all_to_all(
        dense.reshape(rings, MT_DEV * 8, lanes),
        "shot",
        split_axis=0,
        concat_axis=0,
        axis_index_groups=far,
        tiled=True,
    )
    model_grad = jnp.sum(shared, axis=0).reshape(MT_DEV, 8, lanes)
    return (model_grad, wave_end[None], adj_end[None])


def solution(mesh):
    placed = (
        P("shot", None, None, "ap"),
        P("shot", None, None, "ap"),
        P("shot", None, None, "ap"),
        P("shot", None, None, "ap"),
        P("shot", None, None, "ap"),
        P("shot", None, None, "ap"),
        P(("shot", "ap"), None),
        P("shot", None, None),
        P(("shot", "ap"), None),
        P(("shot", "ap")),
        P("shot", "ap"),
        P("shot", None),
        P("shot"),
    )
    return jax.shard_map(
        local,
        mesh=mesh,
        in_specs=placed,
        out_specs=(P("shot", None, "ap"), P("shot", None, None, "ap"), P("shot", None, None, "ap")),
        check_vma=False,
    )
```

```python
import functools

import jax
import jax.numpy as jnp
from jax import lax
from jax.experimental import pallas as pl
from jax.experimental.pallas import tpu as pltpu
from jax.sharding import PartitionSpec as P

STEP = 0.08
MT_DEV = 8
CAP = 2
CAPT = 4
CLASSES = 32
CLASS_SHIFT = 5
RINGS = 4
CODE_ZERO = 4096.0
VMEM_LIMIT = 6 * 1024 * 1024

F32 = jnp.float32
BF16 = jnp.bfloat16
I32 = jnp.int32


def staged_kernel(kernel, stage, late, count_in, count_out, *refs):
    inputs, rest = list(refs[:count_in]), refs[count_in : len(refs) - len(stage) - 1]
    sems, buffers = refs[len(refs) - len(stage) - 1], refs[len(refs) - len(stage) :]
    copies = []
    for n, (i, buffer) in enumerate(zip(stage, buffers)):
        copies.append(pltpu.make_async_copy(inputs[i], buffer, sems.at[n]))
        copies[-1].start()
        inputs[i] = buffer

    def arrived():
        for copy in copies:
            copy.wait()

    if late:
        kernel(arrived, *inputs, *rest)
    else:
        arrived()
        kernel(*inputs, *rest)


def call(
    kernel, name, out_shape, scratch=(), smem=(), hbm_out=(), hbm=(), raw_out=(), stage=(),
    late=False,
):
    def run(*args):
        spaces = [
            pltpu.SMEM if i in smem else pltpu.HBM if i in hbm or i in stage else pltpu.VMEM
            for i in range(len(args))
        ]
        args = [
            x if space is pltpu.SMEM else pltpu.with_memory_space_constraint(x, space)
            for x, space in zip(args, spaces)
        ]
        specs = [pl.BlockSpec(memory_space=space) for space in spaces]
        flat, tree = jax.tree.flatten(out_shape)
        outs = [
            pl.BlockSpec(memory_space=pltpu.HBM if i in raw_out else pltpu.VMEM)
            for i in range(len(flat))
        ]
        shapes = [
            (pltpu.HBM if i in hbm_out or i in raw_out else pltpu.VMEM)(s.shape, s.dtype)
            for i, s in enumerate(flat)
        ]
        body, extra = kernel, []
        if stage:
            body = functools.partial(
                staged_kernel, kernel, stage, late, len(args), len(flat)
            )
            extra = [pltpu.SemaphoreType.DMA((len(stage),))]
            extra += [pltpu.VMEM(args[i].shape, args[i].dtype) for i in stage]
        return pl.pallas_call(
            body,
            out_shape=jax.tree.unflatten(tree, shapes),
            in_specs=specs,
            out_specs=jax.tree.unflatten(tree, outs),
            scratch_shapes=list(scratch) + extra,
            name=name,
            compiler_params=pltpu.CompilerParams(vmem_limit_bytes=VMEM_LIMIT),
        )(*args)

    return run


def sds(shape, dtype=F32):
    return jax.ShapeDtypeStruct(shape, dtype)


def iota(shape, dim):
    return lax.broadcasted_iota(I32, shape, dim)


def pieces(value):
    first = value.astype(BF16)
    rest = value - first.astype(F32)
    second = rest.astype(BF16)
    third = (rest - second.astype(F32)).astype(BF16)
    return first, second, third


def exact_dot(onehot, value):
    first, second, third = pieces(value)
    out = jnp.dot(onehot, third, preferred_element_type=F32)
    out = out + jnp.dot(onehot, second, preferred_element_type=F32)
    return out + jnp.dot(onehot, first, preferred_element_type=F32)


def as_column(row):
    size = row.shape[1]
    eye = iota((size, size), 0) == iota((size, size), 1)
    return jnp.sum(jnp.where(eye, row, 0), axis=1, keepdims=True)


def rank_row(keys):
    size = keys.shape[1]
    first, second = iota((size, size), 0), iota((size, size), 1)
    same = (as_column(keys) == keys) & (first < second)
    return jnp.sum(same.astype(F32), axis=0, keepdims=True)


def which_half():
    low = lax.axis_index("ap") == 0
    return low


def edge_lane(low, lanes):
    return jnp.where(low, lanes - 1, 0)


def put_face(held, plane, at, low):
    lanes = plane.shape[1]
    shift = lax.rem(at - edge_lane(low, lanes) + lanes, lanes)
    return jnp.where(iota(plane.shape, 1) == at, pltpu.roll(plane, shift, 1), held)


def take_face(held, at, low):
    lanes = held.shape[1]
    edge = edge_lane(low, lanes)
    shift = lax.rem(edge - at + lanes, lanes)
    return jnp.where(iota(held.shape, 1) == edge, pltpu.roll(held, shift, 1), 0.0)


def next_second(plane):
    rows = plane.shape[0]
    rolled = pltpu.roll(plane, rows - 1, 0)
    return jnp.where(iota(plane.shape, 0) == rows - 1, 0.0, rolled)


def next_depth(plane, halo):
    lanes = plane.shape[1]
    rolled = pltpu.roll(plane, lanes - 1, 1)
    return jnp.where(iota(plane.shape, 1) == lanes - 1, halo, rolled)


def sums(here, after, halo):
    return here, here + after, here + next_second(here), here + next_depth(here, halo), here + halo


def twice_operate(here, after, halo, before_flux, side_sums):
    buoy, along_x, along_y, along_z, low_z = side_sums
    flux = along_x * (after - here)
    total = flux - before_flux
    flux_y = along_y * (next_second(here) - here)
    under = jnp.where(iota(here.shape, 0) == 0, buoy * here, pltpu.roll(flux_y, 1, 0))
    total = total + (flux_y - under)
    flux_z = along_z * (next_depth(here, halo) - here)
    below = jnp.where(iota(here.shape, 1) == 0, low_z * (here - halo), pltpu.roll(flux_z, 1, 1))
    return total + (flux_z - below), flux


def following(x, count):
    return jnp.minimum(x + 1, count - 1), (x < count - 1).astype(F32)


def faces_kernel(now, buoy, bulk, nxt, out):
    low = which_half()
    count = now.shape[0]

    def body(x, held):
        held = put_face(held, now[x], x, low)
        held = put_face(held, buoy[x], 32 + x, low)
        return put_face(held, bulk[x] * nxt[x], 64 + x, low)

    out[...] = lax.fori_loop(0, count, body, jnp.zeros(now.shape[1:], F32), unroll=2)


def first_kernel(
    faces, now, prev, bulk, buoy, nxt, late, lap_out, mid_out, base_out, face_out
):
    low = which_half()
    count = now.shape[0]

    def body(x, carry):
        flux_v, flux_a, held = carry
        after, keep = following(x, count)
        side_sums = sums(buoy[x], keep * buoy[after], take_face(faces[...], 32 + x, low))
        here = now[x]
        lap, flux_v = twice_operate(
            here, keep * now[after], take_face(faces[...], x, low), flux_v, side_sums
        )
        lap = 0.5 * lap
        lap_out[x] = lap
        mid = 2.0 * here - prev[x] + (STEP * bulk[x]) * lap
        mid_out[x] = mid
        held = put_face(held, mid, x, low)
        scaled = bulk[x] * nxt[x]
        scaled_after = (keep * bulk[after]) * nxt[after]
        lap, flux_a = twice_operate(
            scaled, scaled_after, take_face(faces[...], 64 + x, low), flux_a, side_sums
        )
        base = 2.0 * nxt[x] - late[x] + (0.5 * STEP) * lap
        base_out[x] = base
        return flux_v, flux_a, put_face(held, bulk[x] * base, 32 + x, low)

    start = (buoy[0] * now[0], buoy[0] * (bulk[0] * nxt[0]), jnp.zeros(now.shape[1:], F32))
    _, _, held = lax.fori_loop(0, count, body, start, unroll=4)
    face_out[...] = held


def second_kernel(faces, mid_face, mid, now, bulk, buoy, lap_out, end_out):
    low = which_half()
    count = now.shape[0]

    def body(x, flux):
        after, keep = following(x, count)
        side_sums = sums(buoy[x], keep * buoy[after], take_face(faces[...], 32 + x, low))
        here = mid[x]
        lap, flux = twice_operate(
            here, keep * mid[after], take_face(mid_face[...], x, low), flux, side_sums
        )
        lap = 0.5 * lap
        lap_out[x] = lap
        end_out[x] = 2.0 * here - now[x] + (STEP * bulk[x]) * lap
        return flux

    lax.fori_loop(0, count, body, buoy[0] * mid[0], unroll=4)


def pack_traces_kernel(groups_in, receivers_in, traces_in, out, groups, receivers, traces, sems):
    copies = [
        pltpu.make_async_copy(src, dst, sems.at[i])
        for i, (src, dst) in enumerate(
            ((groups_in, groups), (receivers_in, receivers), (traces_in, traces))
        )
    ]
    for copy in copies:
        copy.start()
    shots, cap, wide = out.shape
    slots = shots * cap
    count, samples = traces.shape
    copies[0].wait()
    keys = groups[...]
    place = keys.astype(F32) * CAP + rank_row(keys)
    chosen = (iota((slots, count), 0).astype(F32) == place).astype(F32).astype(BF16)
    copies[1].wait()
    ids = as_column(receivers[...].astype(F32))
    ids = jnp.where(iota((count, 128), 1) == 0, ids, 0.0).astype(BF16)
    named = jnp.dot(chosen, ids, preferred_element_type=F32).astype(BF16)
    out[:, :, samples:] = named.reshape(shots, cap, wide - samples)
    copies[2].wait()
    moved = jnp.dot(chosen, traces[...], preferred_element_type=F32).astype(BF16)
    out[:, :, :samples] = moved.reshape(shots, cap, samples)


def places_kernel(
    at, cells, mid, end, bulk, owners, slots, about_out, hot_second_out, place_out, cls_out,
    spot_out, ids_out, end_out, rows_mid, rows_end, rows_bulk, sem,
):
    keep_end = pltpu.make_async_copy(end, end_out, sem)
    keep_end.start()
    low = which_half()
    lanes = 128
    count = cells.shape[1]

    def body(r, carry):
        row = lax.shift_right_logical(at[0, r], 7)
        rows_mid[pl.ds(r, 1), :] = mid[pl.ds(row, 1), :]
        rows_end[pl.ds(r, 1), :] = end[pl.ds(row, 1), :]
        rows_bulk[pl.ds(r, 1), :] = bulk[pl.ds(row, 1), :]
        return carry

    lax.fori_loop(0, count, body, 0, unroll=8)
    cell_row = cells[...]
    cell_col = as_column(cell_row)
    lane = iota((count, lanes), 1)
    depth_col = cell_col & (lanes - 1)
    here = lane == depth_col
    seen_mid = jnp.sum(jnp.where(here, rows_mid[...], 0.0), axis=1, keepdims=True)
    seen_end = jnp.sum(jnp.where(here, rows_end[...], 0.0), axis=1, keepdims=True)
    at_edge = here & (lane == edge_lane(low, lanes))
    edge_bulk = jnp.sum(jnp.where(at_edge, rows_bulk[...], 0.0), axis=1, keepdims=True)
    about_out[:, :lanes] = jnp.where(lane == 0, seen_mid, seen_end)
    about_out[:, lanes : 2 * lanes] = here.astype(F32)
    first_col = lax.shift_right_logical(cell_col, 13)
    about_out[:, 2 * lanes :] = jnp.where(lane == first_col + 32, edge_bulk, 0.0)
    rows = hot_second_out.shape[0]
    second_row = lax.shift_right_logical(cell_row, 7) & (rows - 1)
    hot_second_out[...] = (iota((rows, count), 0) == second_row).astype(F32).astype(BF16)

    owner = owners[...]
    tiles = owner.shape[1]
    rank = rank_row(owner).astype(I32)
    cls = owner & (CLASSES - 1)
    spot = lax.shift_right_logical(owner, CLASS_SHIFT) * CAPT + rank
    per_class = RINGS * CAPT
    place_out[...] = cls * (per_class + 1) + spot
    cls_hot = (iota((CLASSES, tiles), 0) == cls).astype(F32).astype(BF16)
    cls_out[...] = cls_hot
    spot_hot = (iota((tiles, lanes), 1) == as_column(spot)).astype(F32)
    spot_out[...] = spot_hot
    slot_col = as_column(slots[...]).astype(F32)
    ids_out[...] = jnp.dot(
        cls_hot, (spot_hot * slot_col).astype(BF16), preferred_element_type=F32
    )
    keep_end.wait()


def residual_kernel(rows_in, filters, about, hot_second, sum_mid, sum_end, face_out):
    samples = filters.shape[1]
    count, lanes = sum_mid.shape
    slots = rows_in.shape[0] * rows_in.shape[1]
    last_dims = (((1,), (1,)), ((), ()))
    values = lax.dot_general(
        rows_in[:, :, :samples].reshape(slots, samples),
        filters[...],
        last_dims,
        preferred_element_type=F32,
    )
    pick = ((iota((8, 128), 0) == 0) & (iota((8, 128), 1) == 0)).astype(F32).astype(BF16)
    ids = lax.dot_general(
        pick,
        rows_in[:, :, samples:].reshape(slots, rows_in.shape[2] - samples),
        last_dims,
        preferred_element_type=F32,
    )
    hot = (iota((count, slots), 0).astype(F32) == ids[0:1, :]).astype(F32).astype(BF16)
    observed = exact_dot(hot, values)
    resid_mid = about[:, 0:1] - observed[:, 0:1]
    resid_end = about[:, 1:2] - observed[:, 1:2]
    hot_depth = about[:, lanes : 2 * lanes]
    sum_mid[...] = hot_depth * resid_mid
    sum_end[...] = hot_depth * resid_end
    face_out[...] = exact_dot(hot_second[...], about[:, 2 * lanes :] * resid_end)


def inject_kernel(at, sum_mid, sum_end, base, mid_out, add_out):
    mid_out[...] = base[...]
    add_out[...] = jnp.zeros_like(add_out)

    def body(r, carry):
        row = lax.shift_right_logical(at[0, r], 7)
        mid_out[pl.ds(row, 1), :] = mid_out[pl.ds(row, 1), :] + sum_end[pl.ds(r, 1), :]
        add_out[pl.ds(row, 1), :] = add_out[pl.ds(row, 1), :] + sum_mid[pl.ds(r, 1), :]
        return carry

    lax.fori_loop(0, sum_mid.shape[0], body, 0, unroll=8)


def image_kernel(
    arrived, faces, mid_face, adj_face, mid, add, nxt, bulk, buoy, lap_mid, lap_now, place, cls_hot, spot_hot, ids,
    last_out, send_out, codes, scaled_face, last_held, sem,
):
    low = which_half()
    count, rows, lanes = mid.shape
    tiles = rows // 8
    per_class = send_out.shape[0] // CLASSES
    scaled_face[...] = mid_face[...] + adj_face[...]

    def clear(c, carry):
        send_out[pl.ds(c * per_class, per_class)] = jnp.zeros((per_class, 8, lanes), jnp.int16)
        return carry

    lax.fori_loop(0, CLASSES, clear, 0)

    def body(x, flux):
        after, keep = following(x, count)
        side_sums = sums(buoy[x], keep * buoy[after], take_face(faces[...], 32 + x, low))
        here = mid[x]
        lap, flux = twice_operate(
            bulk[x] * here,
            (keep * bulk[after]) * mid[after],
            take_face(scaled_face[...], 32 + x, low),
            flux,
            side_sums,
        )
        last_held[x] = 2.0 * here - nxt[x] + (0.5 * STEP) * lap + add[x]
        return flux

    lax.fori_loop(0, count, body, buoy[0] * (bulk[0] * mid[0]), unroll=4)
    keep_last = pltpu.make_async_copy(last_held, last_out, sem)
    keep_last.start()
    arrived()

    def pack(x, carry):
        image = mid[x] * lap_mid[x] + last_held[x] * lap_now[x]
        image = (STEP * image).reshape(tiles, 8, lanes)
        peak = jnp.max(jnp.max(jnp.abs(image), axis=1), axis=1, keepdims=True)
        code = jnp.ceil(16.0 * jnp.log2(jnp.maximum(peak, 1e-30))) + 1.0
        codes[pl.ds(pl.multiple_of(x * tiles, tiles), tiles), :] = jnp.broadcast_to(
            code + CODE_ZERO, (tiles, lanes)
        )
        gain = jnp.broadcast_to(32767.0 * jnp.exp2(code * (-1.0 / 16.0)), (tiles, lanes))
        whole = jnp.round(image * gain[:, None, :]).astype(I32).astype(jnp.int16)
        for t in range(tiles):
            send_out[place[0, x * tiles + t]] = whole[t]
        return carry

    lax.fori_loop(0, count, pack, 0, unroll=4)
    code = codes[...]
    upper = jnp.floor(code * (1.0 / 64.0))
    lower = code - 64.0 * upper
    hot = cls_hot[...]
    spread = spot_hot[...]
    sent = 64.0 * jnp.dot(hot, (spread * upper).astype(BF16), preferred_element_type=F32)
    sent = sent + jnp.dot(hot, (spread * lower).astype(BF16), preferred_element_type=F32)
    place_row = iota((8, lanes), 0)
    for c in range(CLASSES):
        tile = jnp.where(
            place_row == 0,
            ids[c : c + 1, :],
            jnp.where(place_row == 1, sent[c : c + 1, :], 0.0),
        )
        send_out[c * per_class + per_class - 1] = tile.astype(I32).astype(jnp.int16)
    keep_last.wait()


def combine_kernel(got, keep_out, send_out, gains_v, slots_v, gains, slots, sems, total, *partial):
    per_class = got.shape[0] // CLASSES
    used = per_class - 1
    for c in range(CLASSES):
        meta = got[c * per_class + used].astype(I32)
        slots_v[c : c + 1, :] = meta[0:1, :]
        code = meta[1:2, :].astype(F32)
        gain = jnp.exp2((code - CODE_ZERO) * (1.0 / 16.0)) * (1.0 / 32767.0)
        gains_v[c : c + 1, :] = jnp.where(code > 0, gain, 0.0)
    copies = [
        pltpu.make_async_copy(gains_v, gains, sems.at[0]),
        pltpu.make_async_copy(slots_v, slots, sems.at[1]),
    ]
    for copy in copies:
        copy.start()
    for part in partial:
        part[...] = jnp.zeros_like(part)
    for copy in copies:
        copy.wait()

    def body(src, carry):
        for s in range(used):
            ring, rank = s // CAPT, s % CAPT
            part = partial[(ring % 2) * CAPT + rank]
            at = (ring // 2) * MT_DEV + slots[src, s]
            value = got[src * per_class + s].astype(I32).astype(F32) * gains[src, s]
            part[at] = part[at] + value
        return carry

    lax.fori_loop(0, CLASSES, body, 0, unroll=2)
    for ring in range(RINGS):
        own = slice((ring // 2) * MT_DEV, (ring // 2 + 1) * MT_DEV)
        parts = [partial[(ring % 2) * CAPT + rank][own] for rank in range(CAPT)]
        total[ring * MT_DEV : (ring + 1) * MT_DEV] = (parts[0] + parts[1]) + (parts[2] + parts[3])
    low_bit = lax.shift_right_logical(lax.axis_index("shot"), CLASS_SHIFT) & 1
    for high in range(RINGS // 2):
        here = slice(high * MT_DEV, (high + 1) * MT_DEV)
        keep_out[here] = total[pl.ds((2 * high + low_bit) * MT_DEV, MT_DEV)]
        send_out[here] = total[pl.ds((2 * high + 1 - low_bit) * MT_DEV, MT_DEV)]


def fold_kernel(kept, came, keep_out, send_out):
    bit = lax.shift_right_logical(lax.axis_index("shot"), CLASS_SHIFT + 1)
    own, other = pl.ds(bit * MT_DEV, MT_DEV), pl.ds((1 - bit) * MT_DEV, MT_DEV)
    keep_out[...] = kept[own] + came[own]
    send_out[...] = kept[other] + came[other]


def swap(face):
    return lax.ppermute(face, "ap", [(0, 1), (1, 0)])


def local(
    wave_prev,
    wave_now,
    adjoint_late,
    adjoint_next,
    bulk,
    buoyancy,
    traces,
    group_filter,
    trace_group,
    trace_receiver,
    receiver_cell,
    tile_owner,
    tile_slot,
):
    shots = lax.axis_size("shot")
    rings = RINGS
    assert shots == RINGS * CLASSES
    prev, now, late, nxt = wave_prev[0], wave_now[0], adjoint_late[0], adjoint_next[0]
    bulk, buoy = bulk[0], buoyancy[0]
    count, rows, lanes = now.shape
    field = sds(now.shape)
    flat = sds((count * rows, lanes))
    samples = traces.shape[1]
    face = sds((rows, lanes))

    own_rows = traces.shape[0]
    packed = call(
        pack_traces_kernel,
        "pack_traces",
        sds((shots, CAP, samples + 128), BF16),
        [
            pltpu.VMEM((1, own_rows), I32),
            pltpu.VMEM((1, own_rows), I32),
            pltpu.VMEM((own_rows, samples), BF16),
            pltpu.SemaphoreType.DMA((3,)),
        ],
        hbm=(0, 1, 2),
        hbm_out=(0,),
    )(
        trace_group.reshape(1, -1), trace_receiver.reshape(1, -1), traces
    )
    got_rows = lax.all_to_all(
        packed, "shot", split_axis=0, concat_axis=0, tiled=True
    )

    faces = swap(call(faces_kernel, "faces", face)(now, buoy, bulk, nxt))
    lap_now, wave_mid, adj_base, mid_face = call(
        first_kernel, "first_step", (field, field, field, face), hbm_out=(0, 2)
    )(faces, now, prev, bulk, buoy, nxt, late)
    mid_face = swap(mid_face)
    lap_mid, wave_end = call(second_kernel, "second_step", (field, field), hbm_out=(0,))(
        faces, mid_face, wave_mid, now, bulk, buoy
    )
    receivers = receiver_cell.shape[1]
    tiles = tile_owner.shape[0]
    per_receiver = pltpu.VMEM((receivers, lanes), F32)
    about, hot_second, place, cls_hot, spot_hot, ids, wave_end = call(
        places_kernel,
        "places",
        (
            sds((receivers, 3 * lanes)),
            sds((rows, receivers), BF16),
            sds((1, tiles), I32),
            sds((CLASSES, tiles), BF16),
            sds((tiles, lanes)),
            sds((CLASSES, lanes)),
            flat,
        ),
        [per_receiver] * 3 + [pltpu.SemaphoreType.DMA],
        smem=(0,),
        hbm_out=(1, 2, 3, 4, 5),
        raw_out=(6,),
    )(
        receiver_cell,
        receiver_cell,
        wave_mid.reshape(flat.shape),
        wave_end.reshape(flat.shape),
        bulk.reshape(flat.shape),
        tile_owner.reshape(1, -1),
        tile_slot.reshape(1, -1),
    )
    spread = sds((receivers, lanes))
    sum_mid, sum_end, adj_face = call(
        residual_kernel, "residual", (spread, spread, face), stage=(0, 1, 3)
    )(got_rows, group_filter[0], about, hot_second)
    adj_face = swap(adj_face)
    adj_mid, adj_add = call(inject_kernel, "inject", (flat, flat), smem=(0,))(
        receiver_cell, sum_mid, sum_end, adj_base.reshape(flat.shape)
    )
    per_class = rings * CAPT + 1
    adj_end, send = call(
        image_kernel,
        "image",
        (field, sds((CLASSES * per_class, 8, lanes), jnp.int16)),
        [
            pltpu.VMEM((tiles, lanes), F32),
            pltpu.VMEM((rows, lanes), F32),
            pltpu.VMEM(now.shape, F32),
            pltpu.SemaphoreType.DMA,
        ],
        smem=(10,),
        raw_out=(0,),
        stage=(8, 9),
        late=True,
    )(
        faces, mid_face, adj_face, adj_mid.reshape(now.shape), adj_add.reshape(now.shape), nxt,
        bulk, buoy, lap_mid, lap_now, place, cls_hot, spot_hot, ids,
    )
    near = [[r * CLASSES + c for c in range(CLASSES)] for r in range(rings)]
    got = lax.all_to_all(
        send.reshape(CLASSES, per_class * 8, lanes),
        "shot",
        split_axis=0,
        concat_axis=0,
        axis_index_groups=near,
        tiled=True,
    )
    table = (CLASSES, lanes)
    half = sds((rings // 2 * MT_DEV, 8, lanes))
    kept, sent = call(
        combine_kernel,
        "combine",
        (half, half),
        [
            pltpu.VMEM(table, F32),
            pltpu.VMEM(table, I32),
            pltpu.SMEM(table, F32),
            pltpu.SMEM(table, I32),
            pltpu.SemaphoreType.DMA((2,)),
            pltpu.VMEM((rings * MT_DEV, 8, lanes), F32),
        ]
        + [pltpu.VMEM(half.shape, F32)] * (2 * CAPT),
    )(got.reshape(CLASSES * per_class, 8, lanes))
    came = lax.ppermute(sent, "shot", [(i, i ^ CLASSES) for i in range(shots)])
    quarter = sds((MT_DEV, 8, lanes))
    kept, sent = call(fold_kernel, "fold", (quarter, quarter))(kept, came)
    came = lax.ppermute(sent, "shot", [(i, i ^ (2 * CLASSES)) for i in range(shots)])
    model_grad = kept + came
    return (model_grad, wave_end.reshape(1, *now.shape), adj_end[None])


def solution(mesh):
    placed = (
        P("shot", None, None, "ap"),
        P("shot", None, None, "ap"),
        P("shot", None, None, "ap"),
        P("shot", None, None, "ap"),
        P("shot", None, None, "ap"),
        P("shot", None, None, "ap"),
        P(("shot", "ap"), None),
        P("shot", None, None),
        P(("shot", "ap"), None),
        P(("shot", "ap")),
        P("shot", "ap"),
        P("shot", None),
        P("shot"),
    )
    return jax.shard_map(
        local,
        mesh=mesh,
        in_specs=placed,
        out_specs=(P("shot", None, "ap"), P("shot", None, None, "ap"), P("shot", None, None, "ap")),
        check_vma=False,
    )
```

```python
import functools

import jax
import jax.numpy as jnp
from jax import lax
from jax.experimental import pallas as pl
from jax.experimental.pallas import tpu as pltpu
from jax.sharding import PartitionSpec as P

STEP = 0.08
MT_DEV = 8
CAP = 2
CAPT = 4
CLASSES = 32
CLASS_SHIFT = 5
RINGS = 4
CODE_ZERO = 4096.0
VMEM_LIMIT = 6 * 1024 * 1024

F32 = jnp.float32
BF16 = jnp.bfloat16
I32 = jnp.int32


def staged_kernel(kernel, stage, late, count_in, count_out, *refs):
    inputs, rest = list(refs[:count_in]), refs[count_in : len(refs) - len(stage) - 1]
    sems, buffers = refs[len(refs) - len(stage) - 1], refs[len(refs) - len(stage) :]
    copies = []
    for n, (i, buffer) in enumerate(zip(stage, buffers)):
        copies.append(pltpu.make_async_copy(inputs[i], buffer, sems.at[n]))
        copies[-1].start()
        inputs[i] = buffer

    def arrived():
        for copy in copies:
            copy.wait()

    if late:
        kernel(arrived, *inputs, *rest)
    else:
        arrived()
        kernel(*inputs, *rest)


def call(
    kernel, name, out_shape, scratch=(), smem=(), hbm_out=(), hbm=(), raw_out=(), stage=(),
    late=False,
):
    def run(*args):
        spaces = [
            pltpu.SMEM if i in smem else pltpu.HBM if i in hbm or i in stage else pltpu.VMEM
            for i in range(len(args))
        ]
        args = [
            x if space is pltpu.SMEM else pltpu.with_memory_space_constraint(x, space)
            for x, space in zip(args, spaces)
        ]
        specs = [pl.BlockSpec(memory_space=space) for space in spaces]
        flat, tree = jax.tree.flatten(out_shape)
        outs = [
            pl.BlockSpec(memory_space=pltpu.HBM if i in raw_out else pltpu.VMEM)
            for i in range(len(flat))
        ]
        shapes = [
            (pltpu.HBM if i in hbm_out or i in raw_out else pltpu.VMEM)(s.shape, s.dtype)
            for i, s in enumerate(flat)
        ]
        body, extra = kernel, []
        if stage:
            body = functools.partial(
                staged_kernel, kernel, stage, late, len(args), len(flat)
            )
            extra = [pltpu.SemaphoreType.DMA((len(stage),))]
            extra += [pltpu.VMEM(args[i].shape, args[i].dtype) for i in stage]
        return pl.pallas_call(
            body,
            out_shape=jax.tree.unflatten(tree, shapes),
            in_specs=specs,
            out_specs=jax.tree.unflatten(tree, outs),
            scratch_shapes=list(scratch) + extra,
            name=name,
            compiler_params=pltpu.CompilerParams(vmem_limit_bytes=VMEM_LIMIT),
        )(*args)

    return run


def sds(shape, dtype=F32):
    return jax.ShapeDtypeStruct(shape, dtype)


def iota(shape, dim):
    return lax.broadcasted_iota(I32, shape, dim)


def pieces(value):
    first = value.astype(BF16)
    rest = value - first.astype(F32)
    second = rest.astype(BF16)
    third = (rest - second.astype(F32)).astype(BF16)
    return first, second, third


def exact_dot(onehot, value):
    first, second, third = pieces(value)
    out = jnp.dot(onehot, third, preferred_element_type=F32)
    out = out + jnp.dot(onehot, second, preferred_element_type=F32)
    return out + jnp.dot(onehot, first, preferred_element_type=F32)


def as_column(row):
    size = row.shape[1]
    eye = iota((size, size), 0) == iota((size, size), 1)
    return jnp.sum(jnp.where(eye, row, 0), axis=1, keepdims=True)


def rank_row(keys):
    size = keys.shape[1]
    first, second = iota((size, size), 0), iota((size, size), 1)
    same = (as_column(keys) == keys) & (first < second)
    return jnp.sum(same.astype(F32), axis=0, keepdims=True)


def which_half():
    low = lax.axis_index("ap") == 0
    return low


def edge_lane(low, lanes):
    return jnp.where(low, lanes - 1, 0)


def put_face(held, plane, at, low):
    lanes = plane.shape[1]
    shift = lax.rem(at - edge_lane(low, lanes) + lanes, lanes)
    return jnp.where(iota(plane.shape, 1) == at, pltpu.roll(plane, shift, 1), held)


def take_face(held, at, low):
    lanes = held.shape[1]
    edge = edge_lane(low, lanes)
    shift = lax.rem(edge - at + lanes, lanes)
    return jnp.where(iota(held.shape, 1) == edge, pltpu.roll(held, shift, 1), 0.0)


def next_second(plane):
    rows = plane.shape[0]
    rolled = pltpu.roll(plane, rows - 1, 0)
    return jnp.where(iota(plane.shape, 0) == rows - 1, 0.0, rolled)


def next_depth(plane, halo):
    lanes = plane.shape[1]
    rolled = pltpu.roll(plane, lanes - 1, 1)
    return jnp.where(iota(plane.shape, 1) == lanes - 1, halo, rolled)


def sums(here, after, halo):
    return here, here + after, here + next_second(here), here + next_depth(here, halo), here + halo


def twice_operate(here, after, halo, before_flux, side_sums):
    buoy, along_x, along_y, along_z, low_z = side_sums
    flux = along_x * (after - here)
    total = flux - before_flux
    flux_y = along_y * (next_second(here) - here)
    under = jnp.where(iota(here.shape, 0) == 0, buoy * here, pltpu.roll(flux_y, 1, 0))
    total = total + (flux_y - under)
    flux_z = along_z * (next_depth(here, halo) - here)
    below = jnp.where(iota(here.shape, 1) == 0, low_z * (here - halo), pltpu.roll(flux_z, 1, 1))
    return total + (flux_z - below), flux


def following(x, count):
    return jnp.minimum(x + 1, count - 1), (x < count - 1).astype(F32)


def faces_kernel(now, buoy, bulk, nxt, out):
    low = which_half()
    count = now.shape[0]

    def body(x, held):
        held = put_face(held, now[x], x, low)
        held = put_face(held, buoy[x], 32 + x, low)
        return put_face(held, bulk[x] * nxt[x], 64 + x, low)

    out[...] = lax.fori_loop(0, count, body, jnp.zeros(now.shape[1:], F32), unroll=2)


def first_kernel(
    faces, now, prev, bulk, buoy, nxt, late, lap_out, mid_out, base_out, face_out
):
    low = which_half()
    count = now.shape[0]

    def body(x, carry):
        flux_v, flux_a, held = carry
        after, keep = following(x, count)
        side_sums = sums(buoy[x], keep * buoy[after], take_face(faces[...], 32 + x, low))
        here = now[x]
        lap, flux_v = twice_operate(
            here, keep * now[after], take_face(faces[...], x, low), flux_v, side_sums
        )
        lap = 0.5 * lap
        lap_out[x] = lap
        mid = 2.0 * here - prev[x] + (STEP * bulk[x]) * lap
        mid_out[x] = mid
        held = put_face(held, mid, x, low)
        scaled = bulk[x] * nxt[x]
        scaled_after = (keep * bulk[after]) * nxt[after]
        lap, flux_a = twice_operate(
            scaled, scaled_after, take_face(faces[...], 64 + x, low), flux_a, side_sums
        )
        base = 2.0 * nxt[x] - late[x] + (0.5 * STEP) * lap
        base_out[x] = base
        return flux_v, flux_a, put_face(held, bulk[x] * base, 32 + x, low)

    start = (buoy[0] * now[0], buoy[0] * (bulk[0] * nxt[0]), jnp.zeros(now.shape[1:], F32))
    _, _, held = lax.fori_loop(0, count, body, start, unroll=4)
    face_out[...] = held


def second_kernel(faces, mid_face, mid, now, bulk, buoy, lap_out, end_out):
    low = which_half()
    count = now.shape[0]

    def body(x, flux):
        after, keep = following(x, count)
        side_sums = sums(buoy[x], keep * buoy[after], take_face(faces[...], 32 + x, low))
        here = mid[x]
        lap, flux = twice_operate(
            here, keep * mid[after], take_face(mid_face[...], x, low), flux, side_sums
        )
        lap = 0.5 * lap
        lap_out[x] = lap
        end_out[x] = 2.0 * here - now[x] + (STEP * bulk[x]) * lap
        return flux

    lax.fori_loop(0, count, body, buoy[0] * mid[0], unroll=4)


def pack_traces_kernel(
    groups_in, receivers_in, traces_in, out, groups, receivers, traces, made, sems
):
    copies = [
        pltpu.make_async_copy(src, dst, sems.at[i])
        for i, (src, dst) in enumerate(
            ((groups_in, groups), (receivers_in, receivers), (traces_in, traces))
        )
    ]
    for copy in copies:
        copy.start()
    shots, cap, wide = out.shape
    slots = shots * cap
    count, samples = traces.shape
    copies[0].wait()
    keys = groups[...]
    place = keys.astype(F32) * CAP + rank_row(keys)
    chosen = (iota((slots, count), 0).astype(F32) == place).astype(F32).astype(BF16)
    copies[1].wait()
    ids = as_column(receivers[...].astype(F32))
    ids = jnp.where(iota((count, 128), 1) == 0, ids, 0.0).astype(BF16)
    named = jnp.dot(chosen, ids, preferred_element_type=F32).astype(BF16)
    made[:, :, samples:] = named.reshape(shots, cap, wide - samples)
    copies[2].wait()
    stores = []
    for n in range(2):
        part = slice(n * slots // 2, (n + 1) * slots // 2)
        dest = pl.ds(n * shots // 2, shots // 2)
        moved = jnp.dot(chosen[part], traces[...], preferred_element_type=F32).astype(BF16)
        made[dest, :, :samples] = moved.reshape(shots // 2, cap, samples)
        stores.append(pltpu.make_async_copy(made.at[dest], out.at[dest], sems.at[3 + n]))
        stores[-1].start()
    for copy in stores:
        copy.wait()


def places_kernel(
    at, cells, mid, end, bulk, owners, slots, about_out, hot_second_out, place_out, cls_out,
    spot_out, ids_out, end_out, rows_mid, rows_end, rows_bulk, sem,
):
    keep_end = pltpu.make_async_copy(end, end_out, sem)
    keep_end.start()
    low = which_half()
    lanes = 128
    count = cells.shape[1]

    def body(r, carry):
        row = lax.shift_right_logical(at[0, r], 7)
        rows_mid[pl.ds(r, 1), :] = mid[pl.ds(row, 1), :]
        rows_end[pl.ds(r, 1), :] = end[pl.ds(row, 1), :]
        rows_bulk[pl.ds(r, 1), :] = bulk[pl.ds(row, 1), :]
        return carry

    lax.fori_loop(0, count, body, 0, unroll=8)
    cell_row = cells[...]
    cell_col = as_column(cell_row)
    lane = iota((count, lanes), 1)
    depth_col = cell_col & (lanes - 1)
    here = lane == depth_col
    seen_mid = jnp.sum(jnp.where(here, rows_mid[...], 0.0), axis=1, keepdims=True)
    seen_end = jnp.sum(jnp.where(here, rows_end[...], 0.0), axis=1, keepdims=True)
    at_edge = here & (lane == edge_lane(low, lanes))
    edge_bulk = jnp.sum(jnp.where(at_edge, rows_bulk[...], 0.0), axis=1, keepdims=True)
    about_out[:, :lanes] = jnp.where(lane == 0, seen_mid, seen_end)
    about_out[:, lanes : 2 * lanes] = here.astype(F32)
    first_col = lax.shift_right_logical(cell_col, 13)
    about_out[:, 2 * lanes :] = jnp.where(lane == first_col + 32, edge_bulk, 0.0)
    rows = hot_second_out.shape[0]
    second_row = lax.shift_right_logical(cell_row, 7) & (rows - 1)
    hot_second_out[...] = (iota((rows, count), 0) == second_row).astype(F32).astype(BF16)

    owner = owners[...]
    tiles = owner.shape[1]
    rank = rank_row(owner).astype(I32)
    cls = owner & (CLASSES - 1)
    spot = lax.shift_right_logical(owner, CLASS_SHIFT) * CAPT + rank
    per_class = RINGS * CAPT
    place_out[...] = cls * (per_class + 1) + spot
    cls_hot = (iota((CLASSES, tiles), 0) == cls).astype(F32).astype(BF16)
    cls_out[...] = cls_hot
    spot_hot = (iota((tiles, lanes), 1) == as_column(spot)).astype(F32)
    spot_out[...] = spot_hot
    slot_col = as_column(slots[...]).astype(F32)
    ids_out[...] = jnp.dot(
        cls_hot, (spot_hot * slot_col).astype(BF16), preferred_element_type=F32
    )
    keep_end.wait()


def residual_kernel(
    arrived, rows_in, filters, about, hot_second, sum_mid, sum_end, face_out, held, sems
):
    shots, cap, wide = rows_in.shape
    parts = sems.shape[0]
    each = shots // parts
    copies = []
    for n in range(parts):
        part = pl.ds(n * each, each)
        copies.append(pltpu.make_async_copy(rows_in.at[part], held.at[part], sems.at[n]))
        copies[-1].start()
    samples = filters.shape[1]
    count, lanes = sum_mid.shape
    slots = each * cap
    last_dims = (((1,), (1,)), ((), ()))
    pick = ((iota((8, 128), 0) == 0) & (iota((8, 128), 1) == 0)).astype(F32).astype(BF16)
    receiver = iota((count, slots), 0).astype(F32)
    observed = jnp.zeros((count, filters.shape[0]), F32)
    arrived()
    for n in range(parts):
        copies[n].wait()
        here = slice(n * each, (n + 1) * each)
        values = lax.dot_general(
            held[here, :, :samples].reshape(slots, samples),
            filters[...],
            last_dims,
            preferred_element_type=F32,
        )
        ids = lax.dot_general(
            pick,
            held[here, :, samples:].reshape(slots, wide - samples),
            last_dims,
            preferred_element_type=F32,
        )
        hot = (receiver == ids[0:1, :]).astype(F32).astype(BF16)
        observed = observed + exact_dot(hot, values)
    resid_mid = about[:, 0:1] - observed[:, 0:1]
    resid_end = about[:, 1:2] - observed[:, 1:2]
    hot_depth = about[:, lanes : 2 * lanes]
    sum_mid[...] = hot_depth * resid_mid
    sum_end[...] = hot_depth * resid_end
    face_out[...] = exact_dot(hot_second[...], about[:, 2 * lanes :] * resid_end)


def inject_kernel(at, sum_mid, sum_end, base, mid_out, add_out):
    mid_out[...] = base[...]
    add_out[...] = jnp.zeros_like(add_out)

    def body(r, carry):
        row = lax.shift_right_logical(at[0, r], 7)
        mid_out[pl.ds(row, 1), :] = mid_out[pl.ds(row, 1), :] + sum_end[pl.ds(r, 1), :]
        add_out[pl.ds(row, 1), :] = add_out[pl.ds(row, 1), :] + sum_mid[pl.ds(r, 1), :]
        return carry

    lax.fori_loop(0, sum_mid.shape[0], body, 0, unroll=8)


def image_kernel(
    arrived, faces, mid_face, adj_face, mid, add, nxt, bulk, buoy, lap_mid, lap_now, place, cls_hot, spot_hot, ids,
    last_out, send_out, codes, scaled_face, last_held, sem,
):
    low = which_half()
    count, rows, lanes = mid.shape
    tiles = rows // 8
    per_class = send_out.shape[0] // CLASSES
    scaled_face[...] = mid_face[...] + adj_face[...]

    def body(x, flux):
        after, keep = following(x, count)
        side_sums = sums(buoy[x], keep * buoy[after], take_face(faces[...], 32 + x, low))
        here = mid[x]
        lap, flux = twice_operate(
            bulk[x] * here,
            (keep * bulk[after]) * mid[after],
            take_face(scaled_face[...], 32 + x, low),
            flux,
            side_sums,
        )
        last_held[x] = 2.0 * here - nxt[x] + (0.5 * STEP) * lap + add[x]
        return flux

    lax.fori_loop(0, count, body, buoy[0] * (bulk[0] * mid[0]), unroll=8)
    keep_last = pltpu.make_async_copy(last_held, last_out, sem)
    keep_last.start()
    arrived()

    def pack(x, carry):
        image = mid[x] * lap_mid[x] + last_held[x] * lap_now[x]
        image = (STEP * image).reshape(tiles, 8, lanes)
        peak = jnp.max(jnp.max(jnp.abs(image), axis=1), axis=1, keepdims=True)
        code = jnp.ceil(16.0 * jnp.log2(jnp.maximum(peak, 1e-30))) + 1.0
        codes[pl.ds(pl.multiple_of(x * tiles, tiles), tiles), :] = jnp.broadcast_to(
            code + CODE_ZERO, (tiles, lanes)
        )
        gain = jnp.broadcast_to(32767.0 * jnp.exp2(code * (-1.0 / 16.0)), (tiles, lanes))
        whole = jnp.round(image * gain[:, None, :]).astype(I32).astype(jnp.int16)
        for t in range(tiles):
            send_out[place[0, x * tiles + t]] = whole[t]
        return carry

    lax.fori_loop(0, count, pack, 0, unroll=8)
    code = codes[...]
    upper = jnp.floor(code * (1.0 / 64.0))
    lower = code - 64.0 * upper
    hot = cls_hot[...]
    spread = spot_hot[...]
    sent = 64.0 * jnp.dot(hot, (spread * upper).astype(BF16), preferred_element_type=F32)
    sent = sent + jnp.dot(hot, (spread * lower).astype(BF16), preferred_element_type=F32)
    place_row = iota((8, lanes), 0)
    for c in range(CLASSES):
        tile = jnp.where(
            place_row == 0,
            ids[c : c + 1, :],
            jnp.where(place_row == 1, sent[c : c + 1, :], 0.0),
        )
        send_out[c * per_class + per_class - 1] = tile.astype(I32).astype(jnp.int16)
    keep_last.wait()


def combine_kernel(got, keep_out, send_out, gains_v, slots_v, gains, slots, sems, total, *partial):
    per_class = got.shape[0] // CLASSES
    used = per_class - 1
    for c in range(CLASSES):
        meta = got[c * per_class + used].astype(I32)
        slots_v[c : c + 1, :] = meta[0:1, :]
        code = meta[1:2, :].astype(F32)
        gain = jnp.exp2((code - CODE_ZERO) * (1.0 / 16.0)) * (1.0 / 32767.0)
        gains_v[c : c + 1, :] = jnp.where(code > 0, gain, 0.0)
    copies = [
        pltpu.make_async_copy(gains_v, gains, sems.at[0]),
        pltpu.make_async_copy(slots_v, slots, sems.at[1]),
    ]
    for copy in copies:
        copy.start()
    for part in partial:
        part[...] = jnp.zeros_like(part)
    for copy in copies:
        copy.wait()

    def body(src, carry):
        for s in range(used):
            ring, rank = s // CAPT, s % CAPT
            part = partial[(ring % 2) * CAPT + rank]
            at = (ring // 2) * MT_DEV + slots[src, s]
            value = got[src * per_class + s].astype(I32).astype(F32) * gains[src, s]
            part[at] = part[at] + value
        return carry

    lax.fori_loop(0, CLASSES, body, 0, unroll=2)
    for ring in range(RINGS):
        own = slice((ring // 2) * MT_DEV, (ring // 2 + 1) * MT_DEV)
        parts = [partial[(ring % 2) * CAPT + rank][own] for rank in range(CAPT)]
        total[ring * MT_DEV : (ring + 1) * MT_DEV] = (parts[0] + parts[1]) + (parts[2] + parts[3])
    ring = lax.shift_right_logical(lax.axis_index("shot"), CLASS_SHIFT)

    def owned(other):
        return total[pl.ds((ring ^ other) * MT_DEV, MT_DEV)]

    keep_out[:MT_DEV] = owned(0)
    keep_out[MT_DEV:] = owned(3)
    send_out[:MT_DEV] = owned(1)
    send_out[MT_DEV:] = owned(2)


def fold_kernel(kept, came, keep_out, send_out):
    keep_out[...] = kept[:MT_DEV] + came[:MT_DEV]
    send_out[...] = kept[MT_DEV:] + came[MT_DEV:]


def last_kernel(kept, came, out):
    out[...] = kept[...] + came[...]


def swap(face):
    return lax.ppermute(face, "ap", [(0, 1), (1, 0)])


def local(
    wave_prev,
    wave_now,
    adjoint_late,
    adjoint_next,
    bulk,
    buoyancy,
    traces,
    group_filter,
    trace_group,
    trace_receiver,
    receiver_cell,
    tile_owner,
    tile_slot,
):
    shots = lax.axis_size("shot")
    rings = RINGS
    assert shots == RINGS * CLASSES
    prev, now, late, nxt = wave_prev[0], wave_now[0], adjoint_late[0], adjoint_next[0]
    bulk, buoy = bulk[0], buoyancy[0]
    count, rows, lanes = now.shape
    field = sds(now.shape)
    flat = sds((count * rows, lanes))
    samples = traces.shape[1]
    face = sds((rows, lanes))

    own_rows = traces.shape[0]
    packed = call(
        pack_traces_kernel,
        "pack_traces",
        sds((shots, CAP, samples + 128), BF16),
        [
            pltpu.VMEM((1, own_rows), I32),
            pltpu.VMEM((1, own_rows), I32),
            pltpu.VMEM((own_rows, samples), BF16),
            pltpu.VMEM((shots, CAP, samples + 128), BF16),
            pltpu.SemaphoreType.DMA((5,)),
        ],
        hbm=(0, 1, 2),
        raw_out=(0,),
    )(
        trace_group.reshape(1, -1), trace_receiver.reshape(1, -1), traces
    )
    got_rows = lax.all_to_all(
        packed, "shot", split_axis=0, concat_axis=0, tiled=True
    )

    faces = swap(call(faces_kernel, "faces", face)(now, buoy, bulk, nxt))
    lap_now, wave_mid, adj_base, mid_face = call(
        first_kernel, "first_step", (field, field, field, face), hbm_out=(0, 2)
    )(faces, now, prev, bulk, buoy, nxt, late)
    mid_face = swap(mid_face)
    lap_mid, wave_end = call(second_kernel, "second_step", (field, field), hbm_out=(0,))(
        faces, mid_face, wave_mid, now, bulk, buoy
    )
    receivers = receiver_cell.shape[1]
    tiles = tile_owner.shape[0]
    per_receiver = pltpu.VMEM((receivers, lanes), F32)
    about, hot_second, place, cls_hot, spot_hot, ids, wave_end = call(
        places_kernel,
        "places",
        (
            sds((receivers, 3 * lanes)),
            sds((rows, receivers), BF16),
            sds((1, tiles), I32),
            sds((CLASSES, tiles), BF16),
            sds((tiles, lanes)),
            sds((CLASSES, lanes)),
            flat,
        ),
        [per_receiver] * 3 + [pltpu.SemaphoreType.DMA],
        smem=(0,),
        hbm_out=(1, 2, 3, 4, 5),
        raw_out=(6,),
    )(
        receiver_cell,
        receiver_cell,
        wave_mid.reshape(flat.shape),
        wave_end.reshape(flat.shape),
        bulk.reshape(flat.shape),
        tile_owner.reshape(1, -1),
        tile_slot.reshape(1, -1),
    )
    spread = sds((receivers, lanes))
    sum_mid, sum_end, adj_face = call(
        residual_kernel,
        "residual",
        (spread, spread, face),
        [pltpu.VMEM(got_rows.shape, BF16), pltpu.SemaphoreType.DMA((2,))],
        hbm=(0,),
        stage=(1, 3),
        late=True,
    )(got_rows, group_filter[0], about, hot_second)
    adj_face = swap(adj_face)
    adj_mid, adj_add = call(inject_kernel, "inject", (flat, flat), smem=(0,))(
        receiver_cell, sum_mid, sum_end, adj_base.reshape(flat.shape)
    )
    per_class = rings * CAPT + 1
    adj_end, send = call(
        image_kernel,
        "image",
        (field, sds((CLASSES * per_class, 8, lanes), jnp.int16)),
        [
            pltpu.VMEM((tiles, lanes), F32),
            pltpu.VMEM((rows, lanes), F32),
            pltpu.VMEM(now.shape, F32),
            pltpu.SemaphoreType.DMA,
        ],
        smem=(10,),
        raw_out=(0,),
        stage=(8, 9),
        late=True,
    )(
        faces, mid_face, adj_face, adj_mid.reshape(now.shape), adj_add.reshape(now.shape), nxt,
        bulk, buoy, lap_mid, lap_now, place, cls_hot, spot_hot, ids,
    )
    near = [[r * CLASSES + c for c in range(CLASSES)] for r in range(rings)]
    got = lax.all_to_all(
        send.reshape(CLASSES, per_class * 8, lanes),
        "shot",
        split_axis=0,
        concat_axis=0,
        axis_index_groups=near,
        tiled=True,
    )
    table = (CLASSES, lanes)
    half = sds((rings // 2 * MT_DEV, 8, lanes))
    kept, sent = call(
        combine_kernel,
        "combine",
        (half, half),
        [
            pltpu.VMEM(table, F32),
            pltpu.VMEM(table, I32),
            pltpu.SMEM(table, F32),
            pltpu.SMEM(table, I32),
            pltpu.SemaphoreType.DMA((2,)),
            pltpu.VMEM((rings * MT_DEV, 8, lanes), F32),
        ]
        + [pltpu.VMEM(half.shape, F32)] * (2 * CAPT),
    )(got.reshape(CLASSES * per_class, 8, lanes))
    came = lax.ppermute(sent, "shot", [(i, i ^ CLASSES) for i in range(shots)])
    quarter = sds((MT_DEV, 8, lanes))
    kept, sent = call(fold_kernel, "fold", (quarter, quarter))(kept, came)
    came = lax.ppermute(sent, "shot", [(i, i ^ (3 * CLASSES)) for i in range(shots)])
    model_grad = call(last_kernel, "last_sum", quarter, hbm_out=(0,))(kept, came)
    return (model_grad, wave_end.reshape(1, *now.shape), adj_end[None])


def solution(mesh):
    placed = (
        P("shot", None, None, "ap"),
        P("shot", None, None, "ap"),
        P("shot", None, None, "ap"),
        P("shot", None, None, "ap"),
        P("shot", None, None, "ap"),
        P("shot", None, None, "ap"),
        P(("shot", "ap"), None),
        P("shot", None, None),
        P(("shot", "ap"), None),
        P(("shot", "ap")),
        P("shot", "ap"),
        P("shot", None),
        P("shot"),
    )
    return jax.shard_map(
        local,
        mesh=mesh,
        in_specs=placed,
        out_specs=(P("shot", None, "ap"), P("shot", None, None, "ap"), P("shot", None, None, "ap")),
        check_vma=False,
    )
```

```python
import functools

import jax
import jax.numpy as jnp
from jax import lax
from jax.experimental import pallas as pl
from jax.experimental.pallas import tpu as pltpu
from jax.sharding import PartitionSpec as P

STEP = 0.08
MT_DEV = 8
CAP = 2
CAPT = 4
CLASSES = 32
CLASS_SHIFT = 5
RINGS = 4
CODE_ZERO = 4096.0
VMEM_LIMIT = 6 * 1024 * 1024

F32 = jnp.float32
BF16 = jnp.bfloat16
I32 = jnp.int32


def staged_kernel(kernel, stage, late, count_in, count_out, *refs):
    inputs, rest = list(refs[:count_in]), refs[count_in : len(refs) - len(stage) - 1]
    sems, buffers = refs[len(refs) - len(stage) - 1], refs[len(refs) - len(stage) :]
    copies = []
    for n, (i, buffer) in enumerate(zip(stage, buffers)):
        copies.append(pltpu.make_async_copy(inputs[i], buffer, sems.at[n]))
        copies[-1].start()
        inputs[i] = buffer

    def arrived():
        for copy in copies:
            copy.wait()

    if late:
        kernel(arrived, *inputs, *rest)
    else:
        arrived()
        kernel(*inputs, *rest)


def call(
    kernel, name, out_shape, scratch=(), smem=(), hbm_out=(), hbm=(), raw_out=(), stage=(),
    late=False,
):
    def run(*args):
        spaces = [
            pltpu.SMEM if i in smem else pltpu.HBM if i in hbm or i in stage else pltpu.VMEM
            for i in range(len(args))
        ]
        args = [
            x if space is pltpu.SMEM else pltpu.with_memory_space_constraint(x, space)
            for x, space in zip(args, spaces)
        ]
        specs = [pl.BlockSpec(memory_space=space) for space in spaces]
        flat, tree = jax.tree.flatten(out_shape)
        outs = [
            pl.BlockSpec(memory_space=pltpu.HBM if i in raw_out else pltpu.VMEM)
            for i in range(len(flat))
        ]
        shapes = [
            (pltpu.HBM if i in hbm_out or i in raw_out else pltpu.VMEM)(s.shape, s.dtype)
            for i, s in enumerate(flat)
        ]
        body, extra = kernel, []
        if stage:
            body = functools.partial(
                staged_kernel, kernel, stage, late, len(args), len(flat)
            )
            extra = [pltpu.SemaphoreType.DMA((len(stage),))]
            extra += [pltpu.VMEM(args[i].shape, args[i].dtype) for i in stage]
        return pl.pallas_call(
            body,
            out_shape=jax.tree.unflatten(tree, shapes),
            in_specs=specs,
            out_specs=jax.tree.unflatten(tree, outs),
            scratch_shapes=list(scratch) + extra,
            name=name,
            compiler_params=pltpu.CompilerParams(vmem_limit_bytes=VMEM_LIMIT),
        )(*args)

    return run


def sds(shape, dtype=F32):
    return jax.ShapeDtypeStruct(shape, dtype)


def iota(shape, dim):
    return lax.broadcasted_iota(I32, shape, dim)


def pieces(value):
    first = value.astype(BF16)
    rest = value - first.astype(F32)
    second = rest.astype(BF16)
    third = (rest - second.astype(F32)).astype(BF16)
    return first, second, third


def exact_dot(onehot, value):
    first, second, third = pieces(value)
    out = jnp.dot(onehot, third, preferred_element_type=F32)
    out = out + jnp.dot(onehot, second, preferred_element_type=F32)
    return out + jnp.dot(onehot, first, preferred_element_type=F32)


def as_column(row):
    size = row.shape[1]
    eye = iota((size, size), 0) == iota((size, size), 1)
    return jnp.sum(jnp.where(eye, row, 0), axis=1, keepdims=True)


def rank_row(keys):
    size = keys.shape[1]
    first, second = iota((size, size), 0), iota((size, size), 1)
    same = (as_column(keys) == keys) & (first < second)
    return jnp.sum(same.astype(F32), axis=0, keepdims=True)


def which_half():
    low = lax.axis_index("ap") == 0
    return low


def edge_lane(low, lanes):
    return jnp.where(low, lanes - 1, 0)


def put_face(held, plane, at, low):
    lanes = plane.shape[1]
    shift = lax.rem(at - edge_lane(low, lanes) + lanes, lanes)
    return jnp.where(iota(plane.shape, 1) == at, pltpu.roll(plane, shift, 1), held)


def take_face(held, at, low):
    lanes = held.shape[1]
    edge = edge_lane(low, lanes)
    shift = lax.rem(edge - at + lanes, lanes)
    return jnp.where(iota(held.shape, 1) == edge, pltpu.roll(held, shift, 1), 0.0)


def next_second(plane):
    rows = plane.shape[0]
    rolled = pltpu.roll(plane, rows - 1, 0)
    return jnp.where(iota(plane.shape, 0) == rows - 1, 0.0, rolled)


def next_depth(plane, halo):
    lanes = plane.shape[1]
    rolled = pltpu.roll(plane, lanes - 1, 1)
    return jnp.where(iota(plane.shape, 1) == lanes - 1, halo, rolled)


def sums(here, after, halo):
    return here, here + after, here + next_second(here), here + next_depth(here, halo), here + halo


def twice_operate(here, after, halo, before_flux, side_sums):
    buoy, along_x, along_y, along_z, low_z = side_sums
    flux = along_x * (after - here)
    total = flux - before_flux
    flux_y = along_y * (next_second(here) - here)
    under = jnp.where(iota(here.shape, 0) == 0, buoy * here, pltpu.roll(flux_y, 1, 0))
    total = total + (flux_y - under)
    flux_z = along_z * (next_depth(here, halo) - here)
    below = jnp.where(iota(here.shape, 1) == 0, low_z * (here - halo), pltpu.roll(flux_z, 1, 1))
    return total + (flux_z - below), flux


def following(x, count):
    return jnp.minimum(x + 1, count - 1), (x < count - 1).astype(F32)


def faces_kernel(arrived, now, buoy, bulk, nxt, out):
    low = which_half()
    count = now.shape[0]

    def plain(x, held):
        return put_face(put_face(held, now[x], x, low), buoy[x], 32 + x, low)

    def scaled(x, held):
        return put_face(held, bulk[x] * nxt[x], 64 + x, low)

    held = lax.fori_loop(0, count, plain, jnp.zeros(now.shape[1:], F32), unroll=4)
    arrived()
    out[...] = lax.fori_loop(0, count, scaled, held, unroll=8)


def first_kernel(
    faces, now, prev, bulk, buoy, nxt, late, lap_out, mid_out, base_out, face_out
):
    low = which_half()
    count = now.shape[0]

    def body(x, carry):
        flux_v, flux_a, held = carry
        after, keep = following(x, count)
        side_sums = sums(buoy[x], keep * buoy[after], take_face(faces[...], 32 + x, low))
        here = now[x]
        lap, flux_v = twice_operate(
            here, keep * now[after], take_face(faces[...], x, low), flux_v, side_sums
        )
        lap = 0.5 * lap
        lap_out[x] = lap
        mid = 2.0 * here - prev[x] + (STEP * bulk[x]) * lap
        mid_out[x] = mid
        held = put_face(held, mid, x, low)
        scaled = bulk[x] * nxt[x]
        scaled_after = (keep * bulk[after]) * nxt[after]
        lap, flux_a = twice_operate(
            scaled, scaled_after, take_face(faces[...], 64 + x, low), flux_a, side_sums
        )
        base = 2.0 * nxt[x] - late[x] + (0.5 * STEP) * lap
        base_out[x] = base
        return flux_v, flux_a, put_face(held, bulk[x] * base, 32 + x, low)

    start = (buoy[0] * now[0], buoy[0] * (bulk[0] * nxt[0]), jnp.zeros(now.shape[1:], F32))
    _, _, held = lax.fori_loop(0, count, body, start, unroll=4)
    face_out[...] = held


def second_kernel(
    faces, mid_face, mid, now, bulk, buoy, lap_first, base, lap_out, end_out, lap_kept, base_kept,
    sems,
):
    copies = [
        pltpu.make_async_copy(lap_first, lap_kept, sems.at[0]),
        pltpu.make_async_copy(base, base_kept, sems.at[1]),
    ]
    for copy in copies:
        copy.start()
    low = which_half()
    count = now.shape[0]

    def body(x, flux):
        after, keep = following(x, count)
        side_sums = sums(buoy[x], keep * buoy[after], take_face(faces[...], 32 + x, low))
        here = mid[x]
        lap, flux = twice_operate(
            here, keep * mid[after], take_face(mid_face[...], x, low), flux, side_sums
        )
        lap = 0.5 * lap
        lap_out[x] = lap
        end_out[x] = 2.0 * here - now[x] + (STEP * bulk[x]) * lap
        return flux

    lax.fori_loop(0, count, body, buoy[0] * mid[0], unroll=4)
    for copy in copies:
        copy.wait()


def pack_traces_kernel(
    groups_in, receivers_in, traces_in, out, groups, receivers, traces, made, sems
):
    copies = [
        pltpu.make_async_copy(src, dst, sems.at[i])
        for i, (src, dst) in enumerate(
            ((groups_in, groups), (receivers_in, receivers), (traces_in, traces))
        )
    ]
    for copy in copies:
        copy.start()
    shots, cap, wide = out.shape
    slots = shots * cap
    count, samples = traces.shape
    copies[0].wait()
    keys = groups[...]
    place = keys.astype(F32) * CAP + rank_row(keys)
    chosen = (iota((slots, count), 0).astype(F32) == place).astype(F32).astype(BF16)
    copies[1].wait()
    ids = as_column(receivers[...].astype(F32))
    ids = jnp.where(iota((count, 128), 1) == 0, ids, 0.0).astype(BF16)
    named = jnp.dot(chosen, ids, preferred_element_type=F32).astype(BF16)
    made[:, :, samples:] = named.reshape(shots, cap, wide - samples)
    copies[2].wait()
    stores = []
    for n in range(2):
        part = slice(n * slots // 2, (n + 1) * slots // 2)
        dest = pl.ds(n * shots // 2, shots // 2)
        moved = jnp.dot(chosen[part], traces[...], preferred_element_type=F32).astype(BF16)
        made[dest, :, :samples] = moved.reshape(shots // 2, cap, samples)
        stores.append(pltpu.make_async_copy(made.at[dest], out.at[dest], sems.at[3 + n]))
        stores[-1].start()
    for copy in stores:
        copy.wait()


def places_kernel(
    at, cells, bulk, owners, slots, marks_out, hot_second_out, place_out, cls_out, spot_out,
    ids_out, rows_bulk,
):
    low = which_half()
    lanes = 128
    count = cells.shape[1]

    def body(r, carry):
        row = lax.shift_right_logical(at[0, r], 7)
        rows_bulk[pl.ds(r, 1), :] = bulk[pl.ds(row, 1), :]
        return carry

    lax.fori_loop(0, count, body, 0, unroll=8)
    cell_row = cells[...]
    cell_col = as_column(cell_row)
    lane = iota((count, lanes), 1)
    here = lane == (cell_col & (lanes - 1))
    at_edge = here & (lane == edge_lane(low, lanes))
    edge_bulk = jnp.sum(jnp.where(at_edge, rows_bulk[...], 0.0), axis=1, keepdims=True)
    marks_out[:, :lanes] = here.astype(F32)
    first_col = lax.shift_right_logical(cell_col, 13)
    marks_out[:, lanes:] = jnp.where(lane == first_col + 32, edge_bulk, 0.0)
    rows = hot_second_out.shape[0]
    second_row = lax.shift_right_logical(cell_row, 7) & (rows - 1)
    hot_second_out[...] = (iota((rows, count), 0) == second_row).astype(F32).astype(BF16)

    owner = owners[...]
    tiles = owner.shape[1]
    rank = rank_row(owner).astype(I32)
    cls = owner & (CLASSES - 1)
    spot = lax.shift_right_logical(owner, CLASS_SHIFT) * CAPT + rank
    per_class = RINGS * CAPT
    place_out[...] = cls * (per_class + 1) + spot
    cls_hot = (iota((CLASSES, tiles), 0) == cls).astype(F32).astype(BF16)
    cls_out[...] = cls_hot
    spot_hot = (iota((tiles, lanes), 1) == as_column(spot)).astype(F32)
    spot_out[...] = spot_hot
    slot_col = as_column(slots[...]).astype(F32)
    ids_out[...] = jnp.dot(
        cls_hot, (spot_hot * slot_col).astype(BF16), preferred_element_type=F32
    )


def seen_kernel(
    arrived, at, marks, mid, end, lap_mid, seen_out, end_kept, lap_kept, rows_mid, rows_end, sems
):
    copies = [
        pltpu.make_async_copy(end, end_kept, sems.at[0]),
        pltpu.make_async_copy(lap_mid, lap_kept, sems.at[1]),
    ]
    for copy in copies:
        copy.start()
    count, lanes = seen_out.shape

    def body(r, carry):
        row = lax.shift_right_logical(at[0, r], 7)
        rows_mid[pl.ds(r, 1), :] = mid[pl.ds(row, 1), :]
        rows_end[pl.ds(r, 1), :] = end[pl.ds(row, 1), :]
        return carry

    lax.fori_loop(0, count, body, 0, unroll=8)
    arrived()
    here = marks[:, :lanes] > 0.5
    seen_mid = jnp.sum(jnp.where(here, rows_mid[...], 0.0), axis=1, keepdims=True)
    seen_end = jnp.sum(jnp.where(here, rows_end[...], 0.0), axis=1, keepdims=True)
    seen_out[...] = jnp.where(iota((count, lanes), 1) == 0, seen_mid, seen_end)
    for copy in copies:
        copy.wait()


def residual_kernel(rows_in, filters, seen, marks, hot_second, sum_mid, sum_end, face_out):
    samples = filters.shape[1]
    count, lanes = sum_mid.shape
    slots = rows_in.shape[0] * rows_in.shape[1]
    last_dims = (((1,), (1,)), ((), ()))
    values = lax.dot_general(
        rows_in[:, :, :samples].reshape(slots, samples),
        filters[...],
        last_dims,
        preferred_element_type=F32,
    )
    pick = ((iota((8, 128), 0) == 0) & (iota((8, 128), 1) == 0)).astype(F32).astype(BF16)
    ids = lax.dot_general(
        pick,
        rows_in[:, :, samples:].reshape(slots, rows_in.shape[2] - samples),
        last_dims,
        preferred_element_type=F32,
    )
    hot = (iota((count, slots), 0).astype(F32) == ids[0:1, :]).astype(F32).astype(BF16)
    observed = exact_dot(hot, values)
    resid_mid = seen[:, 0:1] - observed[:, 0:1]
    resid_end = seen[:, 1:2] - observed[:, 1:2]
    hot_depth = marks[:, :lanes]
    sum_mid[...] = hot_depth * resid_mid
    sum_end[...] = hot_depth * resid_end
    face_out[...] = exact_dot(hot_second[...], marks[:, lanes:] * resid_end)


def inject_kernel(at, sum_mid, sum_end, base, mid_out, add_out):
    mid_out[...] = base[...]
    add_out[...] = jnp.zeros_like(add_out)

    def body(r, carry):
        row = lax.shift_right_logical(at[0, r], 7)
        mid_out[pl.ds(row, 1), :] = mid_out[pl.ds(row, 1), :] + sum_end[pl.ds(r, 1), :]
        add_out[pl.ds(row, 1), :] = add_out[pl.ds(row, 1), :] + sum_mid[pl.ds(r, 1), :]
        return carry

    lax.fori_loop(0, sum_mid.shape[0], body, 0, unroll=8)


def image_kernel(
    arrived, faces, mid_face, adj_face, mid, add, nxt, bulk, buoy, lap_mid, lap_now, place, cls_hot, spot_hot, ids,
    last_out, send_out, codes, scaled_face, last_held, sem,
):
    low = which_half()
    count, rows, lanes = mid.shape
    tiles = rows // 8
    per_class = send_out.shape[0] // CLASSES
    scaled_face[...] = mid_face[...] + adj_face[...]

    def body(x, flux):
        after, keep = following(x, count)
        side_sums = sums(buoy[x], keep * buoy[after], take_face(faces[...], 32 + x, low))
        here = mid[x]
        lap, flux = twice_operate(
            bulk[x] * here,
            (keep * bulk[after]) * mid[after],
            take_face(scaled_face[...], 32 + x, low),
            flux,
            side_sums,
        )
        last_held[x] = 2.0 * here - nxt[x] + (0.5 * STEP) * lap + add[x]
        return flux

    lax.fori_loop(0, count, body, buoy[0] * (bulk[0] * mid[0]), unroll=8)
    keep_last = pltpu.make_async_copy(last_held, last_out, sem)
    keep_last.start()
    arrived()

    def pack(x, carry):
        image = mid[x] * lap_mid[x] + last_held[x] * lap_now[x]
        image = (STEP * image).reshape(tiles, 8, lanes)
        peak = jnp.max(jnp.max(jnp.abs(image), axis=1), axis=1, keepdims=True)
        code = jnp.ceil(16.0 * jnp.log2(jnp.maximum(peak, 1e-30))) + 1.0
        codes[pl.ds(pl.multiple_of(x * tiles, tiles), tiles), :] = jnp.broadcast_to(
            code + CODE_ZERO, (tiles, lanes)
        )
        gain = jnp.broadcast_to(32767.0 * jnp.exp2(code * (-1.0 / 16.0)), (tiles, lanes))
        whole = jnp.round(image * gain[:, None, :]).astype(I32).astype(jnp.int16)
        for t in range(tiles):
            send_out[place[0, x * tiles + t]] = whole[t]
        return carry

    lax.fori_loop(0, count, pack, 0, unroll=8)
    code = codes[...]
    upper = jnp.floor(code * (1.0 / 64.0))
    lower = code - 64.0 * upper
    hot = cls_hot[...]
    spread = spot_hot[...]
    sent = 64.0 * jnp.dot(hot, (spread * upper).astype(BF16), preferred_element_type=F32)
    sent = sent + jnp.dot(hot, (spread * lower).astype(BF16), preferred_element_type=F32)
    place_row = iota((8, lanes), 0)
    for c in range(CLASSES):
        tile = jnp.where(
            place_row == 0,
            ids[c : c + 1, :],
            jnp.where(place_row == 1, sent[c : c + 1, :], 0.0),
        )
        send_out[c * per_class + per_class - 1] = tile.astype(I32).astype(jnp.int16)
    keep_last.wait()


def combine_kernel(got, keep_out, send_out, gains_v, slots_v, gains, slots, sems, total, *partial):
    per_class = got.shape[0] // CLASSES
    used = per_class - 1
    for c in range(CLASSES):
        meta = got[c * per_class + used].astype(I32)
        slots_v[c : c + 1, :] = meta[0:1, :]
        code = meta[1:2, :].astype(F32)
        gain = jnp.exp2((code - CODE_ZERO) * (1.0 / 16.0)) * (1.0 / 32767.0)
        gains_v[c : c + 1, :] = jnp.where(code > 0, gain, 0.0)
    copies = [
        pltpu.make_async_copy(gains_v, gains, sems.at[0]),
        pltpu.make_async_copy(slots_v, slots, sems.at[1]),
    ]
    for copy in copies:
        copy.start()
    for part in partial:
        part[...] = jnp.zeros_like(part)
    for copy in copies:
        copy.wait()

    def body(src, carry):
        for s in range(used):
            ring, rank = s // CAPT, s % CAPT
            part = partial[(ring % 2) * CAPT + rank]
            at = (ring // 2) * MT_DEV + slots[src, s]
            value = got[src * per_class + s].astype(I32).astype(F32) * gains[src, s]
            part[at] = part[at] + value
        return carry

    lax.fori_loop(0, CLASSES, body, 0, unroll=2)
    for ring in range(RINGS):
        own = slice((ring // 2) * MT_DEV, (ring // 2 + 1) * MT_DEV)
        parts = [partial[(ring % 2) * CAPT + rank][own] for rank in range(CAPT)]
        total[ring * MT_DEV : (ring + 1) * MT_DEV] = (parts[0] + parts[1]) + (parts[2] + parts[3])
    ring = lax.shift_right_logical(lax.axis_index("shot"), CLASS_SHIFT)

    def owned(other):
        return total[pl.ds((ring ^ other) * MT_DEV, MT_DEV)]

    keep_out[:MT_DEV] = owned(0)
    keep_out[MT_DEV:] = owned(3)
    send_out[:MT_DEV] = owned(1)
    send_out[MT_DEV:] = owned(2)


def fold_kernel(kept, came, keep_out, send_out):
    keep_out[...] = kept[:MT_DEV] + came[:MT_DEV]
    send_out[...] = kept[MT_DEV:] + came[MT_DEV:]


def last_kernel(kept, came, out):
    out[...] = kept[...] + came[...]


def swap(face):
    return lax.ppermute(face, "ap", [(0, 1), (1, 0)])


def local(
    wave_prev,
    wave_now,
    adjoint_late,
    adjoint_next,
    bulk,
    buoyancy,
    traces,
    group_filter,
    trace_group,
    trace_receiver,
    receiver_cell,
    tile_owner,
    tile_slot,
):
    shots = lax.axis_size("shot")
    rings = RINGS
    assert shots == RINGS * CLASSES
    prev, now, late, nxt = wave_prev[0], wave_now[0], adjoint_late[0], adjoint_next[0]
    bulk, buoy = bulk[0], buoyancy[0]
    count, rows, lanes = now.shape
    field = sds(now.shape)
    flat = sds((count * rows, lanes))
    samples = traces.shape[1]
    face = sds((rows, lanes))

    own_rows = traces.shape[0]
    packed = call(
        pack_traces_kernel,
        "pack_traces",
        sds((shots, CAP, samples + 128), BF16),
        [
            pltpu.VMEM((1, own_rows), I32),
            pltpu.VMEM((1, own_rows), I32),
            pltpu.VMEM((own_rows, samples), BF16),
            pltpu.VMEM((shots, CAP, samples + 128), BF16),
            pltpu.SemaphoreType.DMA((5,)),
        ],
        hbm=(0, 1, 2),
        raw_out=(0,),
    )(
        trace_group.reshape(1, -1), trace_receiver.reshape(1, -1), traces
    )
    got_rows = lax.all_to_all(
        packed, "shot", split_axis=0, concat_axis=0, tiled=True
    )

    faces = swap(call(faces_kernel, "faces", face, stage=(3,), late=True)(now, buoy, bulk, nxt))
    lap_now, wave_mid, adj_base, mid_face = call(
        first_kernel, "first_step", (field, field, field, face)
    )(faces, now, prev, bulk, buoy, nxt, late)
    mid_face = swap(mid_face)
    lap_mid, wave_end, lap_now, adj_base = call(
        second_kernel,
        "second_step",
        (field, field, field, field),
        [pltpu.SemaphoreType.DMA((2,))],
        raw_out=(2, 3),
    )(faces, mid_face, wave_mid, now, bulk, buoy, lap_now, adj_base)
    receivers = receiver_cell.shape[1]
    tiles = tile_owner.shape[0]
    per_receiver = pltpu.VMEM((receivers, lanes), F32)
    marks, hot_second, place, cls_hot, spot_hot, ids = call(
        places_kernel,
        "places",
        (
            sds((receivers, 2 * lanes)),
            sds((rows, receivers), BF16),
            sds((1, tiles), I32),
            sds((CLASSES, tiles), BF16),
            sds((tiles, lanes)),
            sds((CLASSES, lanes)),
        ),
        [per_receiver],
        smem=(0,),
        hbm_out=(0, 1, 2, 3, 4, 5),
    )(
        receiver_cell,
        receiver_cell,
        bulk.reshape(flat.shape),
        tile_owner.reshape(1, -1),
        tile_slot.reshape(1, -1),
    )
    spread = sds((receivers, lanes))
    seen, wave_end, lap_mid = call(
        seen_kernel,
        "seen",
        (spread, flat, flat),
        [per_receiver, per_receiver, pltpu.SemaphoreType.DMA((2,))],
        smem=(0,),
        raw_out=(1, 2),
        stage=(1,),
        late=True,
    )(
        receiver_cell,
        marks,
        wave_mid.reshape(flat.shape),
        wave_end.reshape(flat.shape),
        lap_mid.reshape(flat.shape),
    )
    lap_mid = lap_mid.reshape(now.shape)
    sum_mid, sum_end, adj_face = call(
        residual_kernel, "residual", (spread, spread, face), stage=(0, 1, 3, 4)
    )(got_rows, group_filter[0], seen, marks, hot_second)
    adj_face = swap(adj_face)
    adj_mid, adj_add = call(inject_kernel, "inject", (flat, flat), smem=(0,))(
        receiver_cell, sum_mid, sum_end, adj_base.reshape(flat.shape)
    )
    per_class = rings * CAPT + 1
    adj_end, send = call(
        image_kernel,
        "image",
        (field, sds((CLASSES * per_class, 8, lanes), jnp.int16)),
        [
            pltpu.VMEM((tiles, lanes), F32),
            pltpu.VMEM((rows, lanes), F32),
            pltpu.VMEM(now.shape, F32),
            pltpu.SemaphoreType.DMA,
        ],
        smem=(10,),
        raw_out=(0,),
        stage=(8, 9),
        late=True,
    )(
        faces, mid_face, adj_face, adj_mid.reshape(now.shape), adj_add.reshape(now.shape), nxt,
        bulk, buoy, lap_mid, lap_now, place, cls_hot, spot_hot, ids,
    )
    near = [[r * CLASSES + c for c in range(CLASSES)] for r in range(rings)]
    got = lax.all_to_all(
        send.reshape(CLASSES, per_class * 8, lanes),
        "shot",
        split_axis=0,
        concat_axis=0,
        axis_index_groups=near,
        tiled=True,
    )
    table = (CLASSES, lanes)
    half = sds((rings // 2 * MT_DEV, 8, lanes))
    kept, sent = call(
        combine_kernel,
        "combine",
        (half, half),
        [
            pltpu.VMEM(table, F32),
            pltpu.VMEM(table, I32),
            pltpu.SMEM(table, F32),
            pltpu.SMEM(table, I32),
            pltpu.SemaphoreType.DMA((2,)),
            pltpu.VMEM((rings * MT_DEV, 8, lanes), F32),
        ]
        + [pltpu.VMEM(half.shape, F32)] * (2 * CAPT),
    )(got.reshape(CLASSES * per_class, 8, lanes))
    came = lax.ppermute(sent, "shot", [(i, i ^ CLASSES) for i in range(shots)])
    quarter = sds((MT_DEV, 8, lanes))
    kept, sent = call(fold_kernel, "fold", (quarter, quarter))(kept, came)
    came = lax.ppermute(sent, "shot", [(i, i ^ (3 * CLASSES)) for i in range(shots)])
    model_grad = call(last_kernel, "last_sum", quarter, hbm_out=(0,))(kept, came)
    return (model_grad, wave_end.reshape(1, *now.shape), adj_end[None])


def solution(mesh):
    placed = (
        P("shot", None, None, "ap"),
        P("shot", None, None, "ap"),
        P("shot", None, None, "ap"),
        P("shot", None, None, "ap"),
        P("shot", None, None, "ap"),
        P("shot", None, None, "ap"),
        P(("shot", "ap"), None),
        P("shot", None, None),
        P(("shot", "ap"), None),
        P(("shot", "ap")),
        P("shot", "ap"),
        P("shot", None),
        P("shot"),
    )
    return jax.shard_map(
        local,
        mesh=mesh,
        in_specs=placed,
        out_specs=(P("shot", None, "ap"), P("shot", None, None, "ap"), P("shot", None, None, "ap")),
        check_vma=False,
    )
```

```python
import functools

import jax
import jax.numpy as jnp
from jax import lax
from jax.experimental import pallas as pl
from jax.experimental.pallas import tpu as pltpu
from jax.sharding import PartitionSpec as P

STEP = 0.08
MT_DEV = 8
CAP = 2
CAPT = 4
CLASSES = 32
CLASS_SHIFT = 5
RINGS = 4
CODE_ZERO = 4096.0
VMEM_LIMIT = 6 * 1024 * 1024

F32 = jnp.float32
BF16 = jnp.bfloat16
I32 = jnp.int32


def staged_kernel(kernel, stage, late, count_in, count_out, *refs):
    inputs, rest = list(refs[:count_in]), refs[count_in : len(refs) - len(stage) - 1]
    sems, buffers = refs[len(refs) - len(stage) - 1], refs[len(refs) - len(stage) :]
    copies = []
    for n, (i, buffer) in enumerate(zip(stage, buffers)):
        copies.append(pltpu.make_async_copy(inputs[i], buffer, sems.at[n]))
        copies[-1].start()
        inputs[i] = buffer

    def arrived():
        for copy in copies:
            copy.wait()

    if late:
        kernel(arrived, *inputs, *rest)
    else:
        arrived()
        kernel(*inputs, *rest)


def call(
    kernel, name, out_shape, scratch=(), smem=(), hbm_out=(), hbm=(), raw_out=(), stage=(),
    late=False,
):
    def run(*args):
        spaces = [
            pltpu.SMEM if i in smem else pltpu.HBM if i in hbm or i in stage else pltpu.VMEM
            for i in range(len(args))
        ]
        args = [
            x if space is pltpu.SMEM else pltpu.with_memory_space_constraint(x, space)
            for x, space in zip(args, spaces)
        ]
        specs = [pl.BlockSpec(memory_space=space) for space in spaces]
        flat, tree = jax.tree.flatten(out_shape)
        outs = [
            pl.BlockSpec(memory_space=pltpu.HBM if i in raw_out else pltpu.VMEM)
            for i in range(len(flat))
        ]
        shapes = [
            (pltpu.HBM if i in hbm_out or i in raw_out else pltpu.VMEM)(s.shape, s.dtype)
            for i, s in enumerate(flat)
        ]
        body, extra = kernel, []
        if stage:
            body = functools.partial(
                staged_kernel, kernel, stage, late, len(args), len(flat)
            )
            extra = [pltpu.SemaphoreType.DMA((len(stage),))]
            extra += [pltpu.VMEM(args[i].shape, args[i].dtype) for i in stage]
        return pl.pallas_call(
            body,
            out_shape=jax.tree.unflatten(tree, shapes),
            in_specs=specs,
            out_specs=jax.tree.unflatten(tree, outs),
            scratch_shapes=list(scratch) + extra,
            name=name,
            compiler_params=pltpu.CompilerParams(vmem_limit_bytes=VMEM_LIMIT),
        )(*args)

    return run


def sds(shape, dtype=F32):
    return jax.ShapeDtypeStruct(shape, dtype)


def iota(shape, dim):
    return lax.broadcasted_iota(I32, shape, dim)


def pieces(value):
    first = value.astype(BF16)
    rest = value - first.astype(F32)
    second = rest.astype(BF16)
    third = (rest - second.astype(F32)).astype(BF16)
    return first, second, third


def exact_dot(onehot, value):
    first, second, third = pieces(value)
    out = jnp.dot(onehot, third, preferred_element_type=F32)
    out = out + jnp.dot(onehot, second, preferred_element_type=F32)
    return out + jnp.dot(onehot, first, preferred_element_type=F32)


def as_column(row):
    size = row.shape[1]
    eye = iota((size, size), 0) == iota((size, size), 1)
    return jnp.sum(jnp.where(eye, row, 0), axis=1, keepdims=True)


def rank_row(keys):
    size = keys.shape[1]
    first, second = iota((size, size), 0), iota((size, size), 1)
    same = (as_column(keys) == keys) & (first < second)
    return jnp.sum(same.astype(F32), axis=0, keepdims=True)


def which_half():
    low = lax.axis_index("ap") == 0
    return low


def edge_lane(low, lanes):
    return jnp.where(low, lanes - 1, 0)


def put_face(held, plane, at, low):
    lanes = plane.shape[1]
    shift = lax.rem(at - edge_lane(low, lanes) + lanes, lanes)
    return jnp.where(iota(plane.shape, 1) == at, pltpu.roll(plane, shift, 1), held)


def take_face(held, at, low):
    lanes = held.shape[1]
    edge = edge_lane(low, lanes)
    shift = lax.rem(edge - at + lanes, lanes)
    return jnp.where(iota(held.shape, 1) == edge, pltpu.roll(held, shift, 1), 0.0)


def next_second(plane):
    rows = plane.shape[0]
    rolled = pltpu.roll(plane, rows - 1, 0)
    return jnp.where(iota(plane.shape, 0) == rows - 1, 0.0, rolled)


def next_depth(plane, halo):
    lanes = plane.shape[1]
    rolled = pltpu.roll(plane, lanes - 1, 1)
    return jnp.where(iota(plane.shape, 1) == lanes - 1, halo, rolled)


def sums(here, after, halo):
    return here, here + after, here + next_second(here), here + next_depth(here, halo), here + halo


def twice_operate(here, after, halo, before_flux, side_sums):
    buoy, along_x, along_y, along_z, low_z = side_sums
    flux = along_x * (after - here)
    total = flux - before_flux
    flux_y = along_y * (next_second(here) - here)
    under = jnp.where(iota(here.shape, 0) == 0, buoy * here, pltpu.roll(flux_y, 1, 0))
    total = total + (flux_y - under)
    flux_z = along_z * (next_depth(here, halo) - here)
    below = jnp.where(iota(here.shape, 1) == 0, low_z * (here - halo), pltpu.roll(flux_z, 1, 1))
    return total + (flux_z - below), flux


def following(x, count):
    return jnp.minimum(x + 1, count - 1), (x < count - 1).astype(F32)


def faces_kernel(arrived, now, buoy, bulk, nxt, out):
    low = which_half()
    count = now.shape[0]

    def plain(x, held):
        return put_face(put_face(held, now[x], x, low), buoy[x], 32 + x, low)

    def scaled(x, held):
        return put_face(held, bulk[x] * nxt[x], 64 + x, low)

    held = lax.fori_loop(0, count, plain, jnp.zeros(now.shape[1:], F32), unroll=4)
    arrived()
    out[...] = lax.fori_loop(0, count, scaled, held, unroll=8)


def first_kernel(
    faces, now, prev, bulk, buoy, nxt, late, lap_out, mid_out, base_out, face_out
):
    low = which_half()
    count = now.shape[0]

    def body(x, carry):
        flux_v, flux_a, held = carry
        after, keep = following(x, count)
        side_sums = sums(buoy[x], keep * buoy[after], take_face(faces[...], 32 + x, low))
        here = now[x]
        lap, flux_v = twice_operate(
            here, keep * now[after], take_face(faces[...], x, low), flux_v, side_sums
        )
        lap = 0.5 * lap
        lap_out[x] = lap
        mid = 2.0 * here - prev[x] + (STEP * bulk[x]) * lap
        mid_out[x] = mid
        held = put_face(held, mid, x, low)
        scaled = bulk[x] * nxt[x]
        scaled_after = (keep * bulk[after]) * nxt[after]
        lap, flux_a = twice_operate(
            scaled, scaled_after, take_face(faces[...], 64 + x, low), flux_a, side_sums
        )
        base = 2.0 * nxt[x] - late[x] + (0.5 * STEP) * lap
        base_out[x] = base
        return flux_v, flux_a, put_face(held, bulk[x] * base, 32 + x, low)

    start = (buoy[0] * now[0], buoy[0] * (bulk[0] * nxt[0]), jnp.zeros(now.shape[1:], F32))
    _, _, held = lax.fori_loop(0, count, body, start, unroll=4)
    face_out[...] = held


def second_kernel(
    faces, mid_face, mid, now, bulk, buoy, lap_first, base, lap_out, end_out, lap_kept, base_kept,
    sems,
):
    copies = [
        pltpu.make_async_copy(lap_first, lap_kept, sems.at[0]),
        pltpu.make_async_copy(base, base_kept, sems.at[1]),
    ]
    for copy in copies:
        copy.start()
    low = which_half()
    count = now.shape[0]

    def body(x, flux):
        after, keep = following(x, count)
        side_sums = sums(buoy[x], keep * buoy[after], take_face(faces[...], 32 + x, low))
        here = mid[x]
        lap, flux = twice_operate(
            here, keep * mid[after], take_face(mid_face[...], x, low), flux, side_sums
        )
        lap = 0.5 * lap
        lap_out[x] = lap
        end_out[x] = 2.0 * here - now[x] + (STEP * bulk[x]) * lap
        return flux

    lax.fori_loop(0, count, body, buoy[0] * mid[0], unroll=4)
    for copy in copies:
        copy.wait()


def pack_traces_kernel(
    groups_in, receivers_in, traces_in, out, groups, receivers, traces, made, sems
):
    copies = [
        pltpu.make_async_copy(src, dst, sems.at[i])
        for i, (src, dst) in enumerate(
            ((groups_in, groups), (receivers_in, receivers), (traces_in, traces))
        )
    ]
    for copy in copies:
        copy.start()
    shots, cap, wide = out.shape
    slots = shots * cap
    count, samples = traces.shape
    copies[0].wait()
    keys = groups[...]
    place = keys.astype(F32) * CAP + rank_row(keys)
    chosen = (iota((slots, count), 0).astype(F32) == place).astype(F32).astype(BF16)
    copies[1].wait()
    ids = as_column(receivers[...].astype(F32))
    ids = jnp.where(iota((count, 128), 1) == 0, ids, 0.0).astype(BF16)
    named = jnp.dot(chosen, ids, preferred_element_type=F32).astype(BF16)
    made[:, :, samples:] = named.reshape(shots, cap, wide - samples)
    copies[2].wait()
    stores = []
    for n in range(2):
        part = slice(n * slots // 2, (n + 1) * slots // 2)
        dest = pl.ds(n * shots // 2, shots // 2)
        moved = jnp.dot(chosen[part], traces[...], preferred_element_type=F32).astype(BF16)
        made[dest, :, :samples] = moved.reshape(shots // 2, cap, samples)
        stores.append(pltpu.make_async_copy(made.at[dest], out.at[dest], sems.at[3 + n]))
        stores[-1].start()
    for copy in stores:
        copy.wait()


def places_kernel(
    at, cells, bulk, owners, slots, marks_out, hot_second_out, place_out, cls_out, spot_out,
    ids_out, rows_bulk,
):
    low = which_half()
    lanes = 128
    count = cells.shape[1]

    def body(r, carry):
        row = lax.shift_right_logical(at[0, r], 7)
        rows_bulk[pl.ds(r, 1), :] = bulk[pl.ds(row, 1), :]
        return carry

    lax.fori_loop(0, count, body, 0, unroll=8)
    cell_row = cells[...]
    cell_col = as_column(cell_row)
    lane = iota((count, lanes), 1)
    here = lane == (cell_col & (lanes - 1))
    at_edge = here & (lane == edge_lane(low, lanes))
    edge_bulk = jnp.sum(jnp.where(at_edge, rows_bulk[...], 0.0), axis=1, keepdims=True)
    marks_out[:, :lanes] = here.astype(F32)
    first_col = lax.shift_right_logical(cell_col, 13)
    marks_out[:, lanes:] = jnp.where(lane == first_col + 32, edge_bulk, 0.0)
    rows = hot_second_out.shape[0]
    second_row = lax.shift_right_logical(cell_row, 7) & (rows - 1)
    hot_second_out[...] = (iota((rows, count), 0) == second_row).astype(F32).astype(BF16)

    owner = owners[...]
    tiles = owner.shape[1]
    rank = rank_row(owner).astype(I32)
    cls = owner & (CLASSES - 1)
    spot = lax.shift_right_logical(owner, CLASS_SHIFT) * CAPT + rank
    per_class = RINGS * CAPT
    place_out[...] = cls * (per_class + 1) + spot
    cls_hot = (iota((CLASSES, tiles), 0) == cls).astype(F32).astype(BF16)
    cls_out[...] = cls_hot
    spot_hot = (iota((tiles, lanes), 1) == as_column(spot)).astype(F32)
    spot_out[...] = spot_hot
    slot_col = as_column(slots[...]).astype(F32)
    ids_out[...] = jnp.dot(
        cls_hot, (spot_hot * slot_col).astype(BF16), preferred_element_type=F32
    )


def seen_kernel(
    arrived, at, marks, mid, end, lap_mid, seen_out, end_kept, lap_kept, rows_mid, rows_end, sems
):
    copies = [
        pltpu.make_async_copy(end, end_kept, sems.at[0]),
        pltpu.make_async_copy(lap_mid, lap_kept, sems.at[1]),
    ]
    for copy in copies:
        copy.start()
    count, lanes = seen_out.shape

    def body(r, carry):
        row = lax.shift_right_logical(at[0, r], 7)
        rows_mid[pl.ds(r, 1), :] = mid[pl.ds(row, 1), :]
        rows_end[pl.ds(r, 1), :] = end[pl.ds(row, 1), :]
        return carry

    lax.fori_loop(0, count, body, 0, unroll=8)
    arrived()
    here = marks[:, :lanes] > 0.5
    seen_mid = jnp.sum(jnp.where(here, rows_mid[...], 0.0), axis=1, keepdims=True)
    seen_end = jnp.sum(jnp.where(here, rows_end[...], 0.0), axis=1, keepdims=True)
    seen_out[...] = jnp.where(iota((count, lanes), 1) == 0, seen_mid, seen_end)
    for copy in copies:
        copy.wait()


def residual_kernel(rows_in, filters, seen, marks, hot_second, sum_mid, sum_end, face_out):
    samples = filters.shape[1]
    count, lanes = sum_mid.shape
    slots = rows_in.shape[0] * rows_in.shape[1]
    last_dims = (((1,), (1,)), ((), ()))
    values = lax.dot_general(
        rows_in[:, :, :samples].reshape(slots, samples),
        filters[...],
        last_dims,
        preferred_element_type=F32,
    )
    pick = ((iota((8, 128), 0) == 0) & (iota((8, 128), 1) == 0)).astype(F32).astype(BF16)
    ids = lax.dot_general(
        pick,
        rows_in[:, :, samples:].reshape(slots, rows_in.shape[2] - samples),
        last_dims,
        preferred_element_type=F32,
    )
    hot = (iota((count, slots), 0).astype(F32) == ids[0:1, :]).astype(F32).astype(BF16)
    observed = exact_dot(hot, values)
    resid_mid = seen[:, 0:1] - observed[:, 0:1]
    resid_end = seen[:, 1:2] - observed[:, 1:2]
    hot_depth = marks[:, :lanes]
    sum_mid[...] = hot_depth * resid_mid
    sum_end[...] = hot_depth * resid_end
    face_out[...] = exact_dot(hot_second[...], marks[:, lanes:] * resid_end)


def inject_kernel(at, sum_mid, sum_end, base, mid_out, add_out):
    mid_out[...] = base[...]
    add_out[...] = jnp.zeros_like(add_out)

    def body(r, carry):
        row = lax.shift_right_logical(at[0, r], 7)
        mid_out[pl.ds(row, 1), :] = mid_out[pl.ds(row, 1), :] + sum_end[pl.ds(r, 1), :]
        add_out[pl.ds(row, 1), :] = add_out[pl.ds(row, 1), :] + sum_mid[pl.ds(r, 1), :]
        return carry

    lax.fori_loop(0, sum_mid.shape[0], body, 0, unroll=8)


def image_kernel(
    arrived, faces, mid_face, adj_face, mid, add, nxt, bulk, buoy, lap_mid, lap_now, place, cls_hot, spot_hot, ids,
    last_out, send_out, codes, scaled_face, last_held, sem,
):
    low = which_half()
    count, rows, lanes = mid.shape
    tiles = rows // 8
    per_class = send_out.shape[0] // CLASSES
    scaled_face[...] = mid_face[...] + adj_face[...]

    def body(x, flux):
        after, keep = following(x, count)
        side_sums = sums(buoy[x], keep * buoy[after], take_face(faces[...], 32 + x, low))
        here = mid[x]
        lap, flux = twice_operate(
            bulk[x] * here,
            (keep * bulk[after]) * mid[after],
            take_face(scaled_face[...], 32 + x, low),
            flux,
            side_sums,
        )
        last_held[x] = 2.0 * here - nxt[x] + (0.5 * STEP) * lap + add[x]
        return flux

    lax.fori_loop(0, count, body, buoy[0] * (bulk[0] * mid[0]), unroll=8)
    keep_last = pltpu.make_async_copy(last_held, last_out, sem)
    keep_last.start()
    arrived()

    def pack(x, carry):
        image = mid[x] * lap_mid[x] + last_held[x] * lap_now[x]
        image = (STEP * image).reshape(tiles, 8, lanes)
        peak = jnp.max(jnp.max(jnp.abs(image), axis=1), axis=1, keepdims=True)
        code = jnp.ceil(16.0 * jnp.log2(jnp.maximum(peak, 1e-30))) + 1.0
        codes[pl.ds(pl.multiple_of(x * tiles, tiles), tiles), :] = jnp.broadcast_to(
            code + CODE_ZERO, (tiles, lanes)
        )
        gain = jnp.broadcast_to(32767.0 * jnp.exp2(code * (-1.0 / 16.0)), (tiles, lanes))
        whole = jnp.round(image * gain[:, None, :]).astype(I32).astype(jnp.int16)
        for t in range(tiles):
            send_out[place[0, x * tiles + t]] = whole[t]
        return carry

    lax.fori_loop(0, count, pack, 0, unroll=8)
    code = codes[...]
    upper = jnp.floor(code * (1.0 / 64.0))
    lower = code - 64.0 * upper
    hot = cls_hot[...]
    spread = spot_hot[...]
    sent = 64.0 * jnp.dot(hot, (spread * upper).astype(BF16), preferred_element_type=F32)
    sent = sent + jnp.dot(hot, (spread * lower).astype(BF16), preferred_element_type=F32)
    place_row = iota((8, lanes), 0)
    for c in range(CLASSES):
        tile = jnp.where(
            place_row == 0,
            ids[c : c + 1, :],
            jnp.where(place_row == 1, sent[c : c + 1, :], 0.0),
        )
        send_out[c * per_class + per_class - 1] = tile.astype(I32).astype(jnp.int16)
    keep_last.wait()


def combine_kernel(
    got, keep_out, one_out, two_out, three_out, gains_v, slots_v, gains, slots, sems, total, *partial
):
    per_class = got.shape[0] // CLASSES
    used = per_class - 1
    for c in range(CLASSES):
        meta = got[c * per_class + used].astype(I32)
        slots_v[c : c + 1, :] = meta[0:1, :]
        code = meta[1:2, :].astype(F32)
        gain = jnp.exp2((code - CODE_ZERO) * (1.0 / 16.0)) * (1.0 / 32767.0)
        gains_v[c : c + 1, :] = jnp.where(code > 0, gain, 0.0)
    copies = [
        pltpu.make_async_copy(gains_v, gains, sems.at[0]),
        pltpu.make_async_copy(slots_v, slots, sems.at[1]),
    ]
    for copy in copies:
        copy.start()
    for part in partial:
        part[...] = jnp.zeros_like(part)
    for copy in copies:
        copy.wait()

    def body(src, carry):
        for s in range(used):
            ring, rank = s // CAPT, s % CAPT
            part = partial[(ring % 2) * CAPT + rank]
            at = (ring // 2) * MT_DEV + slots[src, s]
            value = got[src * per_class + s].astype(I32).astype(F32) * gains[src, s]
            part[at] = part[at] + value
        return carry

    lax.fori_loop(0, CLASSES, body, 0, unroll=2)
    for ring in range(RINGS):
        own = slice((ring // 2) * MT_DEV, (ring // 2 + 1) * MT_DEV)
        parts = [partial[(ring % 2) * CAPT + rank][own] for rank in range(CAPT)]
        total[ring * MT_DEV : (ring + 1) * MT_DEV] = (parts[0] + parts[1]) + (parts[2] + parts[3])
    ring = lax.shift_right_logical(lax.axis_index("shot"), CLASS_SHIFT)
    for other, out in enumerate((keep_out, one_out, two_out, three_out)):
        out[...] = total[pl.ds((ring ^ other) * MT_DEV, MT_DEV)]


def last_kernel(kept, one, two, three, out):
    out[...] = (kept[...] + one[...]) + (two[...] + three[...])


def swap(face):
    return lax.ppermute(face, "ap", [(0, 1), (1, 0)])


def local(
    wave_prev,
    wave_now,
    adjoint_late,
    adjoint_next,
    bulk,
    buoyancy,
    traces,
    group_filter,
    trace_group,
    trace_receiver,
    receiver_cell,
    tile_owner,
    tile_slot,
):
    shots = lax.axis_size("shot")
    rings = RINGS
    assert shots == RINGS * CLASSES
    prev, now, late, nxt = wave_prev[0], wave_now[0], adjoint_late[0], adjoint_next[0]
    bulk, buoy = bulk[0], buoyancy[0]
    count, rows, lanes = now.shape
    field = sds(now.shape)
    flat = sds((count * rows, lanes))
    samples = traces.shape[1]
    face = sds((rows, lanes))

    own_rows = traces.shape[0]
    packed = call(
        pack_traces_kernel,
        "pack_traces",
        sds((shots, CAP, samples + 128), BF16),
        [
            pltpu.VMEM((1, own_rows), I32),
            pltpu.VMEM((1, own_rows), I32),
            pltpu.VMEM((own_rows, samples), BF16),
            pltpu.VMEM((shots, CAP, samples + 128), BF16),
            pltpu.SemaphoreType.DMA((5,)),
        ],
        hbm=(0, 1, 2),
        raw_out=(0,),
    )(
        trace_group.reshape(1, -1), trace_receiver.reshape(1, -1), traces
    )
    got_rows = lax.all_to_all(
        packed, "shot", split_axis=0, concat_axis=0, tiled=True
    )

    faces = swap(call(faces_kernel, "faces", face, stage=(3,), late=True)(now, buoy, bulk, nxt))
    lap_now, wave_mid, adj_base, mid_face = call(
        first_kernel, "first_step", (field, field, field, face)
    )(faces, now, prev, bulk, buoy, nxt, late)
    mid_face = swap(mid_face)
    lap_mid, wave_end, lap_now, adj_base = call(
        second_kernel,
        "second_step",
        (field, field, field, field),
        [pltpu.SemaphoreType.DMA((2,))],
        raw_out=(2, 3),
    )(faces, mid_face, wave_mid, now, bulk, buoy, lap_now, adj_base)
    receivers = receiver_cell.shape[1]
    tiles = tile_owner.shape[0]
    per_receiver = pltpu.VMEM((receivers, lanes), F32)
    marks, hot_second, place, cls_hot, spot_hot, ids = call(
        places_kernel,
        "places",
        (
            sds((receivers, 2 * lanes)),
            sds((rows, receivers), BF16),
            sds((1, tiles), I32),
            sds((CLASSES, tiles), BF16),
            sds((tiles, lanes)),
            sds((CLASSES, lanes)),
        ),
        [per_receiver],
        smem=(0,),
        hbm_out=(0, 1, 2, 3, 4, 5),
    )(
        receiver_cell,
        receiver_cell,
        bulk.reshape(flat.shape),
        tile_owner.reshape(1, -1),
        tile_slot.reshape(1, -1),
    )
    spread = sds((receivers, lanes))
    seen, wave_end, lap_mid = call(
        seen_kernel,
        "seen",
        (spread, flat, flat),
        [per_receiver, per_receiver, pltpu.SemaphoreType.DMA((2,))],
        smem=(0,),
        raw_out=(1, 2),
        stage=(1,),
        late=True,
    )(
        receiver_cell,
        marks,
        wave_mid.reshape(flat.shape),
        wave_end.reshape(flat.shape),
        lap_mid.reshape(flat.shape),
    )
    lap_mid = lap_mid.reshape(now.shape)
    sum_mid, sum_end, adj_face = call(
        residual_kernel, "residual", (spread, spread, face), stage=(0, 1, 3, 4)
    )(got_rows, group_filter[0], seen, marks, hot_second)
    adj_face = swap(adj_face)
    adj_mid, adj_add = call(inject_kernel, "inject", (flat, flat), smem=(0,))(
        receiver_cell, sum_mid, sum_end, adj_base.reshape(flat.shape)
    )
    per_class = rings * CAPT + 1
    adj_end, send = call(
        image_kernel,
        "image",
        (field, sds((CLASSES * per_class, 8, lanes), jnp.int16)),
        [
            pltpu.VMEM((tiles, lanes), F32),
            pltpu.VMEM((rows, lanes), F32),
            pltpu.VMEM(now.shape, F32),
            pltpu.SemaphoreType.DMA,
        ],
        smem=(10,),
        raw_out=(0,),
        stage=(8, 9),
        late=True,
    )(
        faces, mid_face, adj_face, adj_mid.reshape(now.shape), adj_add.reshape(now.shape), nxt,
        bulk, buoy, lap_mid, lap_now, place, cls_hot, spot_hot, ids,
    )
    near = [[r * CLASSES + c for c in range(CLASSES)] for r in range(rings)]
    got = lax.all_to_all(
        send.reshape(CLASSES, per_class * 8, lanes),
        "shot",
        split_axis=0,
        concat_axis=0,
        axis_index_groups=near,
        tiled=True,
    )
    table = (CLASSES, lanes)
    quarter = sds((MT_DEV, 8, lanes))
    kept, *sent = call(
        combine_kernel,
        "combine",
        (quarter,) * RINGS,
        [
            pltpu.VMEM(table, F32),
            pltpu.VMEM(table, I32),
            pltpu.SMEM(table, F32),
            pltpu.SMEM(table, I32),
            pltpu.SemaphoreType.DMA((2,)),
            pltpu.VMEM((rings * MT_DEV, 8, lanes), F32),
        ]
        + [pltpu.VMEM((rings // 2 * MT_DEV, 8, lanes), F32)] * (2 * CAPT),
    )(got.reshape(CLASSES * per_class, 8, lanes))
    came = [
        lax.ppermute(part, "shot", [(i, i ^ (k * CLASSES)) for i in range(shots)])
        for k, part in enumerate(sent, 1)
    ]
    model_grad = call(last_kernel, "last_sum", quarter, hbm_out=(0,))(kept, *came)
    return (model_grad, wave_end.reshape(1, *now.shape), adj_end[None])


def solution(mesh):
    placed = (
        P("shot", None, None, "ap"),
        P("shot", None, None, "ap"),
        P("shot", None, None, "ap"),
        P("shot", None, None, "ap"),
        P("shot", None, None, "ap"),
        P("shot", None, None, "ap"),
        P(("shot", "ap"), None),
        P("shot", None, None),
        P(("shot", "ap"), None),
        P(("shot", "ap")),
        P("shot", "ap"),
        P("shot", None),
        P("shot"),
    )
    return jax.shard_map(
        local,
        mesh=mesh,
        in_specs=placed,
        out_specs=(P("shot", None, "ap"), P("shot", None, None, "ap"), P("shot", None, None, "ap")),
        check_vma=False,
    )
```

```python
import functools

import jax
import jax.numpy as jnp
from jax import lax
from jax.experimental import pallas as pl
from jax.experimental.pallas import tpu as pltpu
from jax.sharding import PartitionSpec as P

STEP = 0.08
MT_DEV = 8
CAP = 2
CAPT = 4
CLASSES = 32
CLASS_SHIFT = 5
RINGS = 4
CODE_ZERO = 4096.0
VMEM_LIMIT = 6 * 1024 * 1024

F32 = jnp.float32
BF16 = jnp.bfloat16
I32 = jnp.int32


def staged_kernel(kernel, stage, late, count_in, count_out, *refs):
    inputs, rest = list(refs[:count_in]), refs[count_in : len(refs) - len(stage) - 1]
    sems, buffers = refs[len(refs) - len(stage) - 1], refs[len(refs) - len(stage) :]
    copies = []
    for n, (i, buffer) in enumerate(zip(stage, buffers)):
        copies.append(pltpu.make_async_copy(inputs[i], buffer, sems.at[n]))
        copies[-1].start()
        inputs[i] = buffer

    def arrived():
        for copy in copies:
            copy.wait()

    if late:
        kernel(arrived, *inputs, *rest)
    else:
        arrived()
        kernel(*inputs, *rest)


def call(
    kernel, name, out_shape, scratch=(), smem=(), hbm_out=(), hbm=(), raw_out=(), stage=(),
    late=False,
):
    def run(*args):
        spaces = [
            pltpu.SMEM if i in smem else pltpu.HBM if i in hbm or i in stage else pltpu.VMEM
            for i in range(len(args))
        ]
        args = [
            x if space is pltpu.SMEM else pltpu.with_memory_space_constraint(x, space)
            for x, space in zip(args, spaces)
        ]
        specs = [pl.BlockSpec(memory_space=space) for space in spaces]
        flat, tree = jax.tree.flatten(out_shape)
        outs = [
            pl.BlockSpec(memory_space=pltpu.HBM if i in raw_out else pltpu.VMEM)
            for i in range(len(flat))
        ]
        shapes = [
            (pltpu.HBM if i in hbm_out or i in raw_out else pltpu.VMEM)(s.shape, s.dtype)
            for i, s in enumerate(flat)
        ]
        body, extra = kernel, []
        if stage:
            body = functools.partial(
                staged_kernel, kernel, stage, late, len(args), len(flat)
            )
            extra = [pltpu.SemaphoreType.DMA((len(stage),))]
            extra += [pltpu.VMEM(args[i].shape, args[i].dtype) for i in stage]
        return pl.pallas_call(
            body,
            out_shape=jax.tree.unflatten(tree, shapes),
            in_specs=specs,
            out_specs=jax.tree.unflatten(tree, outs),
            scratch_shapes=list(scratch) + extra,
            name=name,
            compiler_params=pltpu.CompilerParams(vmem_limit_bytes=VMEM_LIMIT),
        )(*args)

    return run


def sds(shape, dtype=F32):
    return jax.ShapeDtypeStruct(shape, dtype)


def iota(shape, dim):
    return lax.broadcasted_iota(I32, shape, dim)


def pieces(value):
    first = value.astype(BF16)
    rest = value - first.astype(F32)
    second = rest.astype(BF16)
    third = (rest - second.astype(F32)).astype(BF16)
    return first, second, third


def exact_dot(onehot, value):
    first, second, third = pieces(value)
    out = jnp.dot(onehot, third, preferred_element_type=F32)
    out = out + jnp.dot(onehot, second, preferred_element_type=F32)
    return out + jnp.dot(onehot, first, preferred_element_type=F32)


def as_column(row):
    size = row.shape[1]
    eye = iota((size, size), 0) == iota((size, size), 1)
    return jnp.sum(jnp.where(eye, row, 0), axis=1, keepdims=True)


def rank_row(keys):
    size = keys.shape[1]
    first, second = iota((size, size), 0), iota((size, size), 1)
    same = (as_column(keys) == keys) & (first < second)
    return jnp.sum(same.astype(F32), axis=0, keepdims=True)


def which_half():
    low = lax.axis_index("ap") == 0
    return low


def edge_lane(low, lanes):
    return jnp.where(low, lanes - 1, 0)


def put_face(held, plane, at, low):
    lanes = plane.shape[1]
    shift = lax.rem(at - edge_lane(low, lanes) + lanes, lanes)
    return jnp.where(iota(plane.shape, 1) == at, pltpu.roll(plane, shift, 1), held)


def take_face(held, at, low):
    lanes = held.shape[1]
    edge = edge_lane(low, lanes)
    shift = lax.rem(edge - at + lanes, lanes)
    return jnp.where(iota(held.shape, 1) == edge, pltpu.roll(held, shift, 1), 0.0)


def next_second(plane):
    rows = plane.shape[0]
    rolled = pltpu.roll(plane, rows - 1, 0)
    return jnp.where(iota(plane.shape, 0) == rows - 1, 0.0, rolled)


def next_depth(plane, halo):
    lanes = plane.shape[1]
    rolled = pltpu.roll(plane, lanes - 1, 1)
    return jnp.where(iota(plane.shape, 1) == lanes - 1, halo, rolled)


def sums(here, after, halo):
    return here, here + after, here + next_second(here), here + next_depth(here, halo), here + halo


def twice_operate(here, after, halo, before_flux, side_sums):
    buoy, along_x, along_y, along_z, low_z = side_sums
    flux = along_x * (after - here)
    total = flux - before_flux
    flux_y = along_y * (next_second(here) - here)
    under = jnp.where(iota(here.shape, 0) == 0, buoy * here, pltpu.roll(flux_y, 1, 0))
    total = total + (flux_y - under)
    flux_z = along_z * (next_depth(here, halo) - here)
    below = jnp.where(iota(here.shape, 1) == 0, low_z * (here - halo), pltpu.roll(flux_z, 1, 1))
    return total + (flux_z - below), flux


def following(x, count):
    return jnp.minimum(x + 1, count - 1), (x < count - 1).astype(F32)


def faces_kernel(arrived, now, buoy, bulk, nxt, out):
    low = which_half()
    count = now.shape[0]

    def plain(x, held):
        return put_face(put_face(held, now[x], x, low), buoy[x], 32 + x, low)

    def scaled(x, held):
        return put_face(held, bulk[x] * nxt[x], 64 + x, low)

    held = lax.fori_loop(0, count, plain, jnp.zeros(now.shape[1:], F32), unroll=4)
    arrived()
    out[...] = lax.fori_loop(0, count, scaled, held, unroll=8)


def first_kernel(
    faces, now, prev, bulk, buoy, nxt, late, lap_out, mid_out, base_out, face_out
):
    low = which_half()
    count = now.shape[0]

    def body(x, carry):
        flux_v, flux_a, held = carry
        after, keep = following(x, count)
        side_sums = sums(buoy[x], keep * buoy[after], take_face(faces[...], 32 + x, low))
        here = now[x]
        lap, flux_v = twice_operate(
            here, keep * now[after], take_face(faces[...], x, low), flux_v, side_sums
        )
        lap = 0.5 * lap
        lap_out[x] = lap
        mid = 2.0 * here - prev[x] + (STEP * bulk[x]) * lap
        mid_out[x] = mid
        held = put_face(held, mid, x, low)
        scaled = bulk[x] * nxt[x]
        scaled_after = (keep * bulk[after]) * nxt[after]
        lap, flux_a = twice_operate(
            scaled, scaled_after, take_face(faces[...], 64 + x, low), flux_a, side_sums
        )
        base = 2.0 * nxt[x] - late[x] + (0.5 * STEP) * lap
        base_out[x] = base
        return flux_v, flux_a, put_face(held, bulk[x] * base, 32 + x, low)

    start = (buoy[0] * now[0], buoy[0] * (bulk[0] * nxt[0]), jnp.zeros(now.shape[1:], F32))
    _, _, held = lax.fori_loop(0, count, body, start, unroll=4)
    face_out[...] = held


def second_kernel(
    faces, mid_face, mid, now, bulk, buoy, lap_first, base, lap_out, end_out, lap_kept, base_kept,
    sems,
):
    copies = [
        pltpu.make_async_copy(lap_first, lap_kept, sems.at[0]),
        pltpu.make_async_copy(base, base_kept, sems.at[1]),
    ]
    for copy in copies:
        copy.start()
    low = which_half()
    count = now.shape[0]

    def body(x, flux):
        after, keep = following(x, count)
        side_sums = sums(buoy[x], keep * buoy[after], take_face(faces[...], 32 + x, low))
        here = mid[x]
        lap, flux = twice_operate(
            here, keep * mid[after], take_face(mid_face[...], x, low), flux, side_sums
        )
        lap = 0.5 * lap
        lap_out[x] = lap
        end_out[x] = 2.0 * here - now[x] + (STEP * bulk[x]) * lap
        return flux

    lax.fori_loop(0, count, body, buoy[0] * mid[0], unroll=4)
    for copy in copies:
        copy.wait()


def pack_traces_kernel(
    groups_in, receivers_in, traces_in, out, groups, receivers, traces, made, sems
):
    copies = [
        pltpu.make_async_copy(src, dst, sems.at[i])
        for i, (src, dst) in enumerate(
            ((groups_in, groups), (receivers_in, receivers), (traces_in, traces))
        )
    ]
    for copy in copies:
        copy.start()
    shots, cap, wide = out.shape
    slots = shots * cap
    count, samples = traces.shape
    copies[0].wait()
    keys = groups[...]
    place = keys.astype(F32) * CAP + rank_row(keys)
    chosen = (iota((slots, count), 0).astype(F32) == place).astype(F32).astype(BF16)
    copies[1].wait()
    ids = as_column(receivers[...].astype(F32))
    ids = jnp.where(iota((count, 128), 1) == 0, ids, 0.0).astype(BF16)
    named = jnp.dot(chosen, ids, preferred_element_type=F32).astype(BF16)
    made[:, :, samples:] = named.reshape(shots, cap, wide - samples)
    copies[2].wait()
    stores = []
    for n in range(2):
        part = slice(n * slots // 2, (n + 1) * slots // 2)
        dest = pl.ds(n * shots // 2, shots // 2)
        moved = jnp.dot(chosen[part], traces[...], preferred_element_type=F32).astype(BF16)
        made[dest, :, :samples] = moved.reshape(shots // 2, cap, samples)
        stores.append(pltpu.make_async_copy(made.at[dest], out.at[dest], sems.at[3 + n]))
        stores[-1].start()
    for copy in stores:
        copy.wait()


def places_kernel(
    at, cells, bulk, owners, slots, marks_out, hot_second_out, place_out, cls_out, spot_out,
    ids_out, rows_bulk,
):
    low = which_half()
    lanes = 128
    count = cells.shape[1]

    def body(r, carry):
        row = lax.shift_right_logical(at[0, r], 7)
        rows_bulk[pl.ds(r, 1), :] = bulk[pl.ds(row, 1), :]
        return carry

    lax.fori_loop(0, count, body, 0, unroll=8)
    cell_row = cells[...]
    cell_col = as_column(cell_row)
    lane = iota((count, lanes), 1)
    here = lane == (cell_col & (lanes - 1))
    at_edge = here & (lane == edge_lane(low, lanes))
    edge_bulk = jnp.sum(jnp.where(at_edge, rows_bulk[...], 0.0), axis=1, keepdims=True)
    marks_out[:, :lanes] = here.astype(F32)
    first_col = lax.shift_right_logical(cell_col, 13)
    marks_out[:, lanes:] = jnp.where(lane == first_col + 32, edge_bulk, 0.0)
    rows = hot_second_out.shape[0]
    second_row = lax.shift_right_logical(cell_row, 7) & (rows - 1)
    hot_second_out[...] = (iota((rows, count), 0) == second_row).astype(F32).astype(BF16)

    owner = owners[...]
    tiles = owner.shape[1]
    rank = rank_row(owner).astype(I32)
    cls = owner & (CLASSES - 1)
    spot = lax.shift_right_logical(owner, CLASS_SHIFT) * CAPT + rank
    per_class = RINGS * CAPT
    place_out[...] = cls * (per_class + 1) + spot
    cls_hot = (iota((CLASSES, tiles), 0) == cls).astype(F32).astype(BF16)
    cls_out[...] = cls_hot
    spot_hot = (iota((tiles, lanes), 1) == as_column(spot)).astype(F32)
    spot_out[...] = spot_hot
    slot_col = as_column(slots[...]).astype(F32)
    ids_out[...] = jnp.dot(
        cls_hot, (spot_hot * slot_col).astype(BF16), preferred_element_type=F32
    )


def seen_kernel(
    arrived, at, marks, mid, end, lap_mid, seen_out, end_kept, lap_kept, rows_mid, rows_end, sems
):
    copies = [
        pltpu.make_async_copy(end, end_kept, sems.at[0]),
        pltpu.make_async_copy(lap_mid, lap_kept, sems.at[1]),
    ]
    for copy in copies:
        copy.start()
    count, lanes = seen_out.shape

    def body(r, carry):
        row = lax.shift_right_logical(at[0, r], 7)
        rows_mid[pl.ds(r, 1), :] = mid[pl.ds(row, 1), :]
        rows_end[pl.ds(r, 1), :] = end[pl.ds(row, 1), :]
        return carry

    lax.fori_loop(0, count, body, 0, unroll=8)
    arrived()
    here = marks[:, :lanes] > 0.5
    seen_mid = jnp.sum(jnp.where(here, rows_mid[...], 0.0), axis=1, keepdims=True)
    seen_end = jnp.sum(jnp.where(here, rows_end[...], 0.0), axis=1, keepdims=True)
    seen_out[...] = jnp.where(iota((count, lanes), 1) == 0, seen_mid, seen_end)
    for copy in copies:
        copy.wait()


def residual_kernel(rows_in, filters, seen, marks, hot_second, sum_mid, sum_end, face_out):
    samples = filters.shape[1]
    count, lanes = sum_mid.shape
    slots = rows_in.shape[0] * rows_in.shape[1]
    last_dims = (((1,), (1,)), ((), ()))
    values = lax.dot_general(
        rows_in[:, :, :samples].reshape(slots, samples),
        filters[...],
        last_dims,
        preferred_element_type=F32,
    )
    pick = ((iota((8, 128), 0) == 0) & (iota((8, 128), 1) == 0)).astype(F32).astype(BF16)
    ids = lax.dot_general(
        pick,
        rows_in[:, :, samples:].reshape(slots, rows_in.shape[2] - samples),
        last_dims,
        preferred_element_type=F32,
    )
    hot = (iota((count, slots), 0).astype(F32) == ids[0:1, :]).astype(F32).astype(BF16)
    observed = exact_dot(hot, values)
    resid_mid = seen[:, 0:1] - observed[:, 0:1]
    resid_end = seen[:, 1:2] - observed[:, 1:2]
    hot_depth = marks[:, :lanes]
    sum_mid[...] = hot_depth * resid_mid
    sum_end[...] = hot_depth * resid_end
    face_out[...] = exact_dot(hot_second[...], marks[:, lanes:] * resid_end)


def inject_kernel(at, sum_mid, sum_end, base, mid_out, add_out):
    mid_out[...] = base[...]
    add_out[...] = jnp.zeros_like(add_out)

    def body(r, carry):
        row = lax.shift_right_logical(at[0, r], 7)
        mid_out[pl.ds(row, 1), :] = mid_out[pl.ds(row, 1), :] + sum_end[pl.ds(r, 1), :]
        add_out[pl.ds(row, 1), :] = add_out[pl.ds(row, 1), :] + sum_mid[pl.ds(r, 1), :]
        return carry

    lax.fori_loop(0, sum_mid.shape[0], body, 0, unroll=8)


def image_kernel(
    arrived, faces, mid_face, adj_face, mid, add, nxt, bulk, buoy, lap_mid, lap_now, place, cls_hot, spot_hot, ids,
    last_out, send_out, codes, scaled_face, last_held, sem,
):
    low = which_half()
    count, rows, lanes = mid.shape
    tiles = rows // 8
    per_class = send_out.shape[0] // CLASSES
    scaled_face[...] = mid_face[...] + adj_face[...]

    def body(x, flux):
        after, keep = following(x, count)
        side_sums = sums(buoy[x], keep * buoy[after], take_face(faces[...], 32 + x, low))
        here = mid[x]
        lap, flux = twice_operate(
            bulk[x] * here,
            (keep * bulk[after]) * mid[after],
            take_face(scaled_face[...], 32 + x, low),
            flux,
            side_sums,
        )
        last_held[x] = 2.0 * here - nxt[x] + (0.5 * STEP) * lap + add[x]
        return flux

    lax.fori_loop(0, count, body, buoy[0] * (bulk[0] * mid[0]), unroll=8)
    keep_last = pltpu.make_async_copy(last_held, last_out, sem)
    keep_last.start()
    arrived()

    def pack(x, carry):
        image = mid[x] * lap_mid[x] + last_held[x] * lap_now[x]
        image = (STEP * image).reshape(tiles, 8, lanes)
        peak = jnp.max(jnp.max(jnp.abs(image), axis=1), axis=1, keepdims=True)
        code = jnp.ceil(16.0 * jnp.log2(jnp.maximum(peak, 1e-30))) + 1.0
        codes[pl.ds(pl.multiple_of(x * tiles, tiles), tiles), :] = jnp.broadcast_to(
            code + CODE_ZERO, (tiles, lanes)
        )
        gain = jnp.broadcast_to(32767.0 * jnp.exp2(code * (-1.0 / 16.0)), (tiles, lanes))
        whole = jnp.round(image * gain[:, None, :]).astype(I32).astype(jnp.int16)
        for t in range(tiles):
            send_out[place[0, x * tiles + t]] = whole[t]
        return carry

    lax.fori_loop(0, count, pack, 0, unroll=16)
    code = codes[...]
    upper = jnp.floor(code * (1.0 / 64.0))
    lower = code - 64.0 * upper
    hot = cls_hot[...]
    spread = spot_hot[...]
    sent = 64.0 * jnp.dot(hot, (spread * upper).astype(BF16), preferred_element_type=F32)
    sent = sent + jnp.dot(hot, (spread * lower).astype(BF16), preferred_element_type=F32)
    place_row = iota((8, lanes), 0)
    for c in range(CLASSES):
        tile = jnp.where(
            place_row == 0,
            ids[c : c + 1, :],
            jnp.where(place_row == 1, sent[c : c + 1, :], 0.0),
        )
        send_out[c * per_class + per_class - 1] = tile.astype(I32).astype(jnp.int16)
    keep_last.wait()


def combine_kernel(
    got, keep_out, one_out, two_out, three_out, gains_v, slots_v, gains, slots, sems, total, *partial
):
    per_class = got.shape[0] // CLASSES
    used = per_class - 1
    for c in range(CLASSES):
        meta = got[c * per_class + used].astype(I32)
        slots_v[c : c + 1, :] = meta[0:1, :]
        code = meta[1:2, :].astype(F32)
        gain = jnp.exp2((code - CODE_ZERO) * (1.0 / 16.0)) * (1.0 / 32767.0)
        gains_v[c : c + 1, :] = jnp.where(code > 0, gain, 0.0)
    copies = [
        pltpu.make_async_copy(gains_v, gains, sems.at[0]),
        pltpu.make_async_copy(slots_v, slots, sems.at[1]),
    ]
    for copy in copies:
        copy.start()
    for part in partial:
        part[...] = jnp.zeros_like(part)
    for copy in copies:
        copy.wait()

    def body(src, carry):
        for s in range(used):
            ring, rank = s // CAPT, s % CAPT
            part = partial[(ring % 2) * CAPT + rank]
            at = (ring // 2) * MT_DEV + slots[src, s]
            value = got[src * per_class + s].astype(I32).astype(F32) * gains[src, s]
            part[at] = part[at] + value
        return carry

    lax.fori_loop(0, CLASSES, body, 0, unroll=2)
    for ring in range(RINGS):
        own = slice((ring // 2) * MT_DEV, (ring // 2 + 1) * MT_DEV)
        parts = [partial[(ring % 2) * CAPT + rank][own] for rank in range(CAPT)]
        total[ring * MT_DEV : (ring + 1) * MT_DEV] = (parts[0] + parts[1]) + (parts[2] + parts[3])
    ring = lax.shift_right_logical(lax.axis_index("shot"), CLASS_SHIFT)
    for other, out in enumerate((keep_out, one_out, two_out, three_out)):
        out[...] = total[pl.ds((ring ^ other) * MT_DEV, MT_DEV)]


def last_kernel(kept, one, two, three, out):
    out[...] = (kept[...] + one[...]) + (two[...] + three[...])


def swap(face):
    return lax.ppermute(face, "ap", [(0, 1), (1, 0)])


def local(
    wave_prev,
    wave_now,
    adjoint_late,
    adjoint_next,
    bulk,
    buoyancy,
    traces,
    group_filter,
    trace_group,
    trace_receiver,
    receiver_cell,
    tile_owner,
    tile_slot,
):
    shots = lax.axis_size("shot")
    rings = RINGS
    assert shots == RINGS * CLASSES
    prev, now, late, nxt = wave_prev[0], wave_now[0], adjoint_late[0], adjoint_next[0]
    bulk, buoy = bulk[0], buoyancy[0]
    count, rows, lanes = now.shape
    field = sds(now.shape)
    flat = sds((count * rows, lanes))
    samples = traces.shape[1]
    face = sds((rows, lanes))

    own_rows = traces.shape[0]
    packed = call(
        pack_traces_kernel,
        "pack_traces",
        sds((shots, CAP, samples + 128), BF16),
        [
            pltpu.VMEM((1, own_rows), I32),
            pltpu.VMEM((1, own_rows), I32),
            pltpu.VMEM((own_rows, samples), BF16),
            pltpu.VMEM((shots, CAP, samples + 128), BF16),
            pltpu.SemaphoreType.DMA((5,)),
        ],
        hbm=(0, 1, 2),
        raw_out=(0,),
    )(
        trace_group.reshape(1, -1), trace_receiver.reshape(1, -1), traces
    )
    got_rows = lax.all_to_all(
        packed, "shot", split_axis=0, concat_axis=0, tiled=True
    )

    faces = swap(call(faces_kernel, "faces", face, stage=(3,), late=True)(now, buoy, bulk, nxt))
    lap_now, wave_mid, adj_base, mid_face = call(
        first_kernel, "first_step", (field, field, field, face)
    )(faces, now, prev, bulk, buoy, nxt, late)
    mid_face = swap(mid_face)
    lap_mid, wave_end, lap_now, adj_base = call(
        second_kernel,
        "second_step",
        (field, field, field, field),
        [pltpu.SemaphoreType.DMA((2,))],
        raw_out=(2, 3),
    )(faces, mid_face, wave_mid, now, bulk, buoy, lap_now, adj_base)
    receivers = receiver_cell.shape[1]
    tiles = tile_owner.shape[0]
    per_receiver = pltpu.VMEM((receivers, lanes), F32)
    marks, hot_second, place, cls_hot, spot_hot, ids = call(
        places_kernel,
        "places",
        (
            sds((receivers, 2 * lanes)),
            sds((rows, receivers), BF16),
            sds((1, tiles), I32),
            sds((CLASSES, tiles), BF16),
            sds((tiles, lanes)),
            sds((CLASSES, lanes)),
        ),
        [per_receiver],
        smem=(0,),
        hbm_out=(0, 1, 2, 3, 4, 5),
    )(
        receiver_cell,
        receiver_cell,
        bulk.reshape(flat.shape),
        tile_owner.reshape(1, -1),
        tile_slot.reshape(1, -1),
    )
    spread = sds((receivers, lanes))
    seen, wave_end, lap_mid = call(
        seen_kernel,
        "seen",
        (spread, flat, flat),
        [per_receiver, per_receiver, pltpu.SemaphoreType.DMA((2,))],
        smem=(0,),
        raw_out=(1, 2),
        stage=(1,),
        late=True,
    )(
        receiver_cell,
        marks,
        wave_mid.reshape(flat.shape),
        wave_end.reshape(flat.shape),
        lap_mid.reshape(flat.shape),
    )
    lap_mid = lap_mid.reshape(now.shape)
    sum_mid, sum_end, adj_face = call(
        residual_kernel, "residual", (spread, spread, face), stage=(0, 1, 3, 4)
    )(got_rows, group_filter[0], seen, marks, hot_second)
    adj_face = swap(adj_face)
    adj_mid, adj_add = call(inject_kernel, "inject", (flat, flat), smem=(0,))(
        receiver_cell, sum_mid, sum_end, adj_base.reshape(flat.shape)
    )
    per_class = rings * CAPT + 1
    adj_end, send = call(
        image_kernel,
        "image",
        (field, sds((CLASSES * per_class, 8, lanes), jnp.int16)),
        [
            pltpu.VMEM((tiles, lanes), F32),
            pltpu.VMEM((rows, lanes), F32),
            pltpu.VMEM(now.shape, F32),
            pltpu.SemaphoreType.DMA,
        ],
        smem=(10,),
        raw_out=(0,),
        stage=(8, 9),
        late=True,
    )(
        faces, mid_face, adj_face, adj_mid.reshape(now.shape), adj_add.reshape(now.shape), nxt,
        bulk, buoy, lap_mid, lap_now, place, cls_hot, spot_hot, ids,
    )
    near = [[r * CLASSES + c for c in range(CLASSES)] for r in range(rings)]
    got = lax.all_to_all(
        send.reshape(CLASSES, per_class * 8, lanes),
        "shot",
        split_axis=0,
        concat_axis=0,
        axis_index_groups=near,
        tiled=True,
    )
    table = (CLASSES, lanes)
    quarter = sds((MT_DEV, 8, lanes))
    kept, *sent = call(
        combine_kernel,
        "combine",
        (quarter,) * RINGS,
        [
            pltpu.VMEM(table, F32),
            pltpu.VMEM(table, I32),
            pltpu.SMEM(table, F32),
            pltpu.SMEM(table, I32),
            pltpu.SemaphoreType.DMA((2,)),
            pltpu.VMEM((rings * MT_DEV, 8, lanes), F32),
        ]
        + [pltpu.VMEM((rings // 2 * MT_DEV, 8, lanes), F32)] * (2 * CAPT),
    )(got.reshape(CLASSES * per_class, 8, lanes))
    came = [
        lax.ppermute(sent[k - 1], "shot", [(i, i ^ (k * CLASSES)) for i in range(shots)])
        for k in (2, 3, 1)
    ]
    model_grad = call(last_kernel, "last_sum", quarter, hbm_out=(0,))(kept, *came)
    return (model_grad, wave_end.reshape(1, *now.shape), adj_end[None])


def solution(mesh):
    placed = (
        P("shot", None, None, "ap"),
        P("shot", None, None, "ap"),
        P("shot", None, None, "ap"),
        P("shot", None, None, "ap"),
        P("shot", None, None, "ap"),
        P("shot", None, None, "ap"),
        P(("shot", "ap"), None),
        P("shot", None, None),
        P(("shot", "ap"), None),
        P(("shot", "ap")),
        P("shot", "ap"),
        P("shot", None),
        P("shot"),
    )
    return jax.shard_map(
        local,
        mesh=mesh,
        in_specs=placed,
        out_specs=(P("shot", None, "ap"), P("shot", None, None, "ap"), P("shot", None, None, "ap")),
        check_vma=False,
    )
```

```python
import functools

import jax
import jax.numpy as jnp
from jax import lax
from jax.experimental import pallas as pl
from jax.experimental.pallas import tpu as pltpu
from jax.sharding import PartitionSpec as P

STEP = 0.08
MT_DEV = 8
CAP = 2
CAPT = 4
CLASSES = 32
CLASS_SHIFT = 5
RINGS = 4
CODE_ZERO = 4096.0
VMEM_LIMIT = 6 * 1024 * 1024

F32 = jnp.float32
BF16 = jnp.bfloat16
I32 = jnp.int32


def staged_kernel(kernel, stage, late, count_in, count_out, *refs):
    inputs, rest = list(refs[:count_in]), refs[count_in : len(refs) - len(stage) - 1]
    sems, buffers = refs[len(refs) - len(stage) - 1], refs[len(refs) - len(stage) :]
    copies = []
    for n, (i, buffer) in enumerate(zip(stage, buffers)):
        copies.append(pltpu.make_async_copy(inputs[i], buffer, sems.at[n]))
        copies[-1].start()
        inputs[i] = buffer

    def arrived():
        for copy in copies:
            copy.wait()

    if late:
        kernel(arrived, *inputs, *rest)
    else:
        arrived()
        kernel(*inputs, *rest)


def call(
    kernel, name, out_shape, scratch=(), smem=(), hbm_out=(), hbm=(), raw_out=(), stage=(),
    late=False,
):
    def run(*args):
        spaces = [
            pltpu.SMEM if i in smem else pltpu.HBM if i in hbm or i in stage else pltpu.VMEM
            for i in range(len(args))
        ]
        args = [
            x if space is pltpu.SMEM else pltpu.with_memory_space_constraint(x, space)
            for x, space in zip(args, spaces)
        ]
        specs = [pl.BlockSpec(memory_space=space) for space in spaces]
        flat, tree = jax.tree.flatten(out_shape)
        outs = [
            pl.BlockSpec(memory_space=pltpu.HBM if i in raw_out else pltpu.VMEM)
            for i in range(len(flat))
        ]
        shapes = [
            (pltpu.HBM if i in hbm_out or i in raw_out else pltpu.VMEM)(s.shape, s.dtype)
            for i, s in enumerate(flat)
        ]
        body, extra = kernel, []
        if stage:
            body = functools.partial(
                staged_kernel, kernel, stage, late, len(args), len(flat)
            )
            extra = [pltpu.SemaphoreType.DMA((len(stage),))]
            extra += [pltpu.VMEM(args[i].shape, args[i].dtype) for i in stage]
        return pl.pallas_call(
            body,
            out_shape=jax.tree.unflatten(tree, shapes),
            in_specs=specs,
            out_specs=jax.tree.unflatten(tree, outs),
            scratch_shapes=list(scratch) + extra,
            name=name,
            compiler_params=pltpu.CompilerParams(vmem_limit_bytes=VMEM_LIMIT),
        )(*args)

    return run


def sds(shape, dtype=F32):
    return jax.ShapeDtypeStruct(shape, dtype)


def iota(shape, dim):
    return lax.broadcasted_iota(I32, shape, dim)


def pieces(value):
    first = value.astype(BF16)
    rest = value - first.astype(F32)
    second = rest.astype(BF16)
    third = (rest - second.astype(F32)).astype(BF16)
    return first, second, third


def exact_dot(onehot, value):
    first, second, third = pieces(value)
    out = jnp.dot(onehot, third, preferred_element_type=F32)
    out = out + jnp.dot(onehot, second, preferred_element_type=F32)
    return out + jnp.dot(onehot, first, preferred_element_type=F32)


def as_column(row):
    size = row.shape[1]
    eye = iota((size, size), 0) == iota((size, size), 1)
    return jnp.sum(jnp.where(eye, row, 0), axis=1, keepdims=True)


def rank_row(keys):
    size = keys.shape[1]
    first, second = iota((size, size), 0), iota((size, size), 1)
    same = (as_column(keys) == keys) & (first < second)
    return jnp.sum(same.astype(F32), axis=0, keepdims=True)


def which_half():
    low = lax.axis_index("ap") == 0
    return low


def edge_lane(low, lanes):
    return jnp.where(low, lanes - 1, 0)


def put_face(held, plane, at, low):
    lanes = plane.shape[1]
    shift = lax.rem(at - edge_lane(low, lanes) + lanes, lanes)
    return jnp.where(iota(plane.shape, 1) == at, pltpu.roll(plane, shift, 1), held)


def take_face(held, at, low):
    lanes = held.shape[1]
    edge = edge_lane(low, lanes)
    shift = lax.rem(edge - at + lanes, lanes)
    return jnp.where(iota(held.shape, 1) == edge, pltpu.roll(held, shift, 1), 0.0)


def next_second(plane):
    rows = plane.shape[0]
    rolled = pltpu.roll(plane, rows - 1, 0)
    return jnp.where(iota(plane.shape, 0) == rows - 1, 0.0, rolled)


def next_depth(plane, halo):
    lanes = plane.shape[1]
    rolled = pltpu.roll(plane, lanes - 1, 1)
    return jnp.where(iota(plane.shape, 1) == lanes - 1, halo, rolled)


def sums(here, after, halo):
    return here, here + after, here + next_second(here), here + next_depth(here, halo), here + halo


def twice_operate(here, after, halo, before_flux, side_sums):
    buoy, along_x, along_y, along_z, low_z = side_sums
    flux = along_x * (after - here)
    total = flux - before_flux
    flux_y = along_y * (next_second(here) - here)
    under = jnp.where(iota(here.shape, 0) == 0, buoy * here, pltpu.roll(flux_y, 1, 0))
    total = total + (flux_y - under)
    flux_z = along_z * (next_depth(here, halo) - here)
    below = jnp.where(iota(here.shape, 1) == 0, low_z * (here - halo), pltpu.roll(flux_z, 1, 1))
    return total + (flux_z - below), flux


def following(x, count):
    return jnp.minimum(x + 1, count - 1), (x < count - 1).astype(F32)


def faces_kernel(arrived, now, buoy, bulk, nxt, out):
    low = which_half()
    count = now.shape[0]

    def plain(x, held):
        return put_face(put_face(held, now[x], x, low), buoy[x], 32 + x, low)

    def scaled(x, held):
        return put_face(held, bulk[x] * nxt[x], 64 + x, low)

    held = lax.fori_loop(0, count, plain, jnp.zeros(now.shape[1:], F32), unroll=4)
    arrived()
    out[...] = lax.fori_loop(0, count, scaled, held, unroll=8)


def first_kernel(
    faces, now, prev, bulk, buoy, nxt, late, lap_out, mid_out, base_out, face_out
):
    low = which_half()
    count = now.shape[0]

    def body(x, carry):
        flux_v, flux_a, held = carry
        after, keep = following(x, count)
        side_sums = sums(buoy[x], keep * buoy[after], take_face(faces[...], 32 + x, low))
        here = now[x]
        lap, flux_v = twice_operate(
            here, keep * now[after], take_face(faces[...], x, low), flux_v, side_sums
        )
        lap = 0.5 * lap
        lap_out[x] = lap
        mid = 2.0 * here - prev[x] + (STEP * bulk[x]) * lap
        mid_out[x] = mid
        held = put_face(held, mid, x, low)
        scaled = bulk[x] * nxt[x]
        scaled_after = (keep * bulk[after]) * nxt[after]
        lap, flux_a = twice_operate(
            scaled, scaled_after, take_face(faces[...], 64 + x, low), flux_a, side_sums
        )
        base = 2.0 * nxt[x] - late[x] + (0.5 * STEP) * lap
        base_out[x] = base
        return flux_v, flux_a, put_face(held, bulk[x] * base, 32 + x, low)

    start = (buoy[0] * now[0], buoy[0] * (bulk[0] * nxt[0]), jnp.zeros(now.shape[1:], F32))
    _, _, held = lax.fori_loop(0, count, body, start, unroll=4)
    face_out[...] = held


def second_kernel(
    faces, mid_face, mid, now, bulk, buoy, lap_first, base, lap_out, end_out, lap_kept, base_kept,
    sems,
):
    copies = [
        pltpu.make_async_copy(lap_first, lap_kept, sems.at[0]),
        pltpu.make_async_copy(base, base_kept, sems.at[1]),
    ]
    for copy in copies:
        copy.start()
    low = which_half()
    count = now.shape[0]

    def body(x, flux):
        after, keep = following(x, count)
        side_sums = sums(buoy[x], keep * buoy[after], take_face(faces[...], 32 + x, low))
        here = mid[x]
        lap, flux = twice_operate(
            here, keep * mid[after], take_face(mid_face[...], x, low), flux, side_sums
        )
        lap = 0.5 * lap
        lap_out[x] = lap
        end_out[x] = 2.0 * here - now[x] + (STEP * bulk[x]) * lap
        return flux

    lax.fori_loop(0, count, body, buoy[0] * mid[0], unroll=4)
    for copy in copies:
        copy.wait()


def pack_traces_kernel(
    groups_in, receivers_in, traces_in, out, groups, receivers, traces, made, sems
):
    copies = [
        pltpu.make_async_copy(src, dst, sems.at[i])
        for i, (src, dst) in enumerate(
            ((groups_in, groups), (receivers_in, receivers), (traces_in, traces))
        )
    ]
    for copy in copies:
        copy.start()
    shots, cap, wide = out.shape
    slots = shots * cap
    count, samples = traces.shape
    copies[0].wait()
    keys = groups[...]
    place = keys.astype(F32) * CAP + rank_row(keys)
    chosen = (iota((slots, count), 0).astype(F32) == place).astype(F32).astype(BF16)
    copies[1].wait()
    ids = as_column(receivers[...].astype(F32))
    ids = jnp.where(iota((count, 128), 1) == 0, ids, 0.0).astype(BF16)
    named = jnp.dot(chosen, ids, preferred_element_type=F32).astype(BF16)
    made[:, :, samples:] = named.reshape(shots, cap, wide - samples)
    copies[2].wait()
    stores = []
    for n in range(2):
        part = slice(n * slots // 2, (n + 1) * slots // 2)
        dest = pl.ds(n * shots // 2, shots // 2)
        moved = jnp.dot(chosen[part], traces[...], preferred_element_type=F32).astype(BF16)
        made[dest, :, :samples] = moved.reshape(shots // 2, cap, samples)
        stores.append(pltpu.make_async_copy(made.at[dest], out.at[dest], sems.at[3 + n]))
        stores[-1].start()
    for copy in stores:
        copy.wait()


def places_kernel(
    at, cells, bulk, owners, slots, marks_out, hot_second_out, place_out, cls_out, spot_out,
    ids_out, rows_bulk,
):
    low = which_half()
    lanes = 128
    count = cells.shape[1]

    def body(r, carry):
        row = lax.shift_right_logical(at[0, r], 7)
        rows_bulk[pl.ds(r, 1), :] = bulk[pl.ds(row, 1), :]
        return carry

    lax.fori_loop(0, count, body, 0, unroll=8)
    cell_row = cells[...]
    cell_col = as_column(cell_row)
    lane = iota((count, lanes), 1)
    here = lane == (cell_col & (lanes - 1))
    at_edge = here & (lane == edge_lane(low, lanes))
    edge_bulk = jnp.sum(jnp.where(at_edge, rows_bulk[...], 0.0), axis=1, keepdims=True)
    marks_out[:, :lanes] = here.astype(F32)
    first_col = lax.shift_right_logical(cell_col, 13)
    marks_out[:, lanes:] = jnp.where(lane == first_col + 32, edge_bulk, 0.0)
    rows = hot_second_out.shape[0]
    second_row = lax.shift_right_logical(cell_row, 7) & (rows - 1)
    hot_second_out[...] = (iota((rows, count), 0) == second_row).astype(F32).astype(BF16)

    owner = owners[...]
    tiles = owner.shape[1]
    rank = rank_row(owner).astype(I32)
    cls = owner & (CLASSES - 1)
    spot = lax.shift_right_logical(owner, CLASS_SHIFT) * CAPT + rank
    per_class = RINGS * CAPT
    place_out[...] = cls * (per_class + 1) + spot
    cls_hot = (iota((CLASSES, tiles), 0) == cls).astype(F32).astype(BF16)
    cls_out[...] = cls_hot
    spot_hot = (iota((tiles, lanes), 1) == as_column(spot)).astype(F32)
    spot_out[...] = spot_hot
    slot_col = as_column(slots[...]).astype(F32)
    ids_out[...] = jnp.dot(
        cls_hot, (spot_hot * slot_col).astype(BF16), preferred_element_type=F32
    )


def seen_kernel(
    arrived, at, marks, mid, end, lap_mid, seen_out, end_kept, lap_kept, rows_mid, rows_end, sems
):
    copies = [
        pltpu.make_async_copy(end, end_kept, sems.at[0]),
        pltpu.make_async_copy(lap_mid, lap_kept, sems.at[1]),
    ]
    for copy in copies:
        copy.start()
    count, lanes = seen_out.shape

    def body(r, carry):
        row = lax.shift_right_logical(at[0, r], 7)
        rows_mid[pl.ds(r, 1), :] = mid[pl.ds(row, 1), :]
        rows_end[pl.ds(r, 1), :] = end[pl.ds(row, 1), :]
        return carry

    lax.fori_loop(0, count, body, 0, unroll=8)
    arrived()
    here = marks[:, :lanes] > 0.5
    seen_mid = jnp.sum(jnp.where(here, rows_mid[...], 0.0), axis=1, keepdims=True)
    seen_end = jnp.sum(jnp.where(here, rows_end[...], 0.0), axis=1, keepdims=True)
    seen_out[...] = jnp.where(iota((count, lanes), 1) == 0, seen_mid, seen_end)
    for copy in copies:
        copy.wait()


def residual_kernel(rows_in, filters, seen, marks, hot_second, sum_mid, sum_end, face_out):
    samples = filters.shape[1]
    count, lanes = sum_mid.shape
    slots = rows_in.shape[0] * rows_in.shape[1]
    last_dims = (((1,), (1,)), ((), ()))
    values = lax.dot_general(
        rows_in[:, :, :samples].reshape(slots, samples),
        filters[...],
        last_dims,
        preferred_element_type=F32,
    )
    pick = ((iota((8, 128), 0) == 0) & (iota((8, 128), 1) == 0)).astype(F32).astype(BF16)
    ids = lax.dot_general(
        pick,
        rows_in[:, :, samples:].reshape(slots, rows_in.shape[2] - samples),
        last_dims,
        preferred_element_type=F32,
    )
    hot = (iota((count, slots), 0).astype(F32) == ids[0:1, :]).astype(F32).astype(BF16)
    observed = exact_dot(hot, values)
    resid_mid = seen[:, 0:1] - observed[:, 0:1]
    resid_end = seen[:, 1:2] - observed[:, 1:2]
    hot_depth = marks[:, :lanes]
    sum_mid[...] = hot_depth * resid_mid
    sum_end[...] = hot_depth * resid_end
    face_out[...] = exact_dot(hot_second[...], marks[:, lanes:] * resid_end)


def inject_kernel(at, sum_mid, sum_end, base, mid_out, add_out):
    mid_out[...] = base[...]
    add_out[...] = jnp.zeros_like(add_out)

    def body(r, carry):
        row = lax.shift_right_logical(at[0, r], 7)
        mid_out[pl.ds(row, 1), :] = mid_out[pl.ds(row, 1), :] + sum_end[pl.ds(r, 1), :]
        add_out[pl.ds(row, 1), :] = add_out[pl.ds(row, 1), :] + sum_mid[pl.ds(r, 1), :]
        return carry

    lax.fori_loop(0, sum_mid.shape[0], body, 0, unroll=8)


def image_kernel(
    arrived, faces, mid_face, adj_face, mid, add, nxt, bulk, buoy, lap_mid, lap_now, place, cls_hot, spot_hot, ids,
    last_out, send_out, codes, scaled_face, last_held, sem,
):
    low = which_half()
    count, rows, lanes = mid.shape
    tiles = rows // 8
    per_class = send_out.shape[0] // CLASSES
    scaled_face[...] = mid_face[...] + adj_face[...]

    def body(x, flux):
        after, keep = following(x, count)
        side_sums = sums(buoy[x], keep * buoy[after], take_face(faces[...], 32 + x, low))
        here = mid[x]
        lap, flux = twice_operate(
            bulk[x] * here,
            (keep * bulk[after]) * mid[after],
            take_face(scaled_face[...], 32 + x, low),
            flux,
            side_sums,
        )
        last_held[x] = 2.0 * here - nxt[x] + (0.5 * STEP) * lap + add[x]
        return flux

    lax.fori_loop(0, count, body, buoy[0] * (bulk[0] * mid[0]), unroll=16)
    keep_last = pltpu.make_async_copy(last_held, last_out, sem)
    keep_last.start()
    arrived()

    def pack(x, carry):
        image = mid[x] * lap_mid[x] + last_held[x] * lap_now[x]
        image = (STEP * image).reshape(tiles, 8, lanes)
        peak = jnp.max(jnp.max(jnp.abs(image), axis=1), axis=1, keepdims=True)
        code = jnp.ceil(16.0 * jnp.log2(jnp.maximum(peak, 1e-30))) + 1.0
        codes[pl.ds(pl.multiple_of(x * tiles, tiles), tiles), :] = jnp.broadcast_to(
            code + CODE_ZERO, (tiles, lanes)
        )
        gain = jnp.broadcast_to(32767.0 * jnp.exp2(code * (-1.0 / 16.0)), (tiles, lanes))
        whole = jnp.round(image * gain[:, None, :]).astype(I32).astype(jnp.int16)
        for t in range(tiles):
            send_out[place[0, x * tiles + t]] = whole[t]
        return carry

    lax.fori_loop(0, count, pack, 0, unroll=16)
    code = codes[...]
    upper = jnp.floor(code * (1.0 / 64.0))
    lower = code - 64.0 * upper
    hot = cls_hot[...]
    spread = spot_hot[...]
    sent = 64.0 * jnp.dot(hot, (spread * upper).astype(BF16), preferred_element_type=F32)
    sent = sent + jnp.dot(hot, (spread * lower).astype(BF16), preferred_element_type=F32)
    place_row = iota((8, lanes), 0)
    for c in range(CLASSES):
        tile = jnp.where(
            place_row == 0,
            ids[c : c + 1, :],
            jnp.where(place_row == 1, sent[c : c + 1, :], 0.0),
        )
        send_out[c * per_class + per_class - 1] = tile.astype(I32).astype(jnp.int16)
    keep_last.wait()


def combine_kernel(
    got, keep_out, one_out, two_out, three_out, gains_v, slots_v, gains, slots, sems, total, *partial
):
    per_class = got.shape[0] // CLASSES
    used = per_class - 1
    for c in range(CLASSES):
        meta = got[c * per_class + used].astype(I32)
        slots_v[c : c + 1, :] = meta[0:1, :]
        code = meta[1:2, :].astype(F32)
        gain = jnp.exp2((code - CODE_ZERO) * (1.0 / 16.0)) * (1.0 / 32767.0)
        gains_v[c : c + 1, :] = jnp.where(code > 0, gain, 0.0)
    copies = [
        pltpu.make_async_copy(gains_v, gains, sems.at[0]),
        pltpu.make_async_copy(slots_v, slots, sems.at[1]),
    ]
    for copy in copies:
        copy.start()
    for part in partial:
        part[...] = jnp.zeros_like(part)
    for copy in copies:
        copy.wait()

    def body(src, carry):
        for s in range(used):
            ring, rank = s // CAPT, s % CAPT
            part = partial[(ring % 2) * CAPT + rank]
            at = (ring // 2) * MT_DEV + slots[src, s]
            value = got[src * per_class + s].astype(I32).astype(F32) * gains[src, s]
            part[at] = part[at] + value
        return carry

    lax.fori_loop(0, CLASSES, body, 0, unroll=4)
    for ring in range(RINGS):
        own = slice((ring // 2) * MT_DEV, (ring // 2 + 1) * MT_DEV)
        parts = [partial[(ring % 2) * CAPT + rank][own] for rank in range(CAPT)]
        total[ring * MT_DEV : (ring + 1) * MT_DEV] = (parts[0] + parts[1]) + (parts[2] + parts[3])
    ring = lax.shift_right_logical(lax.axis_index("shot"), CLASS_SHIFT)
    for other, out in enumerate((keep_out, one_out, two_out, three_out)):
        out[...] = total[pl.ds((ring ^ other) * MT_DEV, MT_DEV)]


def last_kernel(kept, one, two, three, out):
    out[...] = (kept[...] + one[...]) + (two[...] + three[...])


def swap(face):
    return lax.ppermute(face, "ap", [(0, 1), (1, 0)])


def local(
    wave_prev,
    wave_now,
    adjoint_late,
    adjoint_next,
    bulk,
    buoyancy,
    traces,
    group_filter,
    trace_group,
    trace_receiver,
    receiver_cell,
    tile_owner,
    tile_slot,
):
    shots = lax.axis_size("shot")
    rings = RINGS
    assert shots == RINGS * CLASSES
    prev, now, late, nxt = wave_prev[0], wave_now[0], adjoint_late[0], adjoint_next[0]
    bulk, buoy = bulk[0], buoyancy[0]
    count, rows, lanes = now.shape
    field = sds(now.shape)
    flat = sds((count * rows, lanes))
    samples = traces.shape[1]
    face = sds((rows, lanes))

    own_rows = traces.shape[0]
    packed = call(
        pack_traces_kernel,
        "pack_traces",
        sds((shots, CAP, samples + 128), BF16),
        [
            pltpu.VMEM((1, own_rows), I32),
            pltpu.VMEM((1, own_rows), I32),
            pltpu.VMEM((own_rows, samples), BF16),
            pltpu.VMEM((shots, CAP, samples + 128), BF16),
            pltpu.SemaphoreType.DMA((5,)),
        ],
        hbm=(0, 1, 2),
        raw_out=(0,),
    )(
        trace_group.reshape(1, -1), trace_receiver.reshape(1, -1), traces
    )
    got_rows = lax.all_to_all(
        packed, "shot", split_axis=0, concat_axis=0, tiled=True
    )

    faces = swap(call(faces_kernel, "faces", face, stage=(3,), late=True)(now, buoy, bulk, nxt))
    lap_now, wave_mid, adj_base, mid_face = call(
        first_kernel, "first_step", (field, field, field, face)
    )(faces, now, prev, bulk, buoy, nxt, late)
    mid_face = swap(mid_face)
    lap_mid, wave_end, lap_now, adj_base = call(
        second_kernel,
        "second_step",
        (field, field, field, field),
        [pltpu.SemaphoreType.DMA((2,))],
        raw_out=(2, 3),
    )(faces, mid_face, wave_mid, now, bulk, buoy, lap_now, adj_base)
    receivers = receiver_cell.shape[1]
    tiles = tile_owner.shape[0]
    per_receiver = pltpu.VMEM((receivers, lanes), F32)
    marks, hot_second, place, cls_hot, spot_hot, ids = call(
        places_kernel,
        "places",
        (
            sds((receivers, 2 * lanes)),
            sds((rows, receivers), BF16),
            sds((1, tiles), I32),
            sds((CLASSES, tiles), BF16),
            sds((tiles, lanes)),
            sds((CLASSES, lanes)),
        ),
        [per_receiver],
        smem=(0,),
        hbm_out=(0, 1, 2, 3, 4, 5),
    )(
        receiver_cell,
        receiver_cell,
        bulk.reshape(flat.shape),
        tile_owner.reshape(1, -1),
        tile_slot.reshape(1, -1),
    )
    spread = sds((receivers, lanes))
    seen, wave_end, lap_mid = call(
        seen_kernel,
        "seen",
        (spread, flat, flat),
        [per_receiver, per_receiver, pltpu.SemaphoreType.DMA((2,))],
        smem=(0,),
        raw_out=(1, 2),
        stage=(1,),
        late=True,
    )(
        receiver_cell,
        marks,
        wave_mid.reshape(flat.shape),
        wave_end.reshape(flat.shape),
        lap_mid.reshape(flat.shape),
    )
    lap_mid = lap_mid.reshape(now.shape)
    sum_mid, sum_end, adj_face = call(
        residual_kernel, "residual", (spread, spread, face), stage=(0, 1, 3, 4)
    )(got_rows, group_filter[0], seen, marks, hot_second)
    adj_face = swap(adj_face)
    adj_mid, adj_add = call(inject_kernel, "inject", (flat, flat), smem=(0,))(
        receiver_cell, sum_mid, sum_end, adj_base.reshape(flat.shape)
    )
    per_class = rings * CAPT + 1
    adj_end, send = call(
        image_kernel,
        "image",
        (field, sds((CLASSES * per_class, 8, lanes), jnp.int16)),
        [
            pltpu.VMEM((tiles, lanes), F32),
            pltpu.VMEM((rows, lanes), F32),
            pltpu.VMEM(now.shape, F32),
            pltpu.SemaphoreType.DMA,
        ],
        smem=(10,),
        raw_out=(0,),
        stage=(8, 9),
        late=True,
    )(
        faces, mid_face, adj_face, adj_mid.reshape(now.shape), adj_add.reshape(now.shape), nxt,
        bulk, buoy, lap_mid, lap_now, place, cls_hot, spot_hot, ids,
    )
    near = [[r * CLASSES + c for c in range(CLASSES)] for r in range(rings)]
    got = lax.all_to_all(
        send.reshape(CLASSES, per_class * 8, lanes),
        "shot",
        split_axis=0,
        concat_axis=0,
        axis_index_groups=near,
        tiled=True,
    )
    table = (CLASSES, lanes)
    quarter = sds((MT_DEV, 8, lanes))
    kept, *sent = call(
        combine_kernel,
        "combine",
        (quarter,) * RINGS,
        [
            pltpu.VMEM(table, F32),
            pltpu.VMEM(table, I32),
            pltpu.SMEM(table, F32),
            pltpu.SMEM(table, I32),
            pltpu.SemaphoreType.DMA((2,)),
            pltpu.VMEM((rings * MT_DEV, 8, lanes), F32),
        ]
        + [pltpu.VMEM((rings // 2 * MT_DEV, 8, lanes), F32)] * (2 * CAPT),
    )(got.reshape(CLASSES * per_class, 8, lanes))
    came = [
        lax.ppermute(sent[k - 1], "shot", [(i, i ^ (k * CLASSES)) for i in range(shots)])
        for k in (2, 3, 1)
    ]
    model_grad = call(last_kernel, "last_sum", quarter, hbm_out=(0,))(kept, *came)
    return (model_grad, wave_end.reshape(1, *now.shape), adj_end[None])


def solution(mesh):
    placed = (
        P("shot", None, None, "ap"),
        P("shot", None, None, "ap"),
        P("shot", None, None, "ap"),
        P("shot", None, None, "ap"),
        P("shot", None, None, "ap"),
        P("shot", None, None, "ap"),
        P(("shot", "ap"), None),
        P("shot", None, None),
        P(("shot", "ap"), None),
        P(("shot", "ap")),
        P("shot", "ap"),
        P("shot", None),
        P("shot"),
    )
    return jax.shard_map(
        local,
        mesh=mesh,
        in_specs=placed,
        out_specs=(P("shot", None, "ap"), P("shot", None, None, "ap"), P("shot", None, None, "ap")),
        check_vma=False,
    )
```
